32 devices in a mesh: gx: 4 (over y, core), gy: 4 (over z), gz: 2 (over x).
Axes of the slice: x: 2, y: 2, z: 4, core: 2. Of those that a mesh axis runs over, the one named last changes fastest.
Arguments:
- rhs: float32 [3, 64, 64, 256], P(None, 'gx', 'gy', 'gz'), may hold values from -24 to 24
- blocks: float32 [9, 64, 64, 256], P(None, 'gx', 'gy', 'gz'), may hold values from -1 to 14, as said below
- couplings: float32 [6, 64, 64, 256], P(None, 'gx', 'gy', 'gz'), may hold values from 0.25 to 1
- agg_ids: int32 [2, 64, 64], P('gz', 'gx', 'gy'), may hold values from 0 to 1023, as said below
- coarse_inv: float32 [36, 4, 1024], P(None, 'gx', ('gy', 'gz')), may hold values from -0.15 to 4, as said below
Outputs:
- solution: float32 [3, 64, 64, 256], P(None, 'gx', 'gy', 'gz')
The draws below stay inside these ranges and needn't reach their ends.
Inputs may be any that keep to these rules, and one draw needn't show every extreme that they name: `agg_ids`: of the pencils of one device, at most 64 have ids in one owner's range (128 consecutive ids starting at a multiple of 128); in every x slab one such range gets exactly 64 pencils from every device of that slab. `blocks`: diagonal entries of each block lie in 8.5 to 14, off-diagonal entries in -1 to 1. `coarse_inv`: diagonal entries of each 6 x 6 matrix lie in 1 to 4, off-diagonal entries in -0.15 to 0.15.
All inputs are finite; a program needn't handle non-finite values.
Results may differ from the reference program's by a relative error of at most 0.00005.
Values sent between devices are 32-bit elements; how exact they have to be, the bound alone decides.
No kernel may reach another device: no remote copies, remote signals or barrier semaphores. Data moves between devices by JAX's collectives and lax.ppermute only.
A program may use at most 64 MiB of HBM per device.

```python
import math
import jax
import jax.numpy as jnp
from jax import lax

CX = 16
CY = 16
CZ = 128
AGG_DEV = 128
CAP = 64
NX = 64
NY = 64
NZ = 256
AGGREGATES = 1024
N_GX = 4
N_GY = 4
N_GZ = 2


def draw_blocks(key, part):
    unit = jax.random.uniform(key, (9, NX, NY, NZ), jnp.float32)
    diagonal = (jnp.arange(9) % 4 == 0)[:, None, None, None]
    main = 8.5 + 5.5 * unit
    other = 2.0 * unit - 1.0
    return jnp.where(diagonal, main, other).astype(jnp.float32)


def draw_coarse_inv(key, part):
    unit = jax.random.uniform(key, (36, N_GX, AGG_DEV * N_GY * N_GZ), jnp.float32)
    diagonal = (jnp.arange(36) % 7 == 0)[:, None, None]
    main = 1.0 + 3.0 * unit
    other = 0.3 * unit - 0.15
    return jnp.where(diagonal, main, other).astype(jnp.float32)


def draw_agg_ids(key, part):
    owners = N_GY * N_GZ
    pencils = CX * CY
    slots = owners * CAP
    hot = jax.random.randint(jax.random.fold_in(key, 11), (N_GX,), 0, owners)
    slot_owner = jnp.arange(slots, dtype=jnp.int32) // CAP

    def one_device(index):
        device_key = jax.random.fold_in(jax.random.fold_in(key, 23), index)
        score = jax.random.permutation(jax.random.fold_in(device_key, 1), slots).astype(jnp.int32)
        favoured = hot[index // owners]
        score = jnp.where(slot_owner == favoured, score - slots, score)
        order = jnp.argsort(score, stable=True)
        chosen = slot_owner[order[:pencils]]
        chosen = jax.random.permutation(jax.random.fold_in(device_key, 2), chosen)
        local_id = jax.random.randint(jax.random.fold_in(device_key, 3), (pencils,), 0, AGG_DEV)
        return (chosen * AGG_DEV + local_id).astype(jnp.int32)
    every = jax.vmap(one_device)(jnp.arange(N_GX * N_GY * N_GZ, dtype=jnp.int32))
    every = every.reshape(N_GX, N_GY, N_GZ, CX, CY)
    every = jnp.transpose(every, (2, 0, 3, 1, 4))
    return every.reshape(N_GZ, N_GX * CX, N_GY * CY)


def block_scale(own_key, shape, shards, low, high):
    gain = 1.0
    for position, parts in shards:
        steps = jax.random.uniform(jax.random.fold_in(jax.random.fold_in(own_key, 6), position), (parts,), jnp.float32, low / len(shards), high / len(shards))
        gain = gain * jnp.repeat(jnp.exp(steps), shape[position] // parts).reshape((-1,) + (1,) * (len(shape) - 1 - position))
    return gain


def gaussian(own_key, extent, deviation, bound, split=(), kind=jnp.bfloat16):
    drawn = jax.random.normal(own_key, extent, jnp.float32) * deviation
    if len(split) > 0:
        drawn = block_scale(own_key, extent, split, -0.22, 0.18) * drawn
    return jnp.clip(drawn, min=-bound, max=bound).astype(kind)


def setup_inputs(seed: int = 0) -> dict:
    key_of = jax.random.split(jax.random.key(seed), 6)
    return {
        "rhs": gaussian(key_of[0], (3, NX, NY, NZ), 4.0, 24.0, ((1, 4), (2, 4), (3, 2)), jnp.float32),
        "blocks": draw_blocks(jax.random.fold_in(key_of[5], 71), 0),
        "couplings": jnp.clip(jnp.exp(math.log(1.0) - 1.3862944 * jax.random.uniform(key_of[2], (6, NX, NY, NZ), jnp.float32) ** block_scale(key_of[2], (6, NX, NY, NZ), ((1, 4), (2, 4), (3, 2)), -0.2, 0.2)), 0.25, 1.0),
        "agg_ids": draw_agg_ids(jax.random.fold_in(key_of[5], 71), 0),
        "coarse_inv": draw_coarse_inv(jax.random.fold_in(key_of[5], 71), 0),
    }


damping = 0.8


def invert_blocks(m):
    a, b, c, d, e, f, g, h, i = [m[k] for k in range(9)]
    co_a = e * i - f * h
    co_b = f * g - d * i
    co_c = d * h - e * g
    determ = a * co_a + b * co_b + c * co_c
    rows = [co_a, c * h - b * i, b * f - c * e, co_b, a * i - c * g, c * d - a * f, co_c, b * g - a * h, a * e - b * d]
    return jnp.stack(rows) / determ


def block_times(m, v):
    return jnp.stack([m[3 * r] * v[0] + m[3 * r + 1] * v[1] + m[3 * r + 2] * v[2] for r in range(3)])


def stencil_apply(padded, field, blocks, couplings):
    beside = couplings[0][None] * padded[:, :-2, 1:-1, 1:-1] + couplings[1][None] * padded[:, 2:, 1:-1, 1:-1]
    beside = beside + couplings[2][None] * padded[:, 1:-1, :-2, 1:-1] + couplings[3][None] * padded[:, 1:-1, 2:, 1:-1]
    beside = beside + couplings[4][None] * padded[:, 1:-1, 1:-1, :-2] + couplings[5][None] * padded[:, 1:-1, 1:-1, 2:]
    return block_times(blocks, field) - beside


def mode_table(length):
    steps = jnp.arange(length).astype(jnp.float32)
    along = (steps - (length - 1) / 2.0) / (length / 2.0)
    first_mode = jnp.full((length,), length ** -0.5, jnp.float32)
    return jnp.stack([first_mode, along * (3.0 / length) ** 0.5], axis=1)


def reference(rhs, blocks, couplings, agg_ids, coarse_inv):
    inverse = invert_blocks(blocks)

    def operate(field):
        padded = jnp.pad(field, ((0, 0), (1, 1), (1, 1), (1, 1)))
        return stencil_apply(padded, field, blocks, couplings)

    first = damping * block_times(inverse, rhs)
    second = first + damping * block_times(inverse, rhs - operate(first))
    resid = rhs - operate(second)
    modes = mode_table(CZ)
    pencil = resid.reshape(3, NX, NY, N_GZ, CZ)
    pencil_coarse = jnp.einsum("cxyzk,km->xyzcm", pencil, modes, precision=lax.Precision.HIGHEST)
    pencil_coarse = pencil_coarse.reshape(NX * NY * N_GZ, 6)
    slab = (jnp.arange(NX) // CX).astype(jnp.int32)
    keys = (slab[:, None, None] * AGGREGATES + jnp.transpose(agg_ids, (1, 2, 0))).reshape(-1).astype(jnp.int32)
    coarse = jax.ops.segment_sum(pencil_coarse, keys, num_segments=N_GX * AGGREGATES)
    matrices = coarse_inv.reshape(6, 6, N_GX * AGGREGATES)
    correction = jnp.sum(matrices * coarse.T[None], axis=1)
    pencil_corr = correction[:, keys].reshape(3, 2, NX, NY, N_GZ)
    prolonged = jnp.einsum("cmxyz,km->cxyzk", pencil_corr, modes, precision=lax.Precision.HIGHEST)
    prolonged = prolonged.reshape(3, NX, NY, NZ)
    third = second + (prolonged - damping * block_times(inverse, operate(prolonged)))
    return third + damping * block_times(inverse, rhs - operate(third))
```

```python
import functools

import jax
import jax.numpy as jnp
from jax import lax
from jax.experimental import pallas as pl
from jax.experimental.pallas import tpu as pltpu
from jax.sharding import PartitionSpec as P

DAMPING = 0.8
HIGHEST = lax.Precision.HIGHEST
AXES = ("gx", "gy", "gz")


def dot_tt(a, b):
    return lax.dot_general(
        a, b, (((1,), (1,)), ((), ())), precision=HIGHEST, preferred_element_type=jnp.float32
    )


def dot_00(a, b):
    return lax.dot_general(
        a, b, (((0,), (0,)), ((), ())), precision=HIGHEST, preferred_element_type=jnp.float32
    )


def lane_iota(rows, lanes):
    return lax.broadcasted_iota(jnp.int32, (rows, lanes), 1)


def row_iota(rows, lanes):
    return lax.broadcasted_iota(jnp.int32, (rows, lanes), 0)


def mode_rows(rows, length):
    k = lane_iota(rows, length).astype(jnp.float32)
    m1 = (k - (length - 1) / 2.0) / (length / 2.0) * (3.0 / length) ** 0.5
    m0 = jnp.full((rows, length), length ** (-0.5), jnp.float32)
    return m0, m1


def is_even(axis):
    return lax.rem(lax.axis_index(axis), 2) == 0


def damped_inverse(m):
    a, b, c, d, e, f, g, h, i = m
    co_a = e * i - f * h
    co_b = f * g - d * i
    co_c = d * h - e * g
    determ = a * co_a + b * co_b + c * co_c
    scale = DAMPING / determ
    rows = [
        co_a,
        c * h - b * i,
        b * f - c * e,
        co_b,
        a * i - c * g,
        c * d - a * f,
        co_c,
        b * g - a * h,
        a * e - b * d,
    ]
    return [r * scale for r in rows]


def times(m, v):
    return [m[3 * r] * v[0] + m[3 * r + 1] * v[1] + m[3 * r + 2] * v[2] for r in range(3)]


class Dims:
    def __init__(self, nx, ny, nz):
        self.nx, self.ny, self.nz = nx, ny, nz
        self.rows = nx * ny


def put_faces(dims, field, sends):
    xe, xo, ye, yo, ze, zo = sends
    nx, ny, nz = dims.nx, dims.ny, dims.nz
    even_x, even_y, even_z = [is_even(a) for a in AXES]
    x_e = jnp.where(even_x, nx - 1, 0)
    x_o = (nx - 1) - x_e
    y_e = jnp.where(even_y, ny - 1, 0)
    y_o = (ny - 1) - y_e
    z_e = jnp.where(even_z, nz - 1, 0)
    z_o = (nz - 1) - z_e
    row = row_iota(8, nz)
    lane = lane_iota(8, nz)
    pick = jnp.where(
        ((row == 0) & (lane == z_e)) | ((row == 1) & (lane == z_o)), 1.0, 0.0
    ).astype(jnp.float32)
    for c in range(3):
        for ref, x in ((xe, x_e), (xo, x_o)):
            ref[c] = field[c, pl.ds(pl.multiple_of(x * ny, ny), ny), :]
        for ref, y in ((ye, y_e), (yo, y_o)):
            ref[c] = field[c, pl.ds(y, nx, stride=ny), :]
        z = dot_tt(pick, field[c])
        ze[c : c + 1, :] = z[0:1]
        zo[c : c + 1, :] = z[1:2]


class Halo:
    def __init__(self, dims, recv):
        xe, xo, ye, yo, ze, zo = recv
        self.dims = dims
        self.even = [is_even(a) for a in AXES]
        self.x, self.y = (xe, xo), (ye, yo)
        nz = dims.nz
        even_z = self.even[2]
        row = row_iota(8, nz)
        lane = lane_iota(8, nz)
        place = jnp.where(
            ((row == 0) & (lane == nz - 1)) | ((row == 1) & (lane == 0)), 1.0, 0.0
        ).astype(jnp.float32)
        low = jnp.where(even_z, zo[...], ze[...])
        high = jnp.where(even_z, ze[...], zo[...])
        row = row_iota(8, dims.rows)
        self.z = []
        for c in range(3):
            pair = jnp.where(row == 0, low[c : c + 1], jnp.where(row == 1, high[c : c + 1], 0.0))
            self.z.append(dot_00(pair, place))

    def x_face(self, c, high):
        e, o = self.x[0][c], self.x[1][c]
        return jnp.where(self.even[0], e, o) if high else jnp.where(self.even[0], o, e)

    def y_row(self, c, x, high):
        e, o = self.y[0][c, x : x + 1, :], self.y[1][c, x : x + 1, :]
        return jnp.where(self.even[1], e, o) if high else jnp.where(self.even[1], o, e)

    def z_tile(self, c, x):
        ny = self.dims.ny
        return self.z[c][x * ny : (x + 1) * ny]


def apply_tile(dims, x, center, x_low, x_high, y_tile, z_tile, blocks, coup):
    ny, nz = dims.ny, dims.nz
    row = row_iota(ny, nz)
    lane = lane_iota(ny, nz)
    own = times(blocks, center)
    out = []
    for c in range(3):
        v = center[c]
        beside = coup[0] * x_low[c] + coup[1] * x_high[c]
        y_minus = pltpu.roll(jnp.where(row == ny - 1, y_tile[c][0], v), 1, 0)
        y_plus = pltpu.roll(jnp.where(row == 0, y_tile[c][1], v), ny - 1, 0)
        beside = beside + coup[2] * y_minus + coup[3] * y_plus
        z_minus = pltpu.roll(jnp.where(lane == nz - 1, z_tile[c], v), 1, 1)
        z_plus = pltpu.roll(jnp.where(lane == 0, z_tile[c], v), nz - 1, 1)
        beside = beside + coup[4] * z_minus + coup[5] * z_plus
        out.append(own[c] - beside)
    return out


def tile(dims, ref, c, x):
    return ref[c, x * dims.ny : (x + 1) * dims.ny, :]


def tiles(dims, ref, count, x):
    return [tile(dims, ref, c, x) for c in range(count)]


def apply_at(dims, x, field, halo, blocks, coup):
    center = tiles(dims, field, 3, x)
    x_low = tiles(dims, field, 3, x - 1) if x > 0 else [halo.x_face(c, False) for c in range(3)]
    x_high = (
        tiles(dims, field, 3, x + 1)
        if x < dims.nx - 1
        else [halo.x_face(c, True) for c in range(3)]
    )
    y_tile = [(halo.y_row(c, x, False), halo.y_row(c, x, True)) for c in range(3)]
    z_tile = [halo.z_tile(c, x) for c in range(3)]
    return center, apply_tile(dims, x, center, x_low, x_high, y_tile, z_tile, blocks, coup)


def first_kernel(dims, rhs, blocks, first, inverse, *sends):
    for x in range(dims.nx):
        inv = damped_inverse(tiles(dims, blocks, 9, x))
        rows = slice(x * dims.ny, (x + 1) * dims.ny)
        for k in range(9):
            inverse[k, rows, :] = inv[k]
        v = times(inv, tiles(dims, rhs, 3, x))
        for c in range(3):
            first[c, rows, :] = v[c]
    put_faces(dims, first, sends)


def smooth(dims, rhs, blocks, couplings, inverse, field, recv, out):
    halo = Halo(dims, recv)
    for x in range(dims.nx):
        center, applied = apply_at(
            dims, x, field, halo, tiles(dims, blocks, 9, x), tiles(dims, couplings, 6, x)
        )
        left = tiles(dims, rhs, 3, x)
        step = times(tiles(dims, inverse, 9, x), [left[c] - applied[c] for c in range(3)])
        rows = slice(x * dims.ny, (x + 1) * dims.ny)
        for c in range(3):
            out[c, rows, :] = center[c] + step[c]


def second_kernel(dims, rhs, blocks, couplings, inverse, first, *refs):
    recv, (second, *sends) = refs[:6], refs[6:]
    smooth(dims, rhs, blocks, couplings, inverse, first, recv, second)
    put_faces(dims, second, sends)


def last_kernel(dims, rhs, blocks, couplings, inverse, third, *refs):
    recv, out = refs[:6], refs[6]
    smooth(dims, rhs, blocks, couplings, inverse, third, recv, out)


def coarse_kernel(dims, rhs, blocks, couplings, second, ids, coarse_inv, *refs):
    recv, packet, resid = refs[:6], refs[6], refs[7]
    halo = Halo(dims, recv)
    for x in range(dims.nx):
        _, applied = apply_at(
            dims, x, second, halo, tiles(dims, blocks, 9, x), tiles(dims, couplings, 6, x)
        )
        left = tiles(dims, rhs, 3, x)
        rows = slice(x * dims.ny, (x + 1) * dims.ny)
        for c in range(3):
            resid[c, rows, :] = left[c] - applied[c]
    m0, m1 = mode_rows(8, dims.nz)
    row = row_iota(8, dims.nz)
    modes = jnp.where(row == 0, m0, jnp.where(row == 1, m1, 0.0))
    for c in range(3):
        packet[0, 2 * c : 2 * c + 2, :] = dot_tt(modes, resid[c])[0:2]
    packet[0, 6:7, :] = ids[...].astype(jnp.float32)
    packet[0, 7:8, :] = jnp.zeros((1, dims.rows), jnp.float32)
    half = coarse_inv.shape[0] // 2
    own = coarse_inv.shape[1]
    packet[0, 8 : 8 + half, 0:own] = coarse_inv[0:half]
    packet[0, 8 : 8 + half, own : 2 * own] = coarse_inv[half : 2 * half]


def split3(v):
    high = v.astype(jnp.bfloat16)
    rest = v - high.astype(jnp.float32)
    mid = rest.astype(jnp.bfloat16)
    low = (rest - mid.astype(jnp.float32)).astype(jnp.bfloat16)
    return jnp.concatenate([high, mid, low], axis=0)


def gray(j):
    return lax.bitwise_xor(j, lax.shift_right_logical(j, 1))


def gray_inverse(v, bits):
    out = v
    for b in range(1, bits):
        out = lax.bitwise_xor(out, lax.shift_right_logical(v, b))
    return out


def bits_of(n):
    return max(1, (n - 1).bit_length())


def solve_kernel(dims, sizes, own, packets, own_out, y_out, z_out, coarse, correction):
    n_y, n_z = sizes
    owners = n_y * n_z
    rows = dims.rows
    my_y, my_z = lax.axis_index("gy"), lax.axis_index("gz")
    half = 18

    def owner_at(j):
        jz = lax.rem(j, n_z)
        jy = lax.div(j, n_z)
        return lax.bitwise_xor(my_y, gray(jy)) * n_z + lax.bitwise_xor(my_z, gray(jz))

    def member(j, ids):
        base = (owner_at(j) * own).astype(jnp.float32)
        agg = row_iota(own, rows).astype(jnp.float32) + base
        return jnp.where(agg == ids, 1.0, 0.0).astype(jnp.bfloat16)

    coarse[...] = jnp.zeros_like(coarse)

    def add(d, carry):
        pack = packets[d, 0:8, :]
        ids = pack[6:7]
        parts = split3(jnp.where(row_iota(8, rows) < 6, pack, 0.0))

        def one(j, carry):
            s = lax.dot_general(
                parts,
                member(j, ids),
                (((1,), (1,)), ((), ())),
                preferred_element_type=jnp.float32,
            )
            coarse[j] = coarse[j] + (s[0:8] + (s[8:16] + s[16:24]))
            return carry

        return lax.fori_loop(0, owners, one, carry, unroll=8)

    lax.fori_loop(0, owners, add, 0)

    def correct(j, carry):
        v = coarse[j]
        out = []
        for i in range(6):
            total = None
            for k in range(6):
                at = 6 * i + k
                r, side = 8 + at % half, at // half
                term = packets[j, r : r + 1, side * own : (side + 1) * own] * v[k : k + 1]
                total = term if total is None else total + term
            out.append(total)
        out += [jnp.zeros((2, own), jnp.float32)]
        correction[j] = split3(jnp.concatenate(out, axis=0))
        return carry

    lax.fori_loop(0, owners, correct, 0)

    def gather(y, z):
        inside = (y >= 0) & (y < n_y) & (z >= 0) & (z < n_z)
        y = jnp.clip(y, 0, n_y - 1)
        z = jnp.clip(z, 0, n_z - 1)
        jy = gray_inverse(lax.bitwise_xor(my_y, y), bits_of(n_y))
        jz = gray_inverse(lax.bitwise_xor(my_z, z), bits_of(n_z))
        ids = packets[jy * n_z + jz, 6:7, :]

        def one(j, total):
            return total + lax.dot_general(
                correction[j],
                member(j, ids),
                (((1,), (0,)), ((), ())),
                preferred_element_type=jnp.float32,
            )

        s = lax.fori_loop(0, owners, one, jnp.zeros((24, rows), jnp.float32), unroll=8)
        return jnp.where(inside, s[0:8] + (s[8:16] + s[16:24]), 0.0)

    own_out[...] = gather(my_y, my_z)
    place = lax.rem(lane_iota(8, rows), dims.ny)
    low, high = gather(my_y - 1, my_z), gather(my_y + 1, my_z)
    y_out[...] = jnp.where(place == dims.ny - 1, low, jnp.where(place == 0, high, 0.0))
    z_out[0] = gather(my_y, my_z - 1)
    z_out[1] = gather(my_y, my_z + 1)


def third_kernel(dims, blocks, couplings, inverse, second, own, y_mix, z_mix, xe, xo, *refs):
    third, sends, (field, y_field, z_field) = refs[0], refs[1:7], refs[7:]
    nx, ny, nz, rows = dims.nx, dims.ny, dims.nz, dims.rows
    m0, m1 = mode_rows(8, nz)
    row = row_iota(8, nz)
    lane = lane_iota(8, nz)
    last = jnp.where(lane == nz - 1, 1.0, 0.0)
    start = jnp.where(lane == 0, 1.0, 0.0)
    zero = jnp.zeros((8, nz), jnp.float32)
    even_x = is_even("gx")
    x_low = jnp.where(even_x, xo[...], xe[...])
    x_high = jnp.where(even_x, xe[...], xo[...])
    x_field = []
    row_r = row_iota(8, rows)
    for c in range(3):
        modes = jnp.where(row == 2 * c, m0, jnp.where(row == 2 * c + 1, m1, zero))
        field[c] = dot_00(own[...], modes)
        y_field[c] = dot_00(y_mix[...], modes)
        z_field[c] = dot_00(z_mix[0], modes * last) + dot_00(z_mix[1], modes * start)
        x_field.append(
            (dot_00(x_low, modes)[rows - ny : rows], dot_00(x_high, modes)[0:ny])
        )
    for x in range(nx):
        center = tiles(dims, field, 3, x)
        low = tiles(dims, field, 3, x - 1) if x > 0 else [x_field[c][0] for c in range(3)]
        high = tiles(dims, field, 3, x + 1) if x < nx - 1 else [x_field[c][1] for c in range(3)]
        y_tile = [(tile(dims, y_field, c, x),) * 2 for c in range(3)]
        z_tile = tiles(dims, z_field, 3, x)
        applied = apply_tile(
            dims,
            x,
            center,
            low,
            high,
            y_tile,
            z_tile,
            tiles(dims, blocks, 9, x),
            tiles(dims, couplings, 6, x),
        )
        step = times(tiles(dims, inverse, 9, x), applied)
        at = slice(x * ny, (x + 1) * ny)
        for c in range(3):
            third[c, at, :] = second[c, at, :] + (center[c] - step[c])
    put_faces(dims, third, sends)


def pairs(count, start):
    out = []
    for i in range(start, count - 1, 2):
        out += [(i, i + 1), (i + 1, i)]
    return out


def swap(value, axis, start):
    count = lax.axis_size(axis)
    which = pairs(count, start)
    return lax.ppermute(value, axis, which) if which else jnp.zeros_like(value)


def exchange(sends):
    xe, xo, ye, yo, ze, zo = sends
    ze, zo = swap(ze, "gz", 0), swap(zo, "gz", 1)
    yo, ye = swap(yo, "gy", 1), swap(ye, "gy", 0)
    xo, xe = swap(xo, "gx", 1), swap(xe, "gx", 0)
    return xe, xo, ye, yo, ze, zo


def gather_slab(packet):
    for axis in ("gz", "gy"):
        count = lax.axis_size(axis)
        mask = 1
        while mask < count:
            which = [(i, i ^ mask) for i in range(count)]
            packet = jnp.concatenate([packet, lax.ppermute(packet, axis, which)], axis=0)
            mask = 2 * mask + 1
    return packet


def call(body, name, out_shapes, scratch, *args):
    return pl.pallas_call(
        body,
        name=name,
        out_shape=[jax.ShapeDtypeStruct(s, jnp.float32) for s in out_shapes],
        in_specs=[pl.BlockSpec(memory_space=pltpu.VMEM)] * len(args),
        out_specs=[pl.BlockSpec(memory_space=pltpu.VMEM)] * len(out_shapes),
        scratch_shapes=scratch,
        compiler_params=pltpu.CompilerParams(vmem_limit_bytes=24 * 1024 * 1024),
    )(*args)


def shards(rhs, blocks, couplings, agg_ids, coarse_inv):
    _, nx, ny, nz = rhs.shape
    dims = Dims(nx, ny, nz)
    rows = nx * ny
    rhs = rhs.reshape(3, rows, nz)
    blocks = blocks.reshape(9, rows, nz)
    couplings = couplings.reshape(6, rows, nz)
    ids = agg_ids.reshape(1, rows)
    own = coarse_inv.shape[2]
    coarse_inv = coarse_inv.reshape(36, own)
    n_y, n_z = lax.axis_size("gy"), lax.axis_size("gz")
    owners = n_y * n_z
    vector = (3, rows, nz)
    faces = [(3, ny, nz)] * 2 + [(3, nx, nz)] * 2 + [(8, rows)] * 2
    part = functools.partial

    first, inverse, *sends = call(
        part(first_kernel, dims), "first", [vector, (9, rows, nz)] + faces, [], rhs, blocks
    )
    recv = exchange(sends)
    second, *sends = call(
        part(second_kernel, dims),
        "second",
        [vector] + faces,
        [],
        rhs,
        blocks,
        couplings,
        inverse,
        first,
        *recv,
    )
    recv = exchange(sends)
    (packet,) = call(
        part(coarse_kernel, dims),
        "coarse",
        [(1, 8 + 18, rows)],
        [pltpu.VMEM(vector, jnp.float32)],
        rhs,
        blocks,
        couplings,
        second,
        ids,
        coarse_inv,
        *recv,
    )
    packets = gather_slab(packet)
    corr, y_mix, z_mix = call(
        part(solve_kernel, dims, (n_y, n_z), own),
        "solve",
        [(8, rows), (8, rows), (2, 8, rows)],
        [
            pltpu.VMEM((owners, 8, own), jnp.float32),
            pltpu.VMEM((owners, 24, own), jnp.bfloat16),
        ],
        packets,
    )
    xo, xe = swap(corr, "gx", 1), swap(corr, "gx", 0)
    third, *sends = call(
        part(third_kernel, dims),
        "third",
        [vector] + faces,
        [pltpu.VMEM(vector, jnp.float32)] * 3,
        blocks,
        couplings,
        inverse,
        second,
        corr,
        y_mix,
        z_mix,
        xe,
        xo,
    )
    recv = exchange(sends)
    (out,) = call(
        part(last_kernel, dims),
        "last",
        [vector],
        [],
        rhs,
        blocks,
        couplings,
        inverse,
        third,
        *recv,
    )
    return out.reshape(3, nx, ny, nz)


def solution(mesh):
    return jax.shard_map(
        shards,
        mesh=mesh,
        in_specs=(
            P(None, "gx", "gy", "gz"),
            P(None, "gx", "gy", "gz"),
            P(None, "gx", "gy", "gz"),
            P("gz", "gx", "gy"),
            P(None, "gx", ("gy", "gz")),
        ),
        out_specs=P(None, "gx", "gy", "gz"),
        check_vma=False,
    )
```

```python
import functools

import jax
import jax.numpy as jnp
from jax import lax
from jax.experimental import pallas as pl
from jax.experimental.pallas import tpu as pltpu
from jax.sharding import PartitionSpec as P

DAMPING = 0.8
AXES = ("gx", "gy", "gz")
VMEM_LIMIT = 12 * 1024 * 1024


def dot_tt(a, b):
    return lax.dot_general(
        a, b, (((1,), (1,)), ((), ())), preferred_element_type=jnp.float32
    )


def dot_00(a, b):
    return lax.dot_general(
        a, b, (((0,), (0,)), ((), ())), preferred_element_type=jnp.float32
    )


def parts3(v):
    high = v.astype(jnp.bfloat16)
    rest = v - high.astype(jnp.float32)
    mid = rest.astype(jnp.bfloat16)
    low = (rest - mid.astype(jnp.float32)).astype(jnp.bfloat16)
    return high, mid, low


def split3(v):
    return jnp.concatenate(parts3(v), axis=0)


def pairs6(v):
    high, mid, low = parts3(v)
    return jnp.concatenate([high, high, high, mid, mid, low], axis=0)


def pairs6_right(v):
    high, mid, low = parts3(v)
    return jnp.concatenate([high, mid, low, high, mid, high], axis=0)


def triple(v):
    return jnp.concatenate([v, v, v], axis=0)


def lane_iota(rows, lanes):
    return lax.broadcasted_iota(jnp.int32, (rows, lanes), 1)


def row_iota(rows, lanes):
    return lax.broadcasted_iota(jnp.int32, (rows, lanes), 0)


def mode_rows(rows, length):
    k = lane_iota(rows, length).astype(jnp.float32)
    m1 = (k - (length - 1) / 2.0) / (length / 2.0) * (3.0 / length) ** 0.5
    m0 = jnp.full((rows, length), length ** (-0.5), jnp.float32)
    return m0, m1


def is_even(axis):
    return lax.rem(lax.axis_index(axis), 2) == 0


def damped_inverse(m):
    a, b, c, d, e, f, g, h, i = m
    co_a = e * i - f * h
    co_b = f * g - d * i
    co_c = d * h - e * g
    determ = a * co_a + b * co_b + c * co_c
    scale = DAMPING / determ
    rows = [
        co_a,
        c * h - b * i,
        b * f - c * e,
        co_b,
        a * i - c * g,
        c * d - a * f,
        co_c,
        b * g - a * h,
        a * e - b * d,
    ]
    return [r * scale for r in rows]


def times(m, v):
    return [m[3 * r] * v[0] + m[3 * r + 1] * v[1] + m[3 * r + 2] * v[2] for r in range(3)]


class Dims:
    def __init__(self, nx, ny, nz):
        self.nx, self.ny, self.nz = nx, ny, nz
        self.rows = nx * ny


def put_faces(dims, field, sends):
    xe, xo, ye, yo, ze, zo = sends
    nx, ny, nz = dims.nx, dims.ny, dims.nz
    even_x, even_y, even_z = [is_even(a) for a in AXES]
    x_e = jnp.where(even_x, nx - 1, 0)
    x_o = (nx - 1) - x_e
    y_e = jnp.where(even_y, ny - 1, 0)
    y_o = (ny - 1) - y_e
    z_e = jnp.where(even_z, nz - 1, 0)
    z_o = (nz - 1) - z_e
    row = row_iota(8, nz)
    lane = lane_iota(8, nz)
    pick = jnp.where(
        ((row == 0) & (lane == z_e)) | ((row == 1) & (lane == z_o)), 1.0, 0.0
    ).astype(jnp.float32)
    pick = pick.astype(jnp.bfloat16)
    for c in range(3):
        for ref, x in ((xe, x_e), (xo, x_o)):
            ref[c] = field[c, pl.ds(pl.multiple_of(x * ny, ny), ny), :]
        for ref, y in ((ye, y_e), (yo, y_o)):
            ref[c] = field[c, pl.ds(y, nx, stride=ny), :]
        z = sum(dot_tt(pick, part) for part in parts3(field[c]))
        ze[c : c + 1, :] = z[0:1]
        zo[c : c + 1, :] = z[1:2]


class Halo:
    def __init__(self, dims, recv):
        xe, xo, ye, yo, ze, zo = recv
        self.dims = dims
        self.even = [is_even(a) for a in AXES]
        self.x, self.y = (xe, xo), (ye, yo)
        nz = dims.nz
        even_z = self.even[2]
        low = jnp.where(even_z, zo[...], ze[...])
        high = jnp.where(even_z, ze[...], zo[...])
        row = row_iota(8, dims.rows)
        both = jnp.where(row < 3, low, jnp.where(row < 6, pltpu.roll(high, 3, 0), 0.0))
        row = row_iota(8, nz)
        lane = lane_iota(8, nz)
        place = [
            ((row == c) & (lane == nz - 1)) | ((row == 3 + c) & (lane == 0)) for c in range(3)
        ]
        place = jnp.where(jnp.concatenate(place, axis=1), 1.0, 0.0)
        self.z = dot_00(split3(both), triple(place).astype(jnp.bfloat16))

    def x_face(self, c, high):
        e, o = self.x[0][c], self.x[1][c]
        return jnp.where(self.even[0], e, o) if high else jnp.where(self.even[0], o, e)

    def y_row(self, c, x, high):
        e, o = self.y[0][c, x : x + 1, :], self.y[1][c, x : x + 1, :]
        return jnp.where(self.even[1], e, o) if high else jnp.where(self.even[1], o, e)

    def z_tile(self, c, x):
        ny, nz = self.dims.ny, self.dims.nz
        return self.z[x * ny : (x + 1) * ny, c * nz : (c + 1) * nz]


def apply_tile(dims, x, center, x_low, x_high, y_tile, z_tile, blocks, coup):
    ny, nz = dims.ny, dims.nz
    row = row_iota(ny, nz)
    lane = lane_iota(ny, nz)
    own = times(blocks, center)
    out = []
    for c in range(3):
        v = center[c]
        beside = coup[0] * x_low[c] + coup[1] * x_high[c]
        y_minus = pltpu.roll(jnp.where(row == ny - 1, y_tile[c][0], v), 1, 0)
        y_plus = pltpu.roll(jnp.where(row == 0, y_tile[c][1], v), ny - 1, 0)
        beside = beside + coup[2] * y_minus + coup[3] * y_plus
        z_minus = pltpu.roll(jnp.where(lane == nz - 1, z_tile[c], v), 1, 1)
        z_plus = pltpu.roll(jnp.where(lane == 0, z_tile[c], v), nz - 1, 1)
        beside = beside + coup[4] * z_minus + coup[5] * z_plus
        out.append(own[c] - beside)
    return out


def tile(dims, ref, c, x):
    return ref[c, x * dims.ny : (x + 1) * dims.ny, :]


def tiles(dims, ref, count, x):
    return [tile(dims, ref, c, x) for c in range(count)]


def apply_at(dims, x, field, halo, blocks, coup):
    center = tiles(dims, field, 3, x)
    x_low = tiles(dims, field, 3, x - 1) if x > 0 else [halo.x_face(c, False) for c in range(3)]
    x_high = (
        tiles(dims, field, 3, x + 1)
        if x < dims.nx - 1
        else [halo.x_face(c, True) for c in range(3)]
    )
    y_tile = [(halo.y_row(c, x, False), halo.y_row(c, x, True)) for c in range(3)]
    z_tile = [halo.z_tile(c, x) for c in range(3)]
    return center, apply_tile(dims, x, center, x_low, x_high, y_tile, z_tile, blocks, coup)


def first_kernel(dims, rhs, blocks, first, inverse, *sends):
    for x in range(dims.nx):
        inv = damped_inverse(tiles(dims, blocks, 9, x))
        rows = slice(x * dims.ny, (x + 1) * dims.ny)
        for k in range(9):
            inverse[k, rows, :] = inv[k]
        v = times(inv, tiles(dims, rhs, 3, x))
        for c in range(3):
            first[c, rows, :] = v[c]
    put_faces(dims, first, sends)


def smooth(dims, rhs, blocks, couplings, inverse, field, recv, out):
    halo = Halo(dims, recv)
    for x in range(dims.nx):
        center, applied = apply_at(
            dims, x, field, halo, tiles(dims, blocks, 9, x), tiles(dims, couplings, 6, x)
        )
        left = tiles(dims, rhs, 3, x)
        step = times(tiles(dims, inverse, 9, x), [left[c] - applied[c] for c in range(3)])
        rows = slice(x * dims.ny, (x + 1) * dims.ny)
        for c in range(3):
            out[c, rows, :] = center[c] + step[c]


def second_kernel(dims, rhs, blocks, couplings, inverse, first, *refs):
    recv, (second, *sends) = refs[:6], refs[6:]
    smooth(dims, rhs, blocks, couplings, inverse, first, recv, second)
    put_faces(dims, second, sends)


def last_kernel(dims, rhs, blocks, couplings, inverse, third, *refs):
    recv, out = refs[:6], refs[6]
    smooth(dims, rhs, blocks, couplings, inverse, third, recv, out)


def coarse_kernel(dims, rhs, blocks, couplings, second, ids, *refs):
    recv, packet, resid = refs[:6], refs[6], refs[7]
    halo = Halo(dims, recv)
    for x in range(dims.nx):
        _, applied = apply_at(
            dims, x, second, halo, tiles(dims, blocks, 9, x), tiles(dims, couplings, 6, x)
        )
        left = tiles(dims, rhs, 3, x)
        rows = slice(x * dims.ny, (x + 1) * dims.ny)
        for c in range(3):
            resid[c, rows, :] = left[c] - applied[c]
    m0, m1 = mode_rows(8, dims.nz)
    row = row_iota(8, dims.nz)
    modes = split3(jnp.where(row == 0, m0, jnp.where(row == 1, m1, 0.0)))
    for c in range(3):
        s = sum(dot_tt(modes, part) for part in parts3(resid[c]))
        packet[0, 2 * c : 2 * c + 2, :] = (s[0:8] + (s[8:16] + s[16:24]))[0:2]
    packet[0, 6:7, :] = pencil_row(dims, ids[0].astype(jnp.float32))
    packet[0, 7:8, :] = jnp.zeros((1, dims.rows), jnp.float32)


def pencil_row(dims, square):
    nx, ny, rows = dims.nx, dims.ny, dims.rows
    lane = lane_iota(ny, rows)
    spread = jnp.where(lax.rem(lane, ny) == row_iota(ny, rows), 1.0, 0.0)
    wide = lax.dot_general(
        square,
        spread,
        (((1,), (0,)), ((), ())),
        precision=lax.Precision.HIGHEST,
        preferred_element_type=jnp.float32,
    )
    lane = lane_iota(nx, rows)
    keep = lax.div(lane, ny) == row_iota(nx, rows)
    return jnp.sum(jnp.where(keep, wide, 0.0), axis=0, keepdims=True)


def gray(j):
    return lax.bitwise_xor(j, lax.shift_right_logical(j, 1))


def gray_inverse(v, bits):
    out = v
    for b in range(1, bits):
        out = lax.bitwise_xor(out, lax.shift_right_logical(v, b))
    return out


def bits_of(n):
    return max(1, (n - 1).bit_length())


def solve_kernel(dims, sizes, own, packets, inverses, own_out, y_out, z_out, coarse, correction):
    n_y, n_z = sizes
    owners = n_y * n_z
    rows = dims.rows
    my_y, my_z = lax.axis_index("gy"), lax.axis_index("gz")
    local = row_iota(own, rows).astype(jnp.bfloat16)
    one_b = jnp.ones((own, rows), jnp.bfloat16)
    zero_b = jnp.zeros((own, rows), jnp.bfloat16)

    def owner_at(j):
        jz = lax.rem(j, n_z)
        jy = lax.div(j, n_z)
        return lax.bitwise_xor(my_y, gray(jy)) * n_z + lax.bitwise_xor(my_z, gray(jz))

    def member(j, ids):
        base = (owner_at(j) * own).astype(jnp.float32)
        rel = jnp.clip(ids - base, -1.0, float(own)).astype(jnp.bfloat16)
        return jnp.where(local == rel, one_b, zero_b)

    coarse[...] = jnp.zeros_like(coarse)

    def add(d, carry):
        pack = packets[d]
        ids = pack[6:7]
        parts = split3(jnp.where(row_iota(8, rows) < 6, pack, 0.0))
        for j in range(owners):
            s = dot_tt(parts, member(j, ids))
            coarse[8 * j : 8 * j + 8] = coarse[8 * j : 8 * j + 8] + (s[0:8] + (s[8:16] + s[16:24]))
        return carry

    lax.fori_loop(0, owners, add, 0, unroll=2)

    for block in range(owners // 8):
        v = [coarse[pl.ds(64 * block + k, 8, stride=8), :] for k in range(6)]
        for i in range(6):
            total = None
            for k in range(6):
                m = inverses[pl.ds(36 * 8 * block + 6 * i + k, 8, stride=36), :]
                total = m * v[k] if total is None else total + m * v[k]
            correction[pl.ds(64 * block + i, 8, stride=8), :] = total
        for i in (6, 7):
            correction[pl.ds(64 * block + i, 8, stride=8), :] = jnp.zeros_like(total)

    def ids_of(y, z):
        inside = (y >= 0) & (y < n_y) & (z >= 0) & (z < n_z)
        y = jnp.clip(y, 0, n_y - 1)
        z = jnp.clip(z, 0, n_z - 1)
        jy = gray_inverse(lax.bitwise_xor(my_y, y), bits_of(n_y))
        jz = gray_inverse(lax.bitwise_xor(my_z, z), bits_of(n_z))
        return jnp.where(inside, packets[jy * n_z + jz, 6:7, :], -1.0)

    place = lax.rem(lane_iota(1, rows), dims.ny)
    low, high = ids_of(my_y - 1, my_z), ids_of(my_y + 1, my_z)
    wanted = [
        ids_of(my_y, my_z),
        jnp.where(place == dims.ny - 1, low, jnp.where(place == 0, high, -1.0)),
        ids_of(my_y, my_z - 1),
        ids_of(my_y, my_z + 1),
    ]
    if n_z == 2:
        wanted = wanted[:2] + [ids_of(my_y, 1 - my_z)]
    totals = [jnp.zeros((24, rows), jnp.float32) for _ in wanted]
    for j in range(owners):
        left = split3(correction[8 * j : 8 * j + 8])
        for t in range(len(wanted)):
            totals[t] = totals[t] + lax.dot_general(
                left,
                member(j, wanted[t]),
                (((1,), (0,)), ((), ())),
                preferred_element_type=jnp.float32,
            )
    totals = [s[0:8] + (s[8:16] + s[16:24]) for s in totals]
    own_out[...] = totals[0]
    y_out[...] = totals[1]
    if n_z == 2:
        z_out[0] = jnp.where(my_z == 1, totals[2], 0.0)
        z_out[1] = jnp.where(my_z == 0, totals[2], 0.0)
    else:
        z_out[0] = totals[2]
        z_out[1] = totals[3]


def third_kernel(dims, blocks, couplings, inverse, second, own, y_mix, z_mix, xe, xo, *refs):
    third, sends, (field, y_field, z_field, x_field) = refs[0], refs[1:7], refs[7:]
    nx, ny, nz = dims.nx, dims.ny, dims.nz
    m0, m1 = mode_rows(8, nz)
    row = row_iota(8, nz)
    lane = lane_iota(8, 3 * nz)
    even_x = is_even("gx")
    side = nx * ny // 2
    x_low = jnp.where(even_x, xo[:, side:], xe[:, side:])
    x_high = jnp.where(even_x, xe[:, :side], xo[:, :side])
    x_mix = jnp.where(lane_iota(8, side) < ny, x_high, x_low)
    modes = jnp.concatenate(
        [
            jnp.where(row == 2 * c, m0, jnp.where(row == 2 * c + 1, m1, 0.0))
            for c in range(3)
        ],
        axis=1,
    )
    at = lax.rem(lane, nz)
    wide = pairs6_right(modes)
    last = pairs6_right(jnp.where(at == nz - 1, modes, 0.0))
    start = pairs6_right(jnp.where(at == 0, modes, 0.0))
    field[...] = dot_00(pairs6(own[...]), wide)
    y_field[...] = dot_00(pairs6(y_mix[...]), wide)
    z_field[...] = dot_00(pairs6(z_mix[0]), last) + dot_00(pairs6(z_mix[1]), start)
    x_field[...] = dot_00(pairs6(x_mix), wide)

    def at_x(ref, x):
        return [ref[x * ny : (x + 1) * ny, c * nz : (c + 1) * nz] for c in range(3)]

    for x in range(nx):
        center = at_x(field, x)
        low = at_x(field, x - 1) if x > 0 else at_x(x_field, side // ny - 1)
        high = at_x(field, x + 1) if x < nx - 1 else at_x(x_field, 0)
        y_tile = [(v, v) for v in at_x(y_field, x)]
        z_tile = at_x(z_field, x)
        applied = apply_tile(
            dims,
            x,
            center,
            low,
            high,
            y_tile,
            z_tile,
            tiles(dims, blocks, 9, x),
            tiles(dims, couplings, 6, x),
        )
        step = times(tiles(dims, inverse, 9, x), applied)
        at = slice(x * ny, (x + 1) * ny)
        for c in range(3):
            third[c, at, :] = second[c, at, :] + (center[c] - step[c])
    put_faces(dims, third, sends)


def pairs(count, start):
    out = []
    for i in range(start, count - 1, 2):
        out += [(i, i + 1), (i + 1, i)]
    return out


def swap(value, axis, start):
    count = lax.axis_size(axis)
    which = pairs(count, start)
    return lax.ppermute(value, axis, which) if which else jnp.zeros_like(value)


def exchange(sends):
    xe, xo, ye, yo, ze, zo = sends
    ze, zo = swap(ze, "gz", 0), swap(zo, "gz", 1)
    yo, ye = swap(yo, "gy", 1), swap(ye, "gy", 0)
    xo, xe = swap(xo, "gx", 1), swap(xe, "gx", 0)
    return xe, xo, ye, yo, ze, zo


def gather_slab(packet):
    for axis in ("gz", "gy"):
        count = lax.axis_size(axis)
        mask = 1
        while mask < count:
            which = [(i, i ^ mask) for i in range(count)]
            arrived = lax.ppermute(packet, axis, which)
            tail = (-1,) + packet.shape[-2:] if packet.shape[1] == 8 else (-1, packet.shape[-1])
            packet = jnp.concatenate([packet.reshape(tail), arrived.reshape(tail)], axis=0)
            mask = 2 * mask + 1
    return packet


def call(body, name, out_shapes, scratch, *args):
    return pl.pallas_call(
        body,
        name=name,
        out_shape=[jax.ShapeDtypeStruct(s, jnp.float32) for s in out_shapes],
        in_specs=[pl.BlockSpec(memory_space=pltpu.VMEM)] * len(args),
        out_specs=[pl.BlockSpec(memory_space=pltpu.VMEM)] * len(out_shapes),
        scratch_shapes=scratch,
        compiler_params=pltpu.CompilerParams(vmem_limit_bytes=VMEM_LIMIT),
    )(*args)


def shards(rhs, blocks, couplings, agg_ids, coarse_inv):
    _, nx, ny, nz = rhs.shape
    dims = Dims(nx, ny, nz)
    rows = nx * ny
    rhs = rhs.reshape(3, rows, nz)
    blocks = blocks.reshape(9, rows, nz)
    couplings = couplings.reshape(6, rows, nz)
    own = coarse_inv.shape[2]
    inverses = gather_slab(coarse_inv)
    n_y, n_z = lax.axis_size("gy"), lax.axis_size("gz")
    owners = n_y * n_z
    vector = (3, rows, nz)
    faces = [(3, ny, nz)] * 2 + [(3, nx, nz)] * 2 + [(8, rows)] * 2
    part = functools.partial

    first, inverse, *sends = call(
        part(first_kernel, dims), "first", [vector, (9, rows, nz)] + faces, [], rhs, blocks
    )
    recv = exchange(sends)
    second, *sends = call(
        part(second_kernel, dims),
        "second",
        [vector] + faces,
        [],
        rhs,
        blocks,
        couplings,
        inverse,
        first,
        *recv,
    )
    recv = exchange(sends)
    (packet,) = call(
        part(coarse_kernel, dims),
        "coarse",
        [(1, 8, rows)],
        [pltpu.VMEM(vector, jnp.float32)],
        rhs,
        blocks,
        couplings,
        second,
        agg_ids,
        *recv,
    )
    packets = gather_slab(packet)
    corr, y_mix, z_mix = call(
        part(solve_kernel, dims, (n_y, n_z), own),
        "solve",
        [(8, rows), (8, rows), (2, 8, rows)],
        [
            pltpu.VMEM((owners * 8, own), jnp.float32),
            pltpu.VMEM((owners * 8, own), jnp.float32),
        ],
        packets,
        inverses,
    )
    xo, xe = swap(corr, "gx", 1), swap(corr, "gx", 0)
    third, *sends = call(
        part(third_kernel, dims),
        "third",
        [vector] + faces,
        [pltpu.VMEM((rows, 3 * nz), jnp.float32)] * 3
        + [pltpu.VMEM((rows // 2, 3 * nz), jnp.float32)],
        blocks,
        couplings,
        inverse,
        second,
        corr,
        y_mix,
        z_mix,
        xe,
        xo,
    )
    recv = exchange(sends)
    (out,) = call(
        part(last_kernel, dims),
        "last",
        [vector],
        [],
        rhs,
        blocks,
        couplings,
        inverse,
        third,
        *recv,
    )
    return out.reshape(3, nx, ny, nz)


def solution(mesh):
    return jax.shard_map(
        shards,
        mesh=mesh,
        in_specs=(
            P(None, "gx", "gy", "gz"),
            P(None, "gx", "gy", "gz"),
            P(None, "gx", "gy", "gz"),
            P("gz", "gx", "gy"),
            P(None, "gx", ("gy", "gz")),
        ),
        out_specs=P(None, "gx", "gy", "gz"),
        check_vma=False,
    )
```

```python
import functools

import jax
import jax.numpy as jnp
from jax import lax
from jax.experimental import pallas as pl
from jax.experimental.pallas import tpu as pltpu
from jax.sharding import PartitionSpec as P

DAMPING = 0.8
AXES = ("gx", "gy", "gz")
VMEM_LIMIT = 12 * 1024 * 1024


def dot_tt(a, b):
    return lax.dot_general(
        a, b, (((1,), (1,)), ((), ())), preferred_element_type=jnp.float32
    )


def dot_00(a, b):
    return lax.dot_general(
        a, b, (((0,), (0,)), ((), ())), preferred_element_type=jnp.float32
    )


def parts3(v):
    high = v.astype(jnp.bfloat16)
    rest = v - high.astype(jnp.float32)
    mid = rest.astype(jnp.bfloat16)
    low = (rest - mid.astype(jnp.float32)).astype(jnp.bfloat16)
    return high, mid, low


def split3(v):
    return jnp.concatenate(parts3(v), axis=0)


def pairs6(v):
    high, mid, low = parts3(v)
    return jnp.concatenate([high, high, high, mid, mid, low], axis=0)


def pairs6_right(v):
    high, mid, low = parts3(v)
    return jnp.concatenate([high, mid, low, high, mid, high], axis=0)


def lane_iota(rows, lanes):
    return lax.broadcasted_iota(jnp.int32, (rows, lanes), 1)


def row_iota(rows, lanes):
    return lax.broadcasted_iota(jnp.int32, (rows, lanes), 0)


def mode_rows(rows, length):
    k = lane_iota(rows, length).astype(jnp.float32)
    m1 = (k - (length - 1) / 2.0) / (length / 2.0) * (3.0 / length) ** 0.5
    m0 = jnp.full((rows, length), length ** (-0.5), jnp.float32)
    return m0, m1


def is_even(axis):
    return lax.rem(lax.axis_index(axis), 2) == 0


def damped_inverse(m):
    a, b, c, d, e, f, g, h, i = m
    co_a = e * i - f * h
    co_b = f * g - d * i
    co_c = d * h - e * g
    determ = a * co_a + b * co_b + c * co_c
    scale = DAMPING / determ
    rows = [
        co_a,
        c * h - b * i,
        b * f - c * e,
        co_b,
        a * i - c * g,
        c * d - a * f,
        co_c,
        b * g - a * h,
        a * e - b * d,
    ]
    return [r * scale for r in rows]


def times(m, v):
    return [m[3 * r] * v[0] + m[3 * r + 1] * v[1] + m[3 * r + 2] * v[2] for r in range(3)]


class Dims:
    def __init__(self, nx, ny, nz):
        self.nx, self.ny, self.nz = nx, ny, nz
        self.rows = nx * ny
        self.groups = self.rows // 8


def tile(ref, c, x, size):
    return ref[c, x * size : (x + 1) * size, :]


def tiles(ref, count, x, size):
    return [tile(ref, c, x, size) for c in range(count)]


def flat_tiles(ref, start, count, size):
    return [ref[(start + c) * size : (start + c + 1) * size, :] for c in range(count)]


def face_index(axis, count):
    even = jnp.where(is_even(axis), count - 1, 0)
    return even, (count - 1) - even


def put_faces(dims, fields, sends):
    xe, xo, ye, yo = sends
    nx, ny = dims.nx, dims.ny
    x_at = face_index("gx", nx)
    y_at = face_index("gy", ny)
    at = 0
    for field in fields:
        for c in range(field.shape[0]):
            for ref, x in zip((xe, xo), x_at):
                ref[at * ny : (at + 1) * ny, :] = field[c, pl.ds(pl.multiple_of(x * ny, ny), ny), :]
            for ref, y in zip((ye, yo), y_at):
                ref[at * nx : (at + 1) * nx, :] = field[c, pl.ds(y, nx, stride=ny), :]
            at += 1


def put_z(dims, field, sends):
    groups, nz = dims.groups, dims.nz
    lane = lane_iota(8, nz)
    for ref, k in zip(sends, face_index("gz", nz)):
        total = []
        for c in range(3):
            face = jnp.zeros((8, nz), jnp.float32)
            for g in range(groups):
                to = c * groups + g
                v = pltpu.roll(field[c, 8 * g : 8 * g + 8, :], lax.rem(to + nz - k, nz), 1)
                face = jnp.where(lane == to, v, face)
            total.append(face)
        ref[...] = total[0] + total[1] + total[2]


def neighbour(axis, pair, high):
    e, o = pair
    even = is_even(axis)
    return jnp.where(even, e, o) if high else jnp.where(even, o, e)


class ZHalo:
    def __init__(self, dims, recv):
        self.dims = dims
        self.recv = [r[...] for r in recv]
        if len(recv) == 2:
            self.low = neighbour("gz", self.recv, False)
            self.high = neighbour("gz", self.recv, True)
        else:
            self.low = self.high = None
            self.at = jnp.where(is_even("gz"), 0, dims.nz - 1)

    def tile(self, c, x):
        dims = self.dims
        nz = dims.nz
        lane = lane_iota(8, nz)
        per = dims.ny // 8
        out = []
        for g in range(x * per, (x + 1) * per):
            at = c * dims.groups + g
            if self.low is None:
                v = pltpu.roll(self.recv[0], lax.rem(self.at + nz - at, nz), 1)
                out.append(jnp.where(lane == self.at, v, 0.0))
            else:
                low = pltpu.roll(self.low, (nz - 1 - at) % nz, 1)
                high = pltpu.roll(self.high, (nz - at) % nz, 1)
                out.append(jnp.where(lane == nz - 1, low, high))
        return jnp.concatenate(out, axis=0) if per > 1 else out[0]


def shifted(v, low, high, axis):
    size = v.shape[axis]
    at = lax.broadcasted_iota(jnp.int32, v.shape, axis)
    below = pltpu.roll(jnp.where(at == size - 1, low, v), 1, axis)
    above = pltpu.roll(jnp.where(at == 0, high, v), size - 1, axis)
    return below, above


def beside(coup, x_pair, y_pair, z_pair):
    return (
        coup[0] * x_pair[0]
        + coup[1] * x_pair[1]
        + (coup[2] * y_pair[0] + coup[3] * y_pair[1])
        + (coup[4] * z_pair[0] + coup[5] * z_pair[1])
    )


def sums_at(dims, x, field, x_halo, y_halo, z_halo, coup):
    nx, ny = dims.nx, dims.ny
    center = tiles(field, 3, x, ny)
    out = []
    for c in range(3):
        low = tile(field, c, x - 1, ny) if x > 0 else x_halo(c, False)
        high = tile(field, c, x + 1, ny) if x < nx - 1 else x_halo(c, True)
        y_pair = shifted(center[c], y_halo(c, x, False), y_halo(c, x, True), 0)
        z = z_halo.tile(c, x)
        z_pair = shifted(center[c], z, z, 1)
        out.append(beside(coup, (low, high), y_pair, z_pair))
    return center, out


def received(dims, recv):
    xe, xo, ye, yo = recv
    nx, ny = dims.nx, dims.ny

    def x_halo(c, high):
        pair = [r[c * ny : (c + 1) * ny, :] for r in (xe, xo)]
        return neighbour("gx", pair, high)

    def y_halo(c, x, high):
        pair = [r[c * nx + x : c * nx + x + 1, :] for r in (ye, yo)]
        return neighbour("gy", pair, high)

    return x_halo, y_halo


def rows_at(dims, x):
    return slice(x * dims.ny, (x + 1) * dims.ny)


def first_kernel(dims, counts, *refs):
    n_inv, n_z = counts
    rhs, blocks, couplings = refs[:3]
    pieces, refs = refs[3 : 3 + n_inv], refs[3 + n_inv :]
    first, inverse, xe, xo, ye, yo = refs[:6]
    for x in range(dims.nx):
        inv = damped_inverse(tiles(blocks, 9, x, dims.ny))
        at = rows_at(dims, x)
        for k in range(9):
            inverse[k, at, :] = inv[k]
        v = times(inv, tiles(rhs, 3, x, dims.ny))
        for c in range(3):
            first[c, at, :] = v[c]
    put_faces(dims, (first, inverse, couplings), (xe, xo, ye, yo))
    put_z(dims, first, refs[6 : 6 + n_z])
    at = 18 * dims.nx
    for piece in pieces:
        ye[at : at + piece.shape[0], :] = piece[:, 0, :]
        at += piece.shape[0]


def second_kernel(dims, counts, inverse, couplings, first, *refs):
    n_inv, n_z = counts
    pieces, refs = refs[:n_inv], refs[n_inv:]
    recv, z_recv, refs = refs[:4], refs[4 : 4 + n_z], refs[4 + n_z :]
    second, sums, *sends = refs[:6]
    z_sends, inverses = refs[6 : 6 + n_z], refs[6 + n_z]
    x_halo, y_halo = received(dims, recv)
    z_halo = ZHalo(dims, z_recv)
    for x in range(dims.nx):
        coup = tiles(couplings, 6, x, dims.ny)
        center, total = sums_at(dims, x, first, x_halo, y_halo, z_halo, coup)
        step = times(tiles(inverse, 9, x, dims.ny), total)
        at = rows_at(dims, x)
        for c in range(3):
            sums[c, at, :] = total[c]
            second[c, at, :] = (2.0 - DAMPING) * center[c] + step[c]
    put_faces(dims, (second,), sends)
    put_z(dims, second, z_sends)
    at = 0
    for piece in pieces:
        inverses[at : at + piece.shape[0], :] = piece[:, 0, :]
        at += piece.shape[0]
    start = 18 * dims.nx
    inverses[at : 2 * at, :] = recv[2][start : start + at, :]


def coarse_kernel(dims, n_z, rhs, sums, couplings, second, ids, *refs):
    recv, z_recv, (packet, resid) = refs[:4], refs[4 : 4 + n_z], refs[4 + n_z :]
    x_halo, y_halo = received(dims, recv)
    z_halo = ZHalo(dims, z_recv)
    rest = 1.0 - DAMPING * (2.0 - DAMPING)
    for x in range(dims.nx):
        coup = tiles(couplings, 6, x, dims.ny)
        _, total = sums_at(dims, x, second, x_halo, y_halo, z_halo, coup)
        at = rows_at(dims, x)
        for c in range(3):
            resid[c, at, :] = rest * rhs[c, at, :] + (total[c] - DAMPING * sums[c, at, :])
    m0, m1 = mode_rows(8, dims.nz)
    row = row_iota(8, dims.nz)
    modes = split3(jnp.where(row == 0, m0, jnp.where(row == 1, m1, 0.0)))
    for c in range(3):
        s = sum(dot_tt(modes, part) for part in parts3(resid[c]))
        packet[0, 2 * c : 2 * c + 2, :] = (s[0:8] + (s[8:16] + s[16:24]))[0:2]
    packet[0, 6:7, :] = pencil_row(dims, ids[0].astype(jnp.float32))
    packet[0, 7:8, :] = jnp.zeros((1, dims.rows), jnp.float32)


def pencil_row(dims, square):
    nx, ny, rows = dims.nx, dims.ny, dims.rows
    lane = lane_iota(ny, rows)
    spread = jnp.where(lax.rem(lane, ny) == row_iota(ny, rows), 1.0, 0.0)
    wide = lax.dot_general(
        square,
        spread,
        (((1,), (0,)), ((), ())),
        precision=lax.Precision.HIGHEST,
        preferred_element_type=jnp.float32,
    )
    lane = lane_iota(nx, rows)
    keep = lax.div(lane, ny) == row_iota(nx, rows)
    return jnp.sum(jnp.where(keep, wide, 0.0), axis=0, keepdims=True)


def gray(j):
    return lax.bitwise_xor(j, lax.shift_right_logical(j, 1))


def gray_inverse(v, bits):
    out = v
    for b in range(1, bits):
        out = lax.bitwise_xor(out, lax.shift_right_logical(v, b))
    return out


def bits_of(n):
    return max(1, (n - 1).bit_length())


def solve_kernel(dims, sizes, own, packets, inverses, stack, y_z, coarse, correction):
    n_y, n_z = sizes
    owners = n_y * n_z
    rows = dims.rows
    my_y, my_z = lax.axis_index("gy"), lax.axis_index("gz")
    local = row_iota(own, rows).astype(jnp.bfloat16)
    one_b = jnp.ones((own, rows), jnp.bfloat16)
    zero_b = jnp.zeros((own, rows), jnp.bfloat16)

    def owner_at(j):
        jz = lax.rem(j, n_z)
        jy = lax.div(j, n_z)
        return lax.bitwise_xor(my_y, gray(jy)) * n_z + lax.bitwise_xor(my_z, gray(jz))

    def member(j, ids):
        base = (owner_at(j) * own).astype(jnp.float32)
        rel = jnp.clip(ids - base, -1.0, float(own)).astype(jnp.bfloat16)
        return jnp.where(local == rel, one_b, zero_b)

    coarse[...] = jnp.zeros_like(coarse)

    def add(d, carry):
        pack = packets[d]
        ids = pack[6:7]
        parts = split3(jnp.where(row_iota(8, rows) < 6, pack, 0.0))
        for j in range(owners):
            s = dot_tt(parts, member(j, ids))
            coarse[8 * j : 8 * j + 8] = coarse[8 * j : 8 * j + 8] + (s[0:8] + (s[8:16] + s[16:24]))
        return carry

    lax.fori_loop(0, owners, add, 0, unroll=2)

    for block in range(owners // 8):
        v = [coarse[pl.ds(64 * block + k, 8, stride=8), :] for k in range(6)]
        for i in range(6):
            total = None
            for k in range(6):
                m = inverses[pl.ds(36 * 8 * block + 6 * i + k, 8, stride=36), :]
                total = m * v[k] if total is None else total + m * v[k]
            correction[pl.ds(64 * block + i, 8, stride=8), :] = total
        for i in (6, 7):
            correction[pl.ds(64 * block + i, 8, stride=8), :] = jnp.zeros_like(total)

    def ids_of(y, z):
        inside = (y >= 0) & (y < n_y) & (z >= 0) & (z < n_z)
        y = jnp.clip(y, 0, n_y - 1)
        z = jnp.clip(z, 0, n_z - 1)
        jy = gray_inverse(lax.bitwise_xor(my_y, y), bits_of(n_y))
        jz = gray_inverse(lax.bitwise_xor(my_z, z), bits_of(n_z))
        return jnp.where(inside, packets[jy * n_z + jz, 6:7, :], -1.0)

    upper = lax.rem(lane_iota(1, rows), dims.ny) >= dims.ny // 2

    def y_ids(z):
        return jnp.where(upper, ids_of(my_y - 1, z), ids_of(my_y + 1, z))

    beyond = [1 - my_z] if n_z == 2 else [my_z - 1, my_z + 1]
    wanted = [ids_of(my_y, my_z), y_ids(my_z)]
    wanted += [ids_of(my_y, z) for z in beyond] + [y_ids(z) for z in beyond]
    totals = [jnp.zeros((24, rows), jnp.float32) for _ in wanted]
    for j in range(owners):
        left = split3(correction[8 * j : 8 * j + 8])
        for t in range(len(wanted)):
            totals[t] = totals[t] + lax.dot_general(
                left,
                member(j, wanted[t]),
                (((1,), (0,)), ((), ())),
                preferred_element_type=jnp.float32,
            )
    totals = [s[0:8] + (s[8:16] + s[16:24]) for s in totals]
    stack[0:8] = totals[0]
    stack[8:16] = totals[1]
    if n_z == 2:
        low = my_z == 1
        for ref, at, value in ((stack, 16, totals[2]), (y_z, 0, totals[3])):
            ref[at : at + 8] = jnp.where(low, value, 0.0)
            ref[at + 8 : at + 16] = jnp.where(low, 0.0, value)
    else:
        stack[16:24], stack[24:32] = totals[2], totals[3]
        y_z[0:8], y_z[8:16] = totals[4], totals[5]


def third_kernel(dims, n_z, inverse, couplings, second, stack, y_z, *refs):
    stacks, fat, thin, refs = refs[:2], refs[2:6], refs[6:10], refs[10:]
    third, x_third, y_third = refs[:3]
    z_sends, refs = refs[3 : 3 + n_z], refs[3 + n_z :]
    field, y_field, z_field, yz_field, x_field, xy_field, xz_field = refs
    nx, ny, nz = dims.nx, dims.ny, dims.nz
    side = nx * ny // 2
    m0, m1 = mode_rows(8, nz)
    row = row_iota(8, nz)
    modes = jnp.concatenate(
        [
            jnp.where(row == 2 * c, m0, jnp.where(row == 2 * c + 1, m1, 0.0))
            for c in range(3)
        ],
        axis=1,
    )
    at = lax.rem(lane_iota(8, 3 * nz), nz)
    wide = pairs6_right(modes)
    last = pairs6_right(jnp.where(at == nz - 1, modes, 0.0))
    start = pairs6_right(jnp.where(at == 0, modes, 0.0))
    x_low = neighbour("gx", [s[:, side:] for s in stacks], False)
    x_high = neighbour("gx", [s[:, :side] for s in stacks], True)
    x_mix = jnp.where(lane_iota(4 * 8, side) < side // 2, x_high, x_low)

    def expand(v, ends=None):
        if ends is None:
            return dot_00(pairs6(v), wide)
        return dot_00(pairs6(v), last) + dot_00(pairs6(ends), start)

    for ref, value in (
        (field, expand(stack[0:8])),
        (y_field, expand(stack[8:16])),
        (z_field, expand(stack[16:24], stack[24:32])),
        (yz_field, expand(y_z[0:8], y_z[8:16])),
        (x_field, expand(x_mix[0:8])),
        (xy_field, expand(x_mix[8:16])),
        (xz_field, expand(x_mix[16:24], x_mix[24:32])),
    ):
        for c in range(3):
            ref[c] = value[:, c * nz : (c + 1) * nz]

    def at_x(own, outer, c, x):
        if 0 <= x < nx:
            return tile(own, c, x, ny)
        return tile(outer, c, side // ny + x if x < 0 else x - nx, ny)

    def update(inv, coup, center, base, pairs):
        step = times(inv, [beside(coup, *pairs(c)) for c in range(3)])
        return [base[c] + ((1.0 - DAMPING) * center[c] + step[c]) for c in range(3)]

    for x in range(-1, nx + 1):
        center = [at_x(field, x_field, c, x) for c in range(3)]

        def pairs(c, x=x, center=center):
            y = at_x(y_field, xy_field, c, x)
            z = at_x(z_field, xz_field, c, x)
            x_pair = (at_x(field, x_field, c, x - 1), at_x(field, x_field, c, x + 1))
            return x_pair, shifted(center[c], y, y, 0), shifted(center[c], z, z, 1)

        if 0 <= x < nx:
            out = update(
                tiles(inverse, 9, x, ny),
                tiles(couplings, 6, x, ny),
                center,
                tiles(second, 3, x, ny),
                pairs,
            )
            for c in range(3):
                third[c, rows_at(dims, x), :] = out[c]
        else:
            high = x == nx
            halo = [
                neighbour("gx", [r[c * ny : (c + 1) * ny, :] for r in fat[:2]], high)
                for c in range(3, 18)
            ]
            base = [
                neighbour("gx", [r[c * ny : (c + 1) * ny, :] for r in thin[:2]], high)
                for c in range(3)
            ]
            out = update(halo[:9], halo[9:], center, base, pairs)
            for c in range(3):
                x_third[int(high), c * ny : (c + 1) * ny, :] = out[c]
    for high in (False, True):
        inner, near, far = (ny - 1, 0, 1) if high else (0, ny - 1, ny - 2)

        def line(ref, c, y):
            return ref[c, pl.ds(y, nx, stride=ny), :]

        center = [line(y_field, c, near) for c in range(3)]

        def pairs(c, center=center, inner=inner, near=near, far=far, high=high):
            low_row = xy_field[c, side - ny + near : side - ny + near + 1, :]
            high_row = xy_field[c, near : near + 1, :]
            y_pair = (line(y_field, c, far), line(field, c, inner))
            z = line(yz_field, c, near)
            return (
                shifted(center[c], low_row, high_row, 0),
                y_pair[::-1] if high else y_pair,
                shifted(center[c], z, z, 1),
            )

        halo = [
            neighbour("gy", [r[c * nx : (c + 1) * nx, :] for r in fat[2:]], high)
            for c in range(3, 18)
        ]
        base = [
            neighbour("gy", [r[c * nx : (c + 1) * nx, :] for r in thin[2:]], high)
            for c in range(3)
        ]
        out = update(halo[:9], halo[9:], center, base, pairs)
        for c in range(3):
            y_third[int(high), c * nx : (c + 1) * nx, :] = out[c]
    put_z(dims, third, z_sends)


def last_kernel(dims, inverse, couplings, first, third, x_third, y_third, *refs):
    z_recv, out = refs[:-1], refs[-1]
    nx, ny = dims.nx, dims.ny

    def x_halo(c, high):
        return x_third[int(high), c * ny : (c + 1) * ny, :]

    def y_halo(c, x, high):
        return y_third[int(high), c * nx + x : c * nx + x + 1, :]

    z_halo = ZHalo(dims, z_recv)
    for x in range(nx):
        coup = tiles(couplings, 6, x, ny)
        center, total = sums_at(dims, x, third, x_halo, y_halo, z_halo, coup)
        step = times(tiles(inverse, 9, x, ny), total)
        at = rows_at(dims, x)
        for c in range(3):
            out[c, at, :] = first[c, at, :] + ((1.0 - DAMPING) * center[c] + step[c])


def pairs_of(count, start):
    out = []
    for i in range(start, count - 1, 2):
        out += [(i, i + 1), (i + 1, i)]
    return out


def swap(value, axis, start):
    return lax.ppermute(value, axis, pairs_of(lax.axis_size(axis), start))


def exchange(sends, z_sends):
    xe, xo, ye, yo = sends
    z_recv = [swap(v, "gz", k) for k, v in enumerate(z_sends)]
    yo, ye = swap(yo, "gy", 1), swap(ye, "gy", 0)
    xo, xe = swap(xo, "gx", 1), swap(xe, "gx", 0)
    return [xe, xo, ye, yo], z_recv


def stages(axis, first=0):
    masks = []
    mask = 1
    while mask < lax.axis_size(axis):
        masks.append([(i, i ^ mask) for i in range(lax.axis_size(axis))])
        mask = 2 * mask + 1
    return masks[first:]


def gather_along(value, axis, first=0):
    for which in stages(axis, first):
        value = jnp.concatenate([value, lax.ppermute(value, axis, which)], axis=0)
    return value


def call(body, name, out_shapes, scratch, *args):
    return pl.pallas_call(
        body,
        name=name,
        out_shape=[jax.ShapeDtypeStruct(s, jnp.float32) for s in out_shapes],
        in_specs=[pl.BlockSpec(memory_space=pltpu.VMEM)] * len(args),
        out_specs=[pl.BlockSpec(memory_space=pltpu.VMEM)] * len(out_shapes),
        scratch_shapes=scratch,
        compiler_params=pltpu.CompilerParams(vmem_limit_bytes=VMEM_LIMIT),
    )(*args)


def shards(rhs, blocks, couplings, agg_ids, coarse_inv):
    _, nx, ny, nz = rhs.shape
    dims = Dims(nx, ny, nz)
    rows = nx * ny
    rhs = rhs.reshape(3, rows, nz)
    blocks = blocks.reshape(9, rows, nz)
    couplings = couplings.reshape(6, rows, nz)
    own = coarse_inv.shape[2]
    n_y, n_z = lax.axis_size("gy"), lax.axis_size("gz")
    owners = n_y * n_z
    z_count = 1 if n_z == 2 else 2
    vector = (3, rows, nz)
    part = functools.partial
    f32 = jnp.float32

    def faces(count, extra=0):
        return [(count * ny, nz)] * 2 + [(count * nx + extra, nz), (count * nx, nz)]

    z_faces = [(8, nz)] * z_count
    pieces = [coarse_inv]
    for which in stages("gz"):
        joined = jnp.concatenate(pieces, axis=0) if len(pieces) > 1 else pieces[0]
        pieces.append(lax.ppermute(joined, "gz", which))
    counts = (len(pieces), z_count)
    inv_rows = 36 * n_z

    first, inverse, *sends = call(
        part(first_kernel, dims, counts),
        "first",
        [vector, (9, rows, nz)] + faces(18, inv_rows) + z_faces,
        [],
        rhs,
        blocks,
        couplings,
        *pieces,
    )
    fat, z_recv = exchange(sends[:4], sends[4:])
    second, sums, *sends = call(
        part(second_kernel, dims, counts),
        "second",
        [vector, vector] + faces(3) + z_faces + [(2 * inv_rows, own)],
        [],
        inverse,
        couplings,
        first,
        *pieces,
        *fat,
        *z_recv,
    )
    inverses = gather_along(sends[-1], "gy", 1)
    thin, z_recv = exchange(sends[:4], sends[4:-1])
    (packet,) = call(
        part(coarse_kernel, dims, z_count),
        "coarse",
        [(1, 8, rows)],
        [pltpu.VMEM(vector, f32)],
        rhs,
        sums,
        couplings,
        second,
        agg_ids,
        *thin,
        *z_recv,
    )
    packets = gather_along(gather_along(packet, "gz"), "gy")
    stack, y_z = call(
        part(solve_kernel, dims, (n_y, n_z), own),
        "solve",
        [(4 * 8, rows), (2 * 8, rows)],
        [pltpu.VMEM((owners * 8, own), f32)] * 2,
        packets,
        inverses,
    )
    xo, xe = swap(stack, "gx", 1), swap(stack, "gx", 0)
    third, x_third, y_third, *z_sends = call(
        part(third_kernel, dims, z_count),
        "third",
        [vector, (2, 3 * ny, nz), (2, 3 * nx, nz)] + z_faces,
        [pltpu.VMEM(vector, f32)] * 4 + [pltpu.VMEM((3, rows // 2, nz), f32)] * 3,
        inverse,
        couplings,
        second,
        stack,
        y_z,
        xe,
        xo,
        *fat,
        *thin,
    )
    z_recv = [swap(v, "gz", k) for k, v in enumerate(z_sends)]
    (out,) = call(
        part(last_kernel, dims),
        "last",
        [vector],
        [],
        inverse,
        couplings,
        first,
        third,
        x_third,
        y_third,
        *z_recv,
    )
    return out.reshape(3, nx, ny, nz)


def solution(mesh):
    return jax.shard_map(
        shards,
        mesh=mesh,
        in_specs=(
            P(None, "gx", "gy", "gz"),
            P(None, "gx", "gy", "gz"),
            P(None, "gx", "gy", "gz"),
            P("gz", "gx", "gy"),
            P(None, "gx", ("gy", "gz")),
        ),
        out_specs=P(None, "gx", "gy", "gz"),
        check_vma=False,
    )
```

```python
import functools

import jax
import jax.numpy as jnp
from jax import lax
from jax.experimental import pallas as pl
from jax.experimental.pallas import tpu as pltpu
from jax.sharding import PartitionSpec as P

DAMPING = 0.8
AXES = ("gx", "gy", "gz")
VMEM_LIMIT = 12 * 1024 * 1024


def dot_tt(a, b):
    return lax.dot_general(
        a, b, (((1,), (1,)), ((), ())), preferred_element_type=jnp.float32
    )


def dot_00(a, b):
    return lax.dot_general(
        a, b, (((0,), (0,)), ((), ())), preferred_element_type=jnp.float32
    )


def parts3(v):
    high = v.astype(jnp.bfloat16)
    rest = v - high.astype(jnp.float32)
    mid = rest.astype(jnp.bfloat16)
    low = (rest - mid.astype(jnp.float32)).astype(jnp.bfloat16)
    return high, mid, low


def split3(v):
    return jnp.concatenate(parts3(v), axis=0)


def pairs6(v):
    high, mid, low = parts3(v)
    return jnp.concatenate([high, high, high, mid, mid, low], axis=0)


def pairs6_right(v):
    high, mid, low = parts3(v)
    return jnp.concatenate([high, mid, low, high, mid, high], axis=0)


def lane_iota(rows, lanes):
    return lax.broadcasted_iota(jnp.int32, (rows, lanes), 1)


def row_iota(rows, lanes):
    return lax.broadcasted_iota(jnp.int32, (rows, lanes), 0)


def mode_rows(rows, length):
    k = lane_iota(rows, length).astype(jnp.float32)
    m1 = (k - (length - 1) / 2.0) / (length / 2.0) * (3.0 / length) ** 0.5
    m0 = jnp.full((rows, length), length ** (-0.5), jnp.float32)
    return m0, m1


def is_even(axis):
    return lax.rem(lax.axis_index(axis), 2) == 0


def damped_inverse(m):
    a, b, c, d, e, f, g, h, i = m
    co_a = e * i - f * h
    co_b = f * g - d * i
    co_c = d * h - e * g
    determ = a * co_a + b * co_b + c * co_c
    scale = DAMPING / determ
    rows = [
        co_a,
        c * h - b * i,
        b * f - c * e,
        co_b,
        a * i - c * g,
        c * d - a * f,
        co_c,
        b * g - a * h,
        a * e - b * d,
    ]
    return [r * scale for r in rows]


def times(m, v):
    return [m[3 * r] * v[0] + m[3 * r + 1] * v[1] + m[3 * r + 2] * v[2] for r in range(3)]


class Dims:
    def __init__(self, nx, ny, nz):
        self.nx, self.ny, self.nz = nx, ny, nz
        self.rows = nx * ny
        self.groups = self.rows // 8


def tile(ref, c, x, size):
    return ref[c, x * size : (x + 1) * size, :]


def tiles(ref, count, x, size):
    return [tile(ref, c, x, size) for c in range(count)]


def flat_tiles(ref, start, count, size):
    return [ref[(start + c) * size : (start + c + 1) * size, :] for c in range(count)]


def face_index(axis, count):
    even = jnp.where(is_even(axis), count - 1, 0)
    return even, (count - 1) - even


def inner_odd(axis, value):
    count = lax.axis_size(axis)
    at = lax.axis_index(axis)
    return jnp.where((at > 0) & (at < count - 1), value, 0.0)


def put_faces(dims, fields, sends):
    xe, xo, ye, yo = sends
    nx, ny = dims.nx, dims.ny
    x_e, x_o = face_index("gx", nx)
    y_e, y_o = face_index("gy", ny)
    at = 0
    for field in fields:
        for c in range(field.shape[0]):
            x_rows = slice(at * ny, (at + 1) * ny)
            y_rows = slice(at * nx, (at + 1) * nx)
            xe[x_rows, :] = field[c, pl.ds(pl.multiple_of(x_e * ny, ny), ny), :]
            v = field[c, pl.ds(pl.multiple_of(x_o * ny, ny), ny), :]
            xo[x_rows, :] = inner_odd("gx", v)
            ye[y_rows, :] = field[c, pl.ds(y_e, nx, stride=ny), :]
            yo[y_rows, :] = inner_odd("gy", field[c, pl.ds(y_o, nx, stride=ny), :])
            at += 1


def put_z(dims, field, sends):
    groups, nz = dims.groups, dims.nz
    lane = lane_iota(8, nz)
    for odd, (ref, k) in enumerate(zip(sends, face_index("gz", nz))):
        to = lax.rem(lane + nz - k, nz)
        total = []
        for c in range(3):
            face = jnp.zeros((8, nz), jnp.float32)
            for g in range(groups):
                at = c * groups + g
                face = jnp.where(to == at, pltpu.roll(field[c, 8 * g : 8 * g + 8, :], at, 1), face)
            total.append(face)
        face = pltpu.roll(total[0] + total[1] + total[2], lax.rem(nz - k, nz), 1)
        ref[0:8, :] = inner_odd("gz", face) if odd else face


def neighbour(axis, pair, high):
    e, o = pair
    even = is_even(axis)
    return jnp.where(even, e, o) if high else jnp.where(even, o, e)


class ZHalo:
    def __init__(self, dims, recv):
        self.dims = dims
        self.recv = [r[0:8, :] for r in recv]
        if len(recv) == 2:
            self.low = neighbour("gz", self.recv, False)
            self.high = neighbour("gz", self.recv, True)
        else:
            self.low = self.high = None
            self.at = jnp.where(is_even("gz"), 0, dims.nz - 1)
            self.moved = pltpu.roll(self.recv[0], self.at, 1)

    def tile(self, c, x):
        dims = self.dims
        nz = dims.nz
        lane = lane_iota(8, nz)
        per = dims.ny // 8
        out = []
        for g in range(x * per, (x + 1) * per):
            at = c * dims.groups + g
            if self.low is None:
                v = pltpu.roll(self.moved, (nz - at) % nz, 1)
                out.append(jnp.where(lane == self.at, v, 0.0))
            else:
                low = pltpu.roll(self.low, (nz - 1 - at) % nz, 1)
                high = pltpu.roll(self.high, (nz - at) % nz, 1)
                out.append(jnp.where(lane == nz - 1, low, high))
        return jnp.concatenate(out, axis=0) if per > 1 else out[0]


def shifted(v, low, high, axis):
    size = v.shape[axis]
    at = lax.broadcasted_iota(jnp.int32, v.shape, axis)
    below = pltpu.roll(jnp.where(at == size - 1, low, v), 1, axis)
    above = pltpu.roll(jnp.where(at == 0, high, v), size - 1, axis)
    return below, above


def beside(coup, x_pair, y_pair, z_pair):
    return (
        coup[0] * x_pair[0]
        + coup[1] * x_pair[1]
        + (coup[2] * y_pair[0] + coup[3] * y_pair[1])
        + (coup[4] * z_pair[0] + coup[5] * z_pair[1])
    )


def sums_at(dims, x, field, x_halo, y_halo, z_halo, coup):
    nx, ny = dims.nx, dims.ny
    center = tiles(field, 3, x, ny)
    out = []
    for c in range(3):
        low = tile(field, c, x - 1, ny) if x > 0 else x_halo(c, False)
        high = tile(field, c, x + 1, ny) if x < nx - 1 else x_halo(c, True)
        y_pair = shifted(center[c], y_halo(c, x, False), y_halo(c, x, True), 0)
        z = z_halo.tile(c, x)
        z_pair = shifted(center[c], z, z, 1)
        out.append(beside(coup, (low, high), y_pair, z_pair))
    return center, out


def received(dims, recv):
    xe, xo, ye, yo = recv
    nx, ny = dims.nx, dims.ny

    def x_halo(c, high):
        pair = [r[c * ny : (c + 1) * ny, :] for r in (xe, xo)]
        return neighbour("gx", pair, high)

    def y_halo(c, x, high):
        pair = [r[c * nx + x : c * nx + x + 1, :] for r in (ye, yo)]
        return neighbour("gy", pair, high)

    return x_halo, y_halo


def rows_at(dims, x):
    return slice(x * dims.ny, (x + 1) * dims.ny)


def put_inverses(ref, start, pieces):
    for piece in pieces:
        ref[start : start + 36, :] = piece
        start += 36


CHUNKS = 4


def first_kernel(dims, n_z, *refs):
    rhs_in, blocks_in, couplings_in, coarse_inv = refs[:4]
    first, inverse, rhs, couplings, xe, xo, ye, yo = refs[4:12]
    z_sends, (blocks, sems) = refs[12 : 12 + n_z], refs[12 + n_z :]
    step = dims.rows // CHUNKS

    def copy(k, src, dst, rows):
        return pltpu.make_async_copy(src.at[:, rows, :], dst.at[:, rows, :], sems.at[k])

    copies = []
    for k in range(CHUNKS):
        rows = pl.ds(k * step, step)
        copies.append(copy(2 * k, blocks_in, blocks, rows))
        copies.append(copy(2 * k + 1, rhs_in, rhs, rows))
    copies.append(copy(2 * CHUNKS, couplings_in, couplings, pl.ds(0, dims.rows)))
    for c in copies:
        c.start()
    for x in range(dims.nx):
        if x % (dims.nx // CHUNKS) == 0:
            k = x // (dims.nx // CHUNKS)
            copies[2 * k].wait()
            copies[2 * k + 1].wait()
        inv = damped_inverse(tiles(blocks, 9, x, dims.ny))
        at = rows_at(dims, x)
        for k in range(9):
            inverse[k, at, :] = inv[k]
        v = times(inv, tiles(rhs, 3, x, dims.ny))
        for c in range(3):
            first[c, at, :] = v[c]
    copies[-1].wait()
    put_faces(dims, (first, inverse, couplings), (xe, xo, ye, yo))
    put_z(dims, first, z_sends)
    own = coarse_inv[:, 0, :]
    put_inverses(ye, 18 * dims.nx, [own])
    put_inverses(yo, 18 * dims.nx, [own])
    put_inverses(z_sends[0], 8, [own])


def second_kernel(dims, n_z, inverse, couplings, first, *refs):
    recv, z_recv, refs = refs[:4], refs[4 : 4 + n_z], refs[4 + n_z :]
    second, sums, *sends = refs[:6]
    z_sends = refs[6:]
    x_halo, y_halo = received(dims, recv)
    z_halo = ZHalo(dims, z_recv)
    for x in range(dims.nx):
        coup = tiles(couplings, 6, x, dims.ny)
        center, total = sums_at(dims, x, first, x_halo, y_halo, z_halo, coup)
        step = times(tiles(inverse, 9, x, dims.ny), total)
        at = rows_at(dims, x)
        for c in range(3):
            sums[c, at, :] = total[c]
            second[c, at, :] = (2.0 - DAMPING) * center[c] + step[c]
    put_faces(dims, (second,), sends)
    put_z(dims, second, z_sends)
    even_block, odd_block = [r[18 * dims.nx : 18 * dims.nx + 36, :] for r in recv[2:]]
    put_inverses(sends[2], 3 * dims.nx, [odd_block])
    put_inverses(z_sends[0], 8, [even_block, odd_block])


def coarse_kernel(dims, n_z, rhs, sums, couplings, second, ids, *refs):
    recv, z_recv, (packets, packet, resid) = refs[:4], refs[4 : 4 + n_z], refs[4 + n_z :]
    x_halo, y_halo = received(dims, recv)
    z_halo = ZHalo(dims, z_recv)
    rest = 1.0 - DAMPING * (2.0 - DAMPING)
    for x in range(dims.nx):
        coup = tiles(couplings, 6, x, dims.ny)
        _, total = sums_at(dims, x, second, x_halo, y_halo, z_halo, coup)
        at = rows_at(dims, x)
        for c in range(3):
            resid[c, at, :] = rest * rhs[c, at, :] + (total[c] - DAMPING * sums[c, at, :])
    m0, m1 = mode_rows(8, dims.nz)
    row = row_iota(8, dims.nz)
    modes = split3(jnp.where(row == 0, m0, jnp.where(row == 1, m1, 0.0)))
    for c in range(3):
        s = sum(dot_tt(modes, part) for part in parts3(resid[c]))
        packet[2 * c : 2 * c + 2, :] = (s[0:8] + (s[8:16] + s[16:24]))[0:2]
    packet[6:7, :] = pencil_row(dims, ids[0].astype(jnp.float32))
    packet[7:8, :] = jnp.zeros((1, dims.rows), jnp.float32)
    for d in range(packets.shape[0]):
        packets[d] = packet[...]


def pencil_row(dims, square):
    nx, ny, rows = dims.nx, dims.ny, dims.rows
    lane = lane_iota(ny, rows)
    spread = jnp.where(lax.rem(lane, ny) == row_iota(ny, rows), 1.0, 0.0)
    wide = lax.dot_general(
        square,
        spread,
        (((1,), (0,)), ((), ())),
        precision=lax.Precision.HIGHEST,
        preferred_element_type=jnp.float32,
    )
    lane = lane_iota(nx, rows)
    keep = lax.div(lane, ny) == row_iota(nx, rows)
    return jnp.sum(jnp.where(keep, wide, 0.0), axis=0, keepdims=True)


def partner(index, count, odd):
    if odd:
        return ((index + 1) % count ^ 1) - 1 + (((index + 1) % count ^ 1) == 0) * count
    return index ^ 1


def follow(index, count, word):
    for odd in word:
        index = partner(index, count, odd)
    return index


def words_of(count):
    words, seen = [], set()
    for length in range(count):
        for start in (False, True):
            word = tuple(bool(start) ^ bool(k % 2) for k in range(length))
            to = follow(0, count, word)
            if to not in seen:
                seen.add(to)
                words.append(word)
    return words


def blocks_of(n_y, n_z):
    e, o, none = (False,), (True,), ()
    held = [(none, none), (e, none), (o, none), (none, e), (e, e), (o, e), (e + o, none)]
    found = {(follow(0, n_y, y), follow(0, n_z, z)) for y, z in held}
    rest = []
    for y in words_of(n_y):
        for z in words_of(n_z):
            at = (follow(0, n_y, y), follow(0, n_z, z))
            if at not in found:
                found.add(at)
                rest.append((y, z))
    return held, rest


def solve_kernel(dims, sizes, own, packets, coarse_inv, *refs):
    n_y, n_z = sizes
    owners = n_y * n_z
    rows = dims.rows
    held, rest = blocks_of(n_y, n_z)
    pieces, refs = refs[: 5 + len(rest)], refs[5 + len(rest) :]
    stack, y_z, coarse, correction, inverses = refs
    put_inverses(inverses, 0, [coarse_inv[:, 0, :]])
    at = 36
    fat_ye, fat_yo, fat_z, thin_ye, thin_z = pieces[:5]
    for ref, start, count in (
        (fat_ye, 18 * dims.nx, 36),
        (fat_yo, 18 * dims.nx, 36),
        (fat_z, 8, 36),
        (thin_z, 8, 72),
        (thin_ye, 3 * dims.nx, 36),
    ):
        inverses[at : at + count, :] = ref[start : start + count, :]
        at += count
    for piece in pieces[5:]:
        put_inverses(inverses, at, [piece[:, 0, :]])
        at += 36
    order = held + rest
    my_y, my_z = lax.axis_index("gy"), lax.axis_index("gz")
    local = row_iota(own, rows).astype(jnp.bfloat16)
    one_b = jnp.ones((own, rows), jnp.bfloat16)
    zero_b = jnp.zeros((own, rows), jnp.bfloat16)

    def owner_at(j):
        y, z = order[j]
        return follow(my_y, n_y, y) * n_z + follow(my_z, n_z, z)

    def member(j, ids):
        base = (owner_at(j) * own).astype(jnp.float32)
        rel = jnp.clip(ids - base, -1.0, float(own)).astype(jnp.bfloat16)
        return jnp.where(local == rel, one_b, zero_b)

    coarse[...] = jnp.zeros_like(coarse)

    def add(d, carry):
        pack = packets[d]
        ids = pack[6:7]
        parts = split3(jnp.where(row_iota(8, rows) < 6, pack, 0.0))
        for j in range(owners):
            s = dot_tt(parts, member(j, ids))
            coarse[8 * j : 8 * j + 8] = coarse[8 * j : 8 * j + 8] + (s[0:8] + (s[8:16] + s[16:24]))
        return carry

    lax.fori_loop(0, owners, add, 0, unroll=2)

    for block in range(owners // 8):
        v = [coarse[pl.ds(64 * block + k, 8, stride=8), :] for k in range(6)]
        for i in range(6):
            total = None
            for k in range(6):
                m = inverses[pl.ds(36 * 8 * block + 6 * i + k, 8, stride=36), :]
                total = m * v[k] if total is None else total + m * v[k]
            correction[pl.ds(64 * block + i, 8, stride=8), :] = total
        for i in (6, 7):
            correction[pl.ds(64 * block + i, 8, stride=8), :] = jnp.zeros_like(total)

    def ids_of(y, z):
        inside = (y >= 0) & (y < n_y) & (z >= 0) & (z < n_z)
        y = jnp.clip(y, 0, n_y - 1)
        z = jnp.clip(z, 0, n_z - 1)
        return jnp.where(inside, packets[y * n_z + z, 6:7, :], -1.0)

    upper = lax.rem(lane_iota(1, rows), dims.ny) >= dims.ny // 2

    def y_ids(z):
        return jnp.where(upper, ids_of(my_y - 1, z), ids_of(my_y + 1, z))

    beyond = [1 - my_z] if n_z == 2 else [my_z - 1, my_z + 1]
    wanted = [ids_of(my_y, my_z), y_ids(my_z)]
    wanted += [ids_of(my_y, z) for z in beyond] + [y_ids(z) for z in beyond]
    totals = [jnp.zeros((24, rows), jnp.float32) for _ in wanted]
    for j in range(owners):
        left = split3(correction[8 * j : 8 * j + 8])
        for t in range(len(wanted)):
            totals[t] = totals[t] + lax.dot_general(
                left,
                member(j, wanted[t]),
                (((1,), (0,)), ((), ())),
                preferred_element_type=jnp.float32,
            )
    totals = [s[0:8] + (s[8:16] + s[16:24]) for s in totals]
    stack[0:8] = totals[0]
    stack[8:16] = totals[1]
    if n_z == 2:
        low = my_z == 1
        for ref, at, value in ((stack, 16, totals[2]), (y_z, 0, totals[3])):
            ref[at : at + 8] = jnp.where(low, value, 0.0)
            ref[at + 8 : at + 16] = jnp.where(low, 0.0, value)
    else:
        stack[16:24], stack[24:32] = totals[2], totals[3]
        y_z[0:8], y_z[8:16] = totals[4], totals[5]


def third_kernel(dims, n_z, inverse, couplings, second, stack, y_z, *refs):
    stacks, fat, thin, refs = refs[:2], refs[2:6], refs[6:10], refs[10:]
    third, x_third, y_third = refs[:3]
    z_sends, refs = refs[3 : 3 + n_z], refs[3 + n_z :]
    field, y_field, z_field, yz_field, x_field, xy_field, xz_field = refs
    nx, ny, nz = dims.nx, dims.ny, dims.nz
    side = nx * ny // 2
    m0, m1 = mode_rows(8, nz)
    row = row_iota(8, nz)
    modes = jnp.concatenate(
        [
            jnp.where(row == 2 * c, m0, jnp.where(row == 2 * c + 1, m1, 0.0))
            for c in range(3)
        ],
        axis=1,
    )
    at = lax.rem(lane_iota(8, 3 * nz), nz)
    wide = pairs6_right(modes)
    last = pairs6_right(jnp.where(at == nz - 1, modes, 0.0))
    start = pairs6_right(jnp.where(at == 0, modes, 0.0))
    my_x, n_x = lax.axis_index("gx"), lax.axis_size("gx")
    x_low = neighbour("gx", [s[:, side:] for s in stacks], False)
    x_high = neighbour("gx", [s[:, :side] for s in stacks], True)
    x_low = jnp.where(my_x > 0, x_low, 0.0)
    x_high = jnp.where(my_x < n_x - 1, x_high, 0.0)
    x_mix = jnp.where(lane_iota(4 * 8, side) < side // 2, x_high, x_low)

    def expand(v, ends=None):
        if ends is None:
            return dot_00(pairs6(v), wide)
        return dot_00(pairs6(v), last) + dot_00(pairs6(ends), start)

    for ref, value in (
        (field, expand(stack[0:8])),
        (y_field, expand(stack[8:16])),
        (z_field, expand(stack[16:24], stack[24:32])),
        (yz_field, expand(y_z[0:8], y_z[8:16])),
        (x_field, expand(x_mix[0:8])),
        (xy_field, expand(x_mix[8:16])),
        (xz_field, expand(x_mix[16:24], x_mix[24:32])),
    ):
        for c in range(3):
            ref[c] = value[:, c * nz : (c + 1) * nz]

    def at_x(own, outer, c, x):
        if 0 <= x < nx:
            return tile(own, c, x, ny)
        return tile(outer, c, side // ny + x if x < 0 else x - nx, ny)

    def update(inv, coup, center, base, pairs):
        step = times(inv, [beside(coup, *pairs(c)) for c in range(3)])
        return [base[c] + ((1.0 - DAMPING) * center[c] + step[c]) for c in range(3)]

    for x in range(-1, nx + 1):
        center = [at_x(field, x_field, c, x) for c in range(3)]

        def pairs(c, x=x, center=center):
            y = at_x(y_field, xy_field, c, x)
            z = at_x(z_field, xz_field, c, x)
            x_pair = (at_x(field, x_field, c, x - 1), at_x(field, x_field, c, x + 1))
            return x_pair, shifted(center[c], y, y, 0), shifted(center[c], z, z, 1)

        if 0 <= x < nx:
            out = update(
                tiles(inverse, 9, x, ny),
                tiles(couplings, 6, x, ny),
                center,
                tiles(second, 3, x, ny),
                pairs,
            )
            for c in range(3):
                third[c, rows_at(dims, x), :] = out[c]
        else:
            high = x == nx
            halo = [
                neighbour("gx", [r[c * ny : (c + 1) * ny, :] for r in fat[:2]], high)
                for c in range(3, 18)
            ]
            base = [
                neighbour("gx", [r[c * ny : (c + 1) * ny, :] for r in thin[:2]], high)
                for c in range(3)
            ]
            out = update(halo[:9], halo[9:], center, base, pairs)
            for c in range(3):
                x_third[int(high), c * ny : (c + 1) * ny, :] = out[c]
    for high in (False, True):
        inner, near, far = (ny - 1, 0, 1) if high else (0, ny - 1, ny - 2)

        def line(ref, c, y):
            return ref[c, pl.ds(y, nx, stride=ny), :]

        center = [line(y_field, c, near) for c in range(3)]

        def pairs(c, center=center, inner=inner, near=near, far=far, high=high):
            low_row = xy_field[c, side - ny + near : side - ny + near + 1, :]
            high_row = xy_field[c, near : near + 1, :]
            y_pair = (line(y_field, c, far), line(field, c, inner))
            z = line(yz_field, c, near)
            return (
                shifted(center[c], low_row, high_row, 0),
                y_pair[::-1] if high else y_pair,
                shifted(center[c], z, z, 1),
            )

        halo = [
            neighbour("gy", [r[c * nx : (c + 1) * nx, :] for r in fat[2:]], high)
            for c in range(3, 18)
        ]
        base = [
            neighbour("gy", [r[c * nx : (c + 1) * nx, :] for r in thin[2:]], high)
            for c in range(3)
        ]
        out = update(halo[:9], halo[9:], center, base, pairs)
        for c in range(3):
            y_third[int(high), c * nx : (c + 1) * nx, :] = out[c]
    put_z(dims, third, z_sends)


def last_kernel(dims, inverse, couplings, first, third, x_third, y_third, *refs):
    z_recv, out = refs[:-1], refs[-1]
    nx, ny = dims.nx, dims.ny

    def x_halo(c, high):
        return x_third[int(high), c * ny : (c + 1) * ny, :]

    def y_halo(c, x, high):
        return y_third[int(high), c * nx + x : c * nx + x + 1, :]

    z_halo = ZHalo(dims, z_recv)
    for x in range(nx):
        coup = tiles(couplings, 6, x, ny)
        center, total = sums_at(dims, x, third, x_halo, y_halo, z_halo, coup)
        step = times(tiles(inverse, 9, x, ny), total)
        at = rows_at(dims, x)
        for c in range(3):
            out[c, at, :] = first[c, at, :] + ((1.0 - DAMPING) * center[c] + step[c])


def swap(value, axis, odd):
    count = lax.axis_size(axis)
    return lax.ppermute(value, axis, [(partner(i, count, odd), i) for i in range(count)])


def exchange(sends, z_sends):
    xe, xo, ye, yo = sends
    xe = swap(xe, "gx", 0)
    z_recv = [swap(v, "gz", k) for k, v in enumerate(z_sends)]
    ye, yo = swap(ye, "gy", 0), swap(yo, "gy", 1)
    xo = swap(xo, "gx", 1)
    return [xe, xo, ye, yo], z_recv


def fetch(value, word_y, word_z):
    n_y, n_z = lax.axis_size("gy"), lax.axis_size("gz")
    which = []
    for y in range(n_y):
        for z in range(n_z):
            source = follow(y, n_y, word_y) * n_z + follow(z, n_z, word_z)
            which.append((source, y * n_z + z))
    return lax.ppermute(value, ("gy", "gz"), which)


def call(body, name, out_shapes, scratch, *args, in_hbm=0):
    near = pl.BlockSpec(memory_space=pltpu.VMEM)
    far = pl.BlockSpec(memory_space=pl.ANY)
    return pl.pallas_call(
        body,
        name=name,
        out_shape=[jax.ShapeDtypeStruct(s, jnp.float32) for s in out_shapes],
        in_specs=[far] * in_hbm + [near] * (len(args) - in_hbm),
        out_specs=[near] * len(out_shapes),
        scratch_shapes=scratch,
        compiler_params=pltpu.CompilerParams(vmem_limit_bytes=VMEM_LIMIT),
    )(*args)


def shards(rhs, blocks, couplings, agg_ids, coarse_inv):
    _, nx, ny, nz = rhs.shape
    dims = Dims(nx, ny, nz)
    rows = nx * ny
    rhs = rhs.reshape(3, rows, nz)
    blocks = blocks.reshape(9, rows, nz)
    couplings = couplings.reshape(6, rows, nz)
    own = coarse_inv.shape[2]
    n_y, n_z = lax.axis_size("gy"), lax.axis_size("gz")
    owners = n_y * n_z
    z_count = 1 if n_z == 2 else 2
    vector = (3, rows, nz)
    part = functools.partial
    f32 = jnp.float32

    def faces(count, even, odd):
        return [(count * ny, nz)] * 2 + [(count * nx + even, nz), (count * nx + odd, nz)]

    def z_faces(extra):
        return [(8 + extra, nz)] + [(8, nz)] * (z_count - 1)

    _, rest = blocks_of(n_y, n_z)
    pieces = [fetch(coarse_inv, y, z) for y, z in rest]
    first, inverse, rhs, couplings, *sends = call(
        part(first_kernel, dims, z_count),
        "first",
        [vector, (9, rows, nz), vector, (6, rows, nz)] + faces(18, 36, 36) + z_faces(36),
        [pltpu.VMEM((9, rows, nz), f32), pltpu.SemaphoreType.DMA((2 * CHUNKS + 1,))],
        rhs,
        blocks,
        couplings,
        coarse_inv,
        in_hbm=3,
    )
    fat, fat_z = exchange(sends[:4], sends[4:])
    second, sums, *sends = call(
        part(second_kernel, dims, z_count),
        "second",
        [vector, vector] + faces(3, 36, 0) + z_faces(72),
        [],
        inverse,
        couplings,
        first,
        *fat,
        *fat_z,
    )
    thin, thin_z = exchange(sends[:4], sends[4:])
    (packets,) = call(
        part(coarse_kernel, dims, z_count),
        "coarse",
        [(owners, 8, rows)],
        [pltpu.VMEM((8, rows), f32), pltpu.VMEM(vector, f32)],
        rhs,
        sums,
        couplings,
        second,
        agg_ids,
        *thin,
        *thin_z,
    )
    packets = lax.all_to_all(packets, ("gy", "gz"), 0, 0, tiled=True)
    stack, y_z = call(
        part(solve_kernel, dims, (n_y, n_z), own),
        "solve",
        [(4 * 8, rows), (2 * 8, rows)],
        [pltpu.VMEM((owners * 8, own), f32)] * 2 + [pltpu.VMEM((owners * 36, own), f32)],
        packets,
        coarse_inv,
        fat[2],
        fat[3],
        fat_z[0],
        thin[2],
        thin_z[0],
        *pieces,
    )
    xe, xo = swap(stack, "gx", 0), swap(stack, "gx", 1)
    third, x_third, y_third, *z_sends = call(
        part(third_kernel, dims, z_count),
        "third",
        [vector, (2, 3 * ny, nz), (2, 3 * nx, nz)] + z_faces(0),
        [pltpu.VMEM(vector, f32)] * 4 + [pltpu.VMEM((3, rows // 2, nz), f32)] * 3,
        inverse,
        couplings,
        second,
        stack,
        y_z,
        xe,
        xo,
        *fat,
        *thin,
    )
    z_recv = [swap(v, "gz", k) for k, v in enumerate(z_sends)]
    (out,) = call(
        part(last_kernel, dims),
        "last",
        [vector],
        [],
        inverse,
        couplings,
        first,
        third,
        x_third,
        y_third,
        *z_recv,
    )
    return out.reshape(3, nx, ny, nz)


def solution(mesh):
    return jax.shard_map(
        shards,
        mesh=mesh,
        in_specs=(
            P(None, "gx", "gy", "gz"),
            P(None, "gx", "gy", "gz"),
            P(None, "gx", "gy", "gz"),
            P("gz", "gx", "gy"),
            P(None, "gx", ("gy", "gz")),
        ),
        out_specs=P(None, "gx", "gy", "gz"),
        check_vma=False,
    )
```

```python
import functools

import jax
import jax.numpy as jnp
from jax import lax
from jax.experimental import pallas as pl
from jax.experimental.pallas import tpu as pltpu
from jax.sharding import PartitionSpec as P

DAMPING = 0.8
AXES = ("gx", "gy", "gz")
VMEM_LIMIT = 12 * 1024 * 1024


def dot_tt(a, b):
    return lax.dot_general(
        a, b, (((1,), (1,)), ((), ())), preferred_element_type=jnp.float32
    )


def dot_00(a, b):
    return lax.dot_general(
        a, b, (((0,), (0,)), ((), ())), preferred_element_type=jnp.float32
    )


def parts3(v):
    high = v.astype(jnp.bfloat16)
    rest = v - high.astype(jnp.float32)
    mid = rest.astype(jnp.bfloat16)
    low = (rest - mid.astype(jnp.float32)).astype(jnp.bfloat16)
    return high, mid, low


def split3(v):
    return jnp.concatenate(parts3(v), axis=0)


def pairs6(v):
    high, mid, low = parts3(v)
    return jnp.concatenate([high, high, high, mid, mid, low], axis=0)


def pairs6_right(v):
    high, mid, low = parts3(v)
    return jnp.concatenate([high, mid, low, high, mid, high], axis=0)


def lane_iota(rows, lanes):
    return lax.broadcasted_iota(jnp.int32, (rows, lanes), 1)


def row_iota(rows, lanes):
    return lax.broadcasted_iota(jnp.int32, (rows, lanes), 0)


def mode_rows(rows, length):
    k = lane_iota(rows, length).astype(jnp.float32)
    m1 = (k - (length - 1) / 2.0) / (length / 2.0) * (3.0 / length) ** 0.5
    m0 = jnp.full((rows, length), length ** (-0.5), jnp.float32)
    return m0, m1


def is_even(axis):
    return lax.rem(lax.axis_index(axis), 2) == 0


def damped_inverse(m):
    a, b, c, d, e, f, g, h, i = m
    co_a = e * i - f * h
    co_b = f * g - d * i
    co_c = d * h - e * g
    determ = a * co_a + b * co_b + c * co_c
    scale = DAMPING / determ
    rows = [
        co_a,
        c * h - b * i,
        b * f - c * e,
        co_b,
        a * i - c * g,
        c * d - a * f,
        co_c,
        b * g - a * h,
        a * e - b * d,
    ]
    return [r * scale for r in rows]


def times(m, v):
    return [m[3 * r] * v[0] + m[3 * r + 1] * v[1] + m[3 * r + 2] * v[2] for r in range(3)]


class Dims:
    def __init__(self, nx, ny, nz):
        self.nx, self.ny, self.nz = nx, ny, nz
        self.rows = nx * ny
        self.groups = self.rows // 8


def tile(ref, c, x, size):
    return ref[c, x * size : (x + 1) * size, :]


def tiles(ref, count, x, size):
    return [tile(ref, c, x, size) for c in range(count)]


def flat_tiles(ref, start, count, size):
    return [ref[(start + c) * size : (start + c + 1) * size, :] for c in range(count)]


def face_index(axis, count):
    even = jnp.where(is_even(axis), count - 1, 0)
    return even, (count - 1) - even


def inner_odd(axis, value):
    count = lax.axis_size(axis)
    at = lax.axis_index(axis)
    return jnp.where((at > 0) & (at < count - 1), value, 0.0)


def put_faces(dims, fields, sends):
    xe, xo, ye, yo = sends
    nx, ny = dims.nx, dims.ny
    x_e, x_o = face_index("gx", nx)
    y_e, y_o = face_index("gy", ny)
    at = 0
    for field in fields:
        for c in range(field.shape[0]):
            x_rows = slice(at * ny, (at + 1) * ny)
            y_rows = slice(at * nx, (at + 1) * nx)
            xe[x_rows, :] = field[c, pl.ds(pl.multiple_of(x_e * ny, ny), ny), :]
            v = field[c, pl.ds(pl.multiple_of(x_o * ny, ny), ny), :]
            xo[x_rows, :] = inner_odd("gx", v)
            ye[y_rows, :] = field[c, pl.ds(y_e, nx, stride=ny), :]
            yo[y_rows, :] = inner_odd("gy", field[c, pl.ds(y_o, nx, stride=ny), :])
            at += 1


def put_z(dims, field, sends):
    groups, nz = dims.groups, dims.nz
    lane = lane_iota(8, nz)
    for odd, (ref, k) in enumerate(zip(sends, face_index("gz", nz))):
        to = lax.rem(lane + nz - k, nz)
        total = []
        for c in range(3):
            face = jnp.zeros((8, nz), jnp.float32)
            for g in range(groups):
                at = c * groups + g
                face = jnp.where(to == at, pltpu.roll(field[c, 8 * g : 8 * g + 8, :], at, 1), face)
            total.append(face)
        face = pltpu.roll(total[0] + total[1] + total[2], lax.rem(nz - k, nz), 1)
        ref[0:8, :] = inner_odd("gz", face) if odd else face


def neighbour(axis, pair, high):
    e, o = pair
    even = is_even(axis)
    return jnp.where(even, e, o) if high else jnp.where(even, o, e)


class ZHalo:
    def __init__(self, dims, recv):
        self.dims = dims
        self.recv = [r[0:8, :] for r in recv]
        if len(recv) == 2:
            self.low = neighbour("gz", self.recv, False)
            self.high = neighbour("gz", self.recv, True)
        else:
            self.low = self.high = None
            self.at = jnp.where(is_even("gz"), 0, dims.nz - 1)
            self.moved = pltpu.roll(self.recv[0], self.at, 1)

    def tile(self, c, x):
        dims = self.dims
        nz = dims.nz
        lane = lane_iota(8, nz)
        per = dims.ny // 8
        out = []
        for g in range(x * per, (x + 1) * per):
            at = c * dims.groups + g
            if self.low is None:
                v = pltpu.roll(self.moved, (nz - at) % nz, 1)
                out.append(jnp.where(lane == self.at, v, 0.0))
            else:
                low = pltpu.roll(self.low, (nz - 1 - at) % nz, 1)
                high = pltpu.roll(self.high, (nz - at) % nz, 1)
                out.append(jnp.where(lane == nz - 1, low, high))
        return jnp.concatenate(out, axis=0) if per > 1 else out[0]


def shifted(v, low, high, axis):
    size = v.shape[axis]
    at = lax.broadcasted_iota(jnp.int32, v.shape, axis)
    below = pltpu.roll(jnp.where(at == size - 1, low, v), 1, axis)
    above = pltpu.roll(jnp.where(at == 0, high, v), size - 1, axis)
    return below, above


def beside(coup, x_pair, y_pair, z_pair):
    return (
        coup[0] * x_pair[0]
        + coup[1] * x_pair[1]
        + (coup[2] * y_pair[0] + coup[3] * y_pair[1])
        + (coup[4] * z_pair[0] + coup[5] * z_pair[1])
    )


def sums_at(dims, x, field, x_halo, y_halo, z_halo, coup):
    nx, ny = dims.nx, dims.ny
    center = tiles(field, 3, x, ny)
    out = []
    for c in range(3):
        low = tile(field, c, x - 1, ny) if x > 0 else x_halo(c, False)
        high = tile(field, c, x + 1, ny) if x < nx - 1 else x_halo(c, True)
        y_pair = shifted(center[c], y_halo(c, x, False), y_halo(c, x, True), 0)
        z = z_halo.tile(c, x)
        z_pair = shifted(center[c], z, z, 1)
        out.append(beside(coup, (low, high), y_pair, z_pair))
    return center, out


def received(dims, recv):
    xe, xo, ye, yo = recv
    nx, ny = dims.nx, dims.ny

    def x_halo(c, high):
        pair = [r[c * ny : (c + 1) * ny, :] for r in (xe, xo)]
        return neighbour("gx", pair, high)

    def y_halo(c, x, high):
        pair = [r[c * nx + x : c * nx + x + 1, :] for r in (ye, yo)]
        return neighbour("gy", pair, high)

    return x_halo, y_halo


def rows_at(dims, x):
    return slice(x * dims.ny, (x + 1) * dims.ny)


def put_inverses(ref, start, pieces):
    for piece in pieces:
        ref[start : start + 36, :] = piece
        start += 36


CHUNKS = 4


def first_kernel(dims, n_z, *refs):
    rhs_in, blocks_in, couplings_in, coarse_inv_in, ids_in = refs[:5]
    first, inverse, rhs, couplings, own, ids, xe, xo, ye, yo = refs[5:15]
    z_sends, (blocks, coarse_inv, square, sems) = refs[15 : 15 + n_z], refs[15 + n_z :]
    step = dims.rows // CHUNKS

    def copy(k, src, dst, rows):
        return pltpu.make_async_copy(src.at[:, rows, :], dst.at[:, rows, :], sems.at[k])

    copies = []
    for k in range(CHUNKS):
        rows = pl.ds(k * step, step)
        copies.append(copy(2 * k, blocks_in, blocks, rows))
        copies.append(copy(2 * k + 1, rhs_in, rhs, rows))
    copies.append(copy(2 * CHUNKS, couplings_in, couplings, pl.ds(0, dims.rows)))
    copies.append(pltpu.make_async_copy(coarse_inv_in, coarse_inv, sems.at[2 * CHUNKS + 1]))
    copies.append(pltpu.make_async_copy(ids_in, square, sems.at[2 * CHUNKS + 2]))
    for c in copies:
        c.start()
    for x in range(dims.nx):
        if x % (dims.nx // CHUNKS) == 0:
            k = x // (dims.nx // CHUNKS)
            copies[2 * k].wait()
            copies[2 * k + 1].wait()
        inv = damped_inverse(tiles(blocks, 9, x, dims.ny))
        at = rows_at(dims, x)
        for k in range(9):
            inverse[k, at, :] = inv[k]
        v = times(inv, tiles(rhs, 3, x, dims.ny))
        for c in range(3):
            first[c, at, :] = v[c]
    for c in copies[-3:]:
        c.wait()
    put_faces(dims, (first, inverse, couplings), (xe, xo, ye, yo))
    put_z(dims, first, z_sends)
    own[...] = coarse_inv[:, 0, :]
    put_inverses(ye, 18 * dims.nx, [own[...]])
    put_inverses(yo, 18 * dims.nx, [own[...]])
    put_inverses(z_sends[0], 8, [own[...]])
    ids[...] = pencil_row(dims, square[0].astype(jnp.float32))


def second_kernel(dims, n_z, inverse, couplings, first, *refs):
    recv, z_recv, refs = refs[:4], refs[4 : 4 + n_z], refs[4 + n_z :]
    second, sums, *sends = refs[:6]
    z_sends = refs[6:]
    x_halo, y_halo = received(dims, recv)
    z_halo = ZHalo(dims, z_recv)
    for x in range(dims.nx):
        coup = tiles(couplings, 6, x, dims.ny)
        center, total = sums_at(dims, x, first, x_halo, y_halo, z_halo, coup)
        step = times(tiles(inverse, 9, x, dims.ny), total)
        at = rows_at(dims, x)
        for c in range(3):
            sums[c, at, :] = total[c]
            second[c, at, :] = (2.0 - DAMPING) * center[c] + step[c]
    put_faces(dims, (second,), sends)
    put_z(dims, second, z_sends)
    even_block, odd_block = [r[18 * dims.nx : 18 * dims.nx + 36, :] for r in recv[2:]]
    put_inverses(sends[2], 3 * dims.nx, [odd_block])
    put_inverses(z_sends[0], 8, [even_block, odd_block])


def coarse_kernel(dims, n_z, rhs, sums, couplings, second, ids, *refs):
    recv, z_recv, (packet, resid) = refs[:4], refs[4 : 4 + n_z], refs[4 + n_z :]
    x_halo, y_halo = received(dims, recv)
    z_halo = ZHalo(dims, z_recv)
    rest = 1.0 - DAMPING * (2.0 - DAMPING)
    for x in range(dims.nx):
        coup = tiles(couplings, 6, x, dims.ny)
        _, total = sums_at(dims, x, second, x_halo, y_halo, z_halo, coup)
        at = rows_at(dims, x)
        for c in range(3):
            resid[c, at, :] = rest * rhs[c, at, :] + (total[c] - DAMPING * sums[c, at, :])
    m0, m1 = mode_rows(8, dims.nz)
    row = row_iota(8, dims.nz)
    modes = split3(jnp.where(row == 0, m0, jnp.where(row == 1, m1, 0.0)))
    for c in range(3):
        s = sum(dot_tt(modes, part) for part in parts3(resid[c]))
        packet[0, 2 * c : 2 * c + 2, :] = (s[0:8] + (s[8:16] + s[16:24]))[0:2]
    packet[0, 6:7, :] = ids[...]
    packet[0, 7:8, :] = jnp.zeros((1, dims.rows), jnp.float32)


def pencil_row(dims, square):
    nx, ny, rows = dims.nx, dims.ny, dims.rows
    lane = lane_iota(ny, rows)
    spread = jnp.where(lax.rem(lane, ny) == row_iota(ny, rows), 1.0, 0.0)
    wide = lax.dot_general(
        square,
        spread,
        (((1,), (0,)), ((), ())),
        precision=lax.Precision.HIGHEST,
        preferred_element_type=jnp.float32,
    )
    lane = lane_iota(nx, rows)
    keep = lax.div(lane, ny) == row_iota(nx, rows)
    return jnp.sum(jnp.where(keep, wide, 0.0), axis=0, keepdims=True)


def partner(index, count, odd):
    if odd:
        return ((index + 1) % count ^ 1) - 1 + (((index + 1) % count ^ 1) == 0) * count
    return index ^ 1


def follow(index, count, word):
    for odd in word:
        index = partner(index, count, odd)
    return index


def words_of(count):
    words, seen = [], set()
    for length in range(count):
        for start in (False, True):
            word = tuple(bool(start) ^ bool(k % 2) for k in range(length))
            to = follow(0, count, word)
            if to not in seen:
                seen.add(to)
                words.append(word)
    return words


def blocks_of(n_y, n_z):
    e, o, none = (False,), (True,), ()
    held = [(none, none), (e, none), (o, none), (none, e), (e, e), (o, e), (e + o, none)]
    found = {(follow(0, n_y, y), follow(0, n_z, z)) for y, z in held}
    rest = []
    for y in words_of(n_y):
        for z in words_of(n_z):
            at = (follow(0, n_y, y), follow(0, n_z, z))
            if at not in found:
                found.add(at)
                rest.append((y, z))
    return held, rest


def solve_kernel(dims, sizes, own, *refs):
    n_y, n_z = sizes
    owners = n_y * n_z
    rows = dims.rows
    my_y, my_z = lax.axis_index("gy"), lax.axis_index("gz")
    arrived, coarse_inv, refs = refs[:n_y], refs[n_y], refs[n_y + 1 :]
    held, rest = blocks_of(n_y, n_z)
    pieces, refs = refs[: 5 + len(rest)], refs[5 + len(rest) :]
    stack, y_z, coarse, correction, inverses, packets = refs
    put_inverses(inverses, 0, [coarse_inv[...]])
    at = 36
    fat_ye, fat_yo, fat_z, thin_ye, thin_z = pieces[:5]
    for ref, start, count in (
        (fat_ye, 18 * dims.nx, 36),
        (fat_yo, 18 * dims.nx, 36),
        (fat_z, 8, 36),
        (thin_z, 8, 72),
        (thin_ye, 3 * dims.nx, 36),
    ):
        inverses[at : at + count, :] = ref[start : start + count, :]
        at += count
    for piece in pieces[5:]:
        put_inverses(inverses, at, [piece[:, 0, :]])
        at += 36
    order = held + rest
    for y, ref in zip(words_of(n_y), arrived):
        for k, z in enumerate(words_of(n_z)):
            packets[follow(my_y, n_y, y) * n_z + follow(my_z, n_z, z)] = ref[k]
    local = row_iota(own, rows).astype(jnp.bfloat16)
    one_b = jnp.ones((own, rows), jnp.bfloat16)
    zero_b = jnp.zeros((own, rows), jnp.bfloat16)

    def owner_at(j):
        y, z = order[j]
        return follow(my_y, n_y, y) * n_z + follow(my_z, n_z, z)

    def member(j, ids):
        base = (owner_at(j) * own).astype(jnp.float32)
        rel = jnp.clip(ids - base, -1.0, float(own)).astype(jnp.bfloat16)
        return jnp.where(local == rel, one_b, zero_b)

    coarse[...] = jnp.zeros_like(coarse)

    def add(d, carry):
        pack = packets[d]
        ids = pack[6:7]
        parts = split3(jnp.where(row_iota(8, rows) < 6, pack, 0.0))
        for j in range(owners):
            s = dot_tt(parts, member(j, ids))
            coarse[8 * j : 8 * j + 8] = coarse[8 * j : 8 * j + 8] + (s[0:8] + (s[8:16] + s[16:24]))
        return carry

    lax.fori_loop(0, owners, add, 0, unroll=2)

    for block in range(owners // 8):
        v = [coarse[pl.ds(64 * block + k, 8, stride=8), :] for k in range(6)]
        for i in range(6):
            total = None
            for k in range(6):
                m = inverses[pl.ds(36 * 8 * block + 6 * i + k, 8, stride=36), :]
                total = m * v[k] if total is None else total + m * v[k]
            correction[pl.ds(64 * block + i, 8, stride=8), :] = total
        for i in (6, 7):
            correction[pl.ds(64 * block + i, 8, stride=8), :] = jnp.zeros_like(total)

    def ids_of(y, z):
        inside = (y >= 0) & (y < n_y) & (z >= 0) & (z < n_z)
        y = jnp.clip(y, 0, n_y - 1)
        z = jnp.clip(z, 0, n_z - 1)
        return jnp.where(inside, packets[y * n_z + z, 6:7, :], -1.0)

    upper = lax.rem(lane_iota(1, rows), dims.ny) >= dims.ny // 2

    def y_ids(z):
        return jnp.where(upper, ids_of(my_y - 1, z), ids_of(my_y + 1, z))

    beyond = [1 - my_z] if n_z == 2 else [my_z - 1, my_z + 1]
    wanted = [ids_of(my_y, my_z), y_ids(my_z)]
    wanted += [ids_of(my_y, z) for z in beyond] + [y_ids(z) for z in beyond]
    totals = [jnp.zeros((24, rows), jnp.float32) for _ in wanted]
    for j in range(owners):
        left = split3(correction[8 * j : 8 * j + 8])
        for t in range(len(wanted)):
            totals[t] = totals[t] + lax.dot_general(
                left,
                member(j, wanted[t]),
                (((1,), (0,)), ((), ())),
                preferred_element_type=jnp.float32,
            )
    totals = [s[0:8] + (s[8:16] + s[16:24]) for s in totals]
    stack[0:8] = totals[0]
    stack[8:16] = totals[1]
    if n_z == 2:
        low = my_z == 1
        for ref, at, value in ((stack, 16, totals[2]), (y_z, 0, totals[3])):
            ref[at : at + 8] = jnp.where(low, value, 0.0)
            ref[at + 8 : at + 16] = jnp.where(low, 0.0, value)
    else:
        stack[16:24], stack[24:32] = totals[2], totals[3]
        y_z[0:8], y_z[8:16] = totals[4], totals[5]


def third_kernel(dims, n_z, inverse, couplings, second, stack, y_z, *refs):
    stacks, fat, thin, refs = refs[:2], refs[2:6], refs[6:10], refs[10:]
    third, x_third, y_third = refs[:3]
    z_sends, refs = refs[3 : 3 + n_z], refs[3 + n_z :]
    field, y_field, z_field, yz_field, x_field, xy_field, xz_field = refs
    nx, ny, nz = dims.nx, dims.ny, dims.nz
    side = nx * ny // 2
    m0, m1 = mode_rows(8, nz)
    row = row_iota(8, nz)
    modes = jnp.concatenate(
        [
            jnp.where(row == 2 * c, m0, jnp.where(row == 2 * c + 1, m1, 0.0))
            for c in range(3)
        ],
        axis=1,
    )
    at = lax.rem(lane_iota(8, 3 * nz), nz)
    wide = pairs6_right(modes)
    last = pairs6_right(jnp.where(at == nz - 1, modes, 0.0))
    start = pairs6_right(jnp.where(at == 0, modes, 0.0))
    my_x, n_x = lax.axis_index("gx"), lax.axis_size("gx")
    x_low = neighbour("gx", [s[:, side:] for s in stacks], False)
    x_high = neighbour("gx", [s[:, :side] for s in stacks], True)
    x_low = jnp.where(my_x > 0, x_low, 0.0)
    x_high = jnp.where(my_x < n_x - 1, x_high, 0.0)
    x_mix = jnp.where(lane_iota(4 * 8, side) < side // 2, x_high, x_low)

    def expand(v, ends=None):
        if ends is None:
            return dot_00(pairs6(v), wide)
        return dot_00(pairs6(v), last) + dot_00(pairs6(ends), start)

    for ref, value in (
        (field, expand(stack[0:8])),
        (y_field, expand(stack[8:16])),
        (z_field, expand(stack[16:24], stack[24:32])),
        (yz_field, expand(y_z[0:8], y_z[8:16])),
        (x_field, expand(x_mix[0:8])),
        (xy_field, expand(x_mix[8:16])),
        (xz_field, expand(x_mix[16:24], x_mix[24:32])),
    ):
        for c in range(3):
            ref[c] = value[:, c * nz : (c + 1) * nz]

    def at_x(own, outer, c, x):
        if 0 <= x < nx:
            return tile(own, c, x, ny)
        return tile(outer, c, side // ny + x if x < 0 else x - nx, ny)

    def update(inv, coup, center, base, pairs):
        step = times(inv, [beside(coup, *pairs(c)) for c in range(3)])
        return [base[c] + ((1.0 - DAMPING) * center[c] + step[c]) for c in range(3)]

    for x in range(-1, nx + 1):
        center = [at_x(field, x_field, c, x) for c in range(3)]

        def pairs(c, x=x, center=center):
            y = at_x(y_field, xy_field, c, x)
            z = at_x(z_field, xz_field, c, x)
            x_pair = (at_x(field, x_field, c, x - 1), at_x(field, x_field, c, x + 1))
            return x_pair, shifted(center[c], y, y, 0), shifted(center[c], z, z, 1)

        if 0 <= x < nx:
            out = update(
                tiles(inverse, 9, x, ny),
                tiles(couplings, 6, x, ny),
                center,
                tiles(second, 3, x, ny),
                pairs,
            )
            for c in range(3):
                third[c, rows_at(dims, x), :] = out[c]
        else:
            high = x == nx
            halo = [
                neighbour("gx", [r[c * ny : (c + 1) * ny, :] for r in fat[:2]], high)
                for c in range(3, 18)
            ]
            base = [
                neighbour("gx", [r[c * ny : (c + 1) * ny, :] for r in thin[:2]], high)
                for c in range(3)
            ]
            out = update(halo[:9], halo[9:], center, base, pairs)
            for c in range(3):
                x_third[int(high), c * ny : (c + 1) * ny, :] = out[c]
    for high in (False, True):
        inner, near, far = (ny - 1, 0, 1) if high else (0, ny - 1, ny - 2)

        def line(ref, c, y):
            return ref[c, pl.ds(y, nx, stride=ny), :]

        center = [line(y_field, c, near) for c in range(3)]

        def pairs(c, center=center, inner=inner, near=near, far=far, high=high):
            low_row = xy_field[c, side - ny + near : side - ny + near + 1, :]
            high_row = xy_field[c, near : near + 1, :]
            y_pair = (line(y_field, c, far), line(field, c, inner))
            z = line(yz_field, c, near)
            return (
                shifted(center[c], low_row, high_row, 0),
                y_pair[::-1] if high else y_pair,
                shifted(center[c], z, z, 1),
            )

        halo = [
            neighbour("gy", [r[c * nx : (c + 1) * nx, :] for r in fat[2:]], high)
            for c in range(3, 18)
        ]
        base = [
            neighbour("gy", [r[c * nx : (c + 1) * nx, :] for r in thin[2:]], high)
            for c in range(3)
        ]
        out = update(halo[:9], halo[9:], center, base, pairs)
        for c in range(3):
            y_third[int(high), c * nx : (c + 1) * nx, :] = out[c]
    put_z(dims, third, z_sends)


def last_kernel(dims, inverse, couplings, first, third, x_third, y_third, *refs):
    z_recv, out = refs[:-1], refs[-1]
    nx, ny = dims.nx, dims.ny

    def x_halo(c, high):
        return x_third[int(high), c * ny : (c + 1) * ny, :]

    def y_halo(c, x, high):
        return y_third[int(high), c * nx + x : c * nx + x + 1, :]

    z_halo = ZHalo(dims, z_recv)
    for x in range(nx):
        coup = tiles(couplings, 6, x, ny)
        center, total = sums_at(dims, x, third, x_halo, y_halo, z_halo, coup)
        step = times(tiles(inverse, 9, x, ny), total)
        at = rows_at(dims, x)
        for c in range(3):
            out[c, at, :] = first[c, at, :] + ((1.0 - DAMPING) * center[c] + step[c])


def swap(value, axis, odd):
    count = lax.axis_size(axis)
    return lax.ppermute(value, axis, [(partner(i, count, odd), i) for i in range(count)])


def exchange(sends, z_sends):
    xe, xo, ye, yo = sends
    xe = swap(xe, "gx", 0)
    z_recv = [swap(v, "gz", k) for k, v in enumerate(z_sends)]
    ye, yo = swap(ye, "gy", 0), swap(yo, "gy", 1)
    xo = swap(xo, "gx", 1)
    return [xe, xo, ye, yo], z_recv


def fetch(value, word_y, word_z):
    n_y, n_z = lax.axis_size("gy"), lax.axis_size("gz")
    which = []
    for y in range(n_y):
        for z in range(n_z):
            source = follow(y, n_y, word_y) * n_z + follow(z, n_z, word_z)
            which.append((source, y * n_z + z))
    return lax.ppermute(value, ("gy", "gz"), which)


def call(body, name, out_shapes, scratch, *args, in_hbm=0):
    near = pl.BlockSpec(memory_space=pltpu.VMEM)
    far = pl.BlockSpec(memory_space=pltpu.HBM)
    return pl.pallas_call(
        body,
        name=name,
        out_shape=[jax.ShapeDtypeStruct(s, jnp.float32) for s in out_shapes],
        in_specs=[far] * in_hbm + [near] * (len(args) - in_hbm),
        out_specs=[near] * len(out_shapes),
        scratch_shapes=scratch,
        compiler_params=pltpu.CompilerParams(vmem_limit_bytes=VMEM_LIMIT),
    )(*args)


def shards(rhs, blocks, couplings, agg_ids, coarse_inv):
    _, nx, ny, nz = rhs.shape
    dims = Dims(nx, ny, nz)
    rows = nx * ny
    rhs = rhs.reshape(3, rows, nz)
    blocks = blocks.reshape(9, rows, nz)
    couplings = couplings.reshape(6, rows, nz)
    own = coarse_inv.shape[2]
    n_y, n_z = lax.axis_size("gy"), lax.axis_size("gz")
    owners = n_y * n_z
    z_count = 1 if n_z == 2 else 2
    vector = (3, rows, nz)
    part = functools.partial
    f32 = jnp.float32

    def faces(count, even, odd):
        return [(count * ny, nz)] * 2 + [(count * nx + even, nz), (count * nx + odd, nz)]

    def z_faces(extra):
        return [(8 + extra, nz)] + [(8, nz)] * (z_count - 1)

    _, rest = blocks_of(n_y, n_z)
    pieces = [fetch(coarse_inv, y, z) for y, z in rest]
    first, inverse, rhs, couplings, own_inv, ids, *sends = call(
        part(first_kernel, dims, z_count),
        "first",
        [vector, (9, rows, nz), vector, (6, rows, nz), (36, own), (1, rows)]
        + faces(18, 36, 36)
        + z_faces(36),
        [
            pltpu.VMEM((9, rows, nz), f32),
            pltpu.VMEM(coarse_inv.shape, f32),
            pltpu.VMEM(agg_ids.shape, jnp.int32),
            pltpu.SemaphoreType.DMA((2 * CHUNKS + 3,)),
        ],
        *[
            pltpu.with_memory_space_constraint(v, pltpu.HBM)
            for v in (rhs, blocks, couplings, coarse_inv, agg_ids)
        ],
        in_hbm=5,
    )
    fat, fat_z = exchange(sends[:4], sends[4:])
    second, sums, *sends = call(
        part(second_kernel, dims, z_count),
        "second",
        [vector, vector] + faces(3, 36, 0) + z_faces(72),
        [],
        inverse,
        couplings,
        first,
        *fat,
        *fat_z,
    )
    thin, thin_z = exchange(sends[:4], sends[4:])
    (packet,) = call(
        part(coarse_kernel, dims, z_count),
        "coarse",
        [(1, 8, rows)],
        [pltpu.VMEM(vector, f32)],
        rhs,
        sums,
        couplings,
        second,
        ids,
        *thin,
        *thin_z,
    )
    z_words, y_words = words_of(n_z), words_of(n_y)
    packet = jnp.concatenate([fetch(packet, (), z) if z else packet for z in z_words], axis=0)
    packets = [fetch(packet, y, ()) if y else packet for y in y_words]
    stack, y_z = call(
        part(solve_kernel, dims, (n_y, n_z), own),
        "solve",
        [(4 * 8, rows), (2 * 8, rows)],
        [pltpu.VMEM((owners * 8, own), f32)] * 2 + [pltpu.VMEM((owners * 36, own), f32)]
        + [pltpu.VMEM((owners, 8, rows), f32)],
        *packets,
        own_inv,
        fat[2],
        fat[3],
        fat_z[0],
        thin[2],
        thin_z[0],
        *pieces,
    )
    xe, xo = swap(stack, "gx", 0), swap(stack, "gx", 1)
    third, x_third, y_third, *z_sends = call(
        part(third_kernel, dims, z_count),
        "third",
        [vector, (2, 3 * ny, nz), (2, 3 * nx, nz)] + z_faces(0),
        [pltpu.VMEM(vector, f32)] * 4 + [pltpu.VMEM((3, rows // 2, nz), f32)] * 3,
        inverse,
        couplings,
        second,
        stack,
        y_z,
        xe,
        xo,
        *fat,
        *thin,
    )
    z_recv = [swap(v, "gz", k) for k, v in enumerate(z_sends)]
    (out,) = call(
        part(last_kernel, dims),
        "last",
        [vector],
        [],
        inverse,
        couplings,
        first,
        third,
        x_third,
        y_third,
        *z_recv,
    )
    return out.reshape(3, nx, ny, nz)


def solution(mesh):
    return jax.shard_map(
        shards,
        mesh=mesh,
        in_specs=(
            P(None, "gx", "gy", "gz"),
            P(None, "gx", "gy", "gz"),
            P(None, "gx", "gy", "gz"),
            P("gz", "gx", "gy"),
            P(None, "gx", ("gy", "gz")),
        ),
        out_specs=P(None, "gx", "gy", "gz"),
        check_vma=False,
    )
```

```python
import functools

import jax
import jax.numpy as jnp
from jax import lax
from jax.experimental import pallas as pl
from jax.experimental.pallas import tpu as pltpu
from jax.sharding import PartitionSpec as P

DAMPING = 0.8
AXES = ("gx", "gy", "gz")
VMEM_LIMIT = 12 * 1024 * 1024


def dot_tt(a, b):
    return lax.dot_general(
        a, b, (((1,), (1,)), ((), ())), preferred_element_type=jnp.float32
    )


def dot_00(a, b):
    return lax.dot_general(
        a, b, (((0,), (0,)), ((), ())), preferred_element_type=jnp.float32
    )


def parts3(v):
    high = v.astype(jnp.bfloat16)
    rest = v - high.astype(jnp.float32)
    mid = rest.astype(jnp.bfloat16)
    low = (rest - mid.astype(jnp.float32)).astype(jnp.bfloat16)
    return high, mid, low


def split3(v):
    return jnp.concatenate(parts3(v), axis=0)


def pairs6(v):
    high, mid, low = parts3(v)
    return jnp.concatenate([high, high, high, mid, mid, low], axis=0)


def pairs6_right(v):
    high, mid, low = parts3(v)
    return jnp.concatenate([high, mid, low, high, mid, high], axis=0)


def lane_iota(rows, lanes):
    return lax.broadcasted_iota(jnp.int32, (rows, lanes), 1)


def row_iota(rows, lanes):
    return lax.broadcasted_iota(jnp.int32, (rows, lanes), 0)


def mode_rows(rows, length):
    k = lane_iota(rows, length).astype(jnp.float32)
    m1 = (k - (length - 1) / 2.0) / (length / 2.0) * (3.0 / length) ** 0.5
    m0 = jnp.full((rows, length), length ** (-0.5), jnp.float32)
    return m0, m1


def is_even(axis):
    return lax.rem(lax.axis_index(axis), 2) == 0


def damped_inverse(m):
    a, b, c, d, e, f, g, h, i = m
    co_a = e * i - f * h
    co_b = f * g - d * i
    co_c = d * h - e * g
    determ = a * co_a + b * co_b + c * co_c
    scale = DAMPING / determ
    rows = [
        co_a,
        c * h - b * i,
        b * f - c * e,
        co_b,
        a * i - c * g,
        c * d - a * f,
        co_c,
        b * g - a * h,
        a * e - b * d,
    ]
    return [r * scale for r in rows]


def times(m, v):
    return [m[3 * r] * v[0] + m[3 * r + 1] * v[1] + m[3 * r + 2] * v[2] for r in range(3)]


class Dims:
    def __init__(self, nx, ny, nz):
        self.nx, self.ny, self.nz = nx, ny, nz
        self.rows = nx * ny
        self.groups = self.rows // 8


def tile(ref, c, x, size):
    return ref[c, x * size : (x + 1) * size, :]


def tiles(ref, count, x, size):
    return [tile(ref, c, x, size) for c in range(count)]


def flat_tiles(ref, start, count, size):
    return [ref[(start + c) * size : (start + c + 1) * size, :] for c in range(count)]


def face_index(axis, count):
    even = jnp.where(is_even(axis), count - 1, 0)
    return even, (count - 1) - even


def inner_odd(axis, value):
    count = lax.axis_size(axis)
    at = lax.axis_index(axis)
    return jnp.where((at > 0) & (at < count - 1), value, 0.0)


def put_faces(dims, fields, sends):
    xe, xo, ye, yo = sends
    nx, ny = dims.nx, dims.ny
    x_e, x_o = face_index("gx", nx)
    y_e, y_o = face_index("gy", ny)
    at = 0
    for field in fields:
        for c in range(field.shape[0]):
            x_rows = slice(at * ny, (at + 1) * ny)
            y_rows = slice(at * nx, (at + 1) * nx)
            xe[x_rows, :] = field[c, pl.ds(pl.multiple_of(x_e * ny, ny), ny), :]
            v = field[c, pl.ds(pl.multiple_of(x_o * ny, ny), ny), :]
            xo[x_rows, :] = inner_odd("gx", v)
            ye[y_rows, :] = field[c, pl.ds(y_e, nx, stride=ny), :]
            yo[y_rows, :] = inner_odd("gy", field[c, pl.ds(y_o, nx, stride=ny), :])
            at += 1


def put_z(dims, field, sends):
    groups, nz = dims.groups, dims.nz
    lane = lane_iota(8, nz)
    for odd, (ref, k) in enumerate(zip(sends, face_index("gz", nz))):
        to = lax.rem(lane + nz - k, nz)
        total = []
        for c in range(3):
            face = jnp.zeros((8, nz), jnp.float32)
            for g in range(groups):
                at = c * groups + g
                face = jnp.where(to == at, pltpu.roll(field[c, 8 * g : 8 * g + 8, :], at, 1), face)
            total.append(face)
        face = pltpu.roll(total[0] + total[1] + total[2], lax.rem(nz - k, nz), 1)
        ref[0:8, :] = inner_odd("gz", face) if odd else face


def neighbour(axis, pair, high):
    e, o = pair
    even = is_even(axis)
    return jnp.where(even, e, o) if high else jnp.where(even, o, e)


def place_z(dims, recv, out):
    nz = dims.nz
    lane = lane_iota(8, nz)
    recv = [r[0:8, :] for r in recv]
    if len(recv) == 2:
        low, high = neighbour("gz", recv, False), neighbour("gz", recv, True)
    else:
        at = jnp.where(is_even("gz"), 0, nz - 1)
        moved = pltpu.roll(recv[0], at, 1)
    for c in range(3):
        for g in range(dims.groups):
            k = c * dims.groups + g
            if len(recv) == 2:
                v = jnp.where(
                    lane == nz - 1,
                    pltpu.roll(low, (nz - 1 - k) % nz, 1),
                    pltpu.roll(high, (nz - k) % nz, 1),
                )
            else:
                v = jnp.where(lane == at, pltpu.roll(moved, (nz - k) % nz, 1), 0.0)
            out[c, 8 * g : 8 * g + 8, :] = v


def shifted(v, low, high, axis):
    size = v.shape[axis]
    at = lax.broadcasted_iota(jnp.int32, v.shape, axis)
    below = pltpu.roll(jnp.where(at == size - 1, low, v), 1, axis)
    above = pltpu.roll(jnp.where(at == 0, high, v), size - 1, axis)
    return below, above


def beside(coup, x_pair, y_pair, z_pair):
    return (
        coup[0] * x_pair[0]
        + coup[1] * x_pair[1]
        + (coup[2] * y_pair[0] + coup[3] * y_pair[1])
        + (coup[4] * z_pair[0] + coup[5] * z_pair[1])
    )


def sums_at(dims, x, field, x_halo, y_halo, z_halo, coup):
    nx, ny = dims.nx, dims.ny
    center = tiles(field, 3, x, ny)
    out = []
    for c in range(3):
        low = tile(field, c, x - 1, ny) if x > 0 else x_halo(c, False)
        high = tile(field, c, x + 1, ny) if x < nx - 1 else x_halo(c, True)
        y_pair = shifted(center[c], y_halo(c, x, False), y_halo(c, x, True), 0)
        z = tile(z_halo, c, x, ny)
        z_pair = shifted(center[c], z, z, 1)
        out.append(beside(coup, (low, high), y_pair, z_pair))
    return center, out


def received(dims, recv):
    xe, xo, ye, yo = recv
    nx, ny = dims.nx, dims.ny

    def x_halo(c, high):
        pair = [r[c * ny : (c + 1) * ny, :] for r in (xe, xo)]
        return neighbour("gx", pair, high)

    def y_halo(c, x, high):
        pair = [r[c * nx + x : c * nx + x + 1, :] for r in (ye, yo)]
        return neighbour("gy", pair, high)

    return x_halo, y_halo


def rows_at(dims, x):
    return slice(x * dims.ny, (x + 1) * dims.ny)


def put_inverses(ref, start, pieces):
    for piece in pieces:
        ref[start : start + 36, :] = piece
        start += 36


CHUNKS = 4


def first_kernel(dims, n_z, *refs):
    rhs_in, blocks_in, couplings_in, coarse_inv_in, ids_in = refs[:5]
    first, inverse, rhs, couplings, own, ids, xe, xo, ye, yo = refs[5:15]
    z_sends, (blocks, coarse_inv, square, sems) = refs[15 : 15 + n_z], refs[15 + n_z :]
    step = dims.rows // CHUNKS

    def copy(k, src, dst, rows):
        return pltpu.make_async_copy(src.at[:, rows, :], dst.at[:, rows, :], sems.at[k])

    copies = []
    for k in range(CHUNKS):
        rows = pl.ds(k * step, step)
        copies.append(copy(2 * k, blocks_in, blocks, rows))
        copies.append(copy(2 * k + 1, rhs_in, rhs, rows))
    copies.append(copy(2 * CHUNKS, couplings_in, couplings, pl.ds(0, dims.rows)))
    copies.append(pltpu.make_async_copy(coarse_inv_in, coarse_inv, sems.at[2 * CHUNKS + 1]))
    copies.append(pltpu.make_async_copy(ids_in, square, sems.at[2 * CHUNKS + 2]))
    for c in copies:
        c.start()
    for x in range(dims.nx):
        if x % (dims.nx // CHUNKS) == 0:
            k = x // (dims.nx // CHUNKS)
            copies[2 * k].wait()
            copies[2 * k + 1].wait()
        inv = damped_inverse(tiles(blocks, 9, x, dims.ny))
        at = rows_at(dims, x)
        for k in range(9):
            inverse[k, at, :] = inv[k]
        v = times(inv, tiles(rhs, 3, x, dims.ny))
        for c in range(3):
            first[c, at, :] = v[c]
    for c in copies[-3:]:
        c.wait()
    put_faces(dims, (first, inverse, couplings), (xe, xo, ye, yo))
    put_z(dims, first, z_sends)
    own[...] = coarse_inv[:, 0, :]
    put_inverses(ye, 18 * dims.nx, [own[...]])
    put_inverses(yo, 18 * dims.nx, [own[...]])
    put_inverses(z_sends[0], 8, [own[...]])
    ids[...] = pencil_row(dims, square[0].astype(jnp.float32))


def second_kernel(dims, n_z, inverse, couplings, first, *refs):
    recv, z_recv, refs = refs[:4], refs[4 : 4 + n_z], refs[4 + n_z :]
    second, sums, *sends = refs[:6]
    z_sends, z_halo = refs[6:-1], refs[-1]
    x_halo, y_halo = received(dims, recv)
    place_z(dims, z_recv, z_halo)
    for x in range(dims.nx):
        coup = tiles(couplings, 6, x, dims.ny)
        center, total = sums_at(dims, x, first, x_halo, y_halo, z_halo, coup)
        step = times(tiles(inverse, 9, x, dims.ny), total)
        at = rows_at(dims, x)
        for c in range(3):
            sums[c, at, :] = total[c]
            second[c, at, :] = (2.0 - DAMPING) * center[c] + step[c]
    put_faces(dims, (second,), sends)
    put_z(dims, second, z_sends)
    even_block, odd_block = [r[18 * dims.nx : 18 * dims.nx + 36, :] for r in recv[2:]]
    put_inverses(sends[2], 3 * dims.nx, [odd_block])
    put_inverses(z_sends[0], 8, [even_block, odd_block])


def coarse_kernel(dims, n_z, rhs, sums, couplings, second, ids, *refs):
    half = dims.rows // 2
    recv, z_recv, refs = refs[:4], refs[4 : 4 + n_z], refs[4 + n_z :]
    packet, resid, z_halo = refs
    x_halo, y_halo = received(dims, recv)
    place_z(dims, z_recv, z_halo)
    rest = 1.0 - DAMPING * (2.0 - DAMPING)
    for x in range(dims.nx):
        coup = tiles(couplings, 6, x, dims.ny)
        _, total = sums_at(dims, x, second, x_halo, y_halo, z_halo, coup)
        at = rows_at(dims, x)
        for c in range(3):
            resid[c, at, :] = rest * rhs[c, at, :] + (total[c] - DAMPING * sums[c, at, :])
    m0, m1 = mode_rows(8, dims.nz)
    row = row_iota(8, dims.nz)
    modes = split3(jnp.where(row == 0, m0, jnp.where(row == 1, m1, 0.0)))
    for c in range(3):
        s = sum(dot_tt(modes, part) for part in parts3(resid[c]))
        s = (s[0:8] + (s[8:16] + s[16:24]))[0:2]
        packet[2 * c : 2 * c + 2, :] = s[:, :half]
        packet[8 + 2 * c : 10 + 2 * c, :] = s[:, half:]
    for k in range(2):
        packet[8 * k + 6 : 8 * k + 7, :] = ids[:, k * half : (k + 1) * half]
        packet[8 * k + 7 : 8 * k + 8, :] = jnp.zeros((1, half), jnp.float32)
    put_inverses(packet, 16, [recv[2][3 * dims.nx : 3 * dims.nx + 36, :]])


def pencil_row(dims, square):
    nx, ny, rows = dims.nx, dims.ny, dims.rows
    lane = lane_iota(ny, rows)
    spread = jnp.where(lax.rem(lane, ny) == row_iota(ny, rows), 1.0, 0.0)
    wide = lax.dot_general(
        square,
        spread,
        (((1,), (0,)), ((), ())),
        precision=lax.Precision.HIGHEST,
        preferred_element_type=jnp.float32,
    )
    lane = lane_iota(nx, rows)
    keep = lax.div(lane, ny) == row_iota(nx, rows)
    return jnp.sum(jnp.where(keep, wide, 0.0), axis=0, keepdims=True)


def partner(index, count, odd):
    if odd:
        return ((index + 1) % count ^ 1) - 1 + (((index + 1) % count ^ 1) == 0) * count
    return index ^ 1


def follow(index, count, word):
    for odd in word:
        index = partner(index, count, odd)
    return index


def words_of(count):
    words, seen = [], set()
    for length in range(count):
        for start in (False, True):
            word = tuple(bool(start) ^ bool(k % 2) for k in range(length))
            to = follow(0, count, word)
            if to not in seen:
                seen.add(to)
                words.append(word)
    return words


def blocks_of(n_y, n_z):
    e, o, none = (False,), (True,), ()
    held = [(none, none), (e, none), (o, none), (none, e), (e, e), (o, e), (e + o, none), (e + o, e)]
    found = {(follow(0, n_y, y), follow(0, n_z, z)) for y, z in held}
    rest = []
    for y in words_of(n_y):
        for z in words_of(n_z):
            at = (follow(0, n_y, y), follow(0, n_z, z))
            if at not in found:
                found.add(at)
                rest.append((y, z))
    return held, rest


def solve_kernel(dims, sizes, own, *refs):
    n_y, n_z = sizes
    owners = n_y * n_z
    rows = dims.rows
    my_y, my_z = lax.axis_index("gy"), lax.axis_index("gz")
    arrived, coarse_inv, refs = refs[:n_y], refs[n_y], refs[n_y + 1 :]
    held, rest = blocks_of(n_y, n_z)
    pieces, refs = refs[: 6 + len(rest)], refs[6 + len(rest) :]
    stack, y_z, coarse, correction, inverses, packets = refs
    put_inverses(inverses, 0, [coarse_inv[...]])
    at = 36
    fat_ye, fat_yo, fat_z, thin_ye, thin_z, first_z = pieces[:6]
    for ref, start, count in (
        (fat_ye, 18 * dims.nx, 36),
        (fat_yo, 18 * dims.nx, 36),
        (fat_z, 8, 36),
        (thin_z, 8, 72),
        (thin_ye, 3 * dims.nx, 36),
        (first_z, 16, 36),
    ):
        inverses[at : at + count, :] = ref[start : start + count, :]
        at += count
    for piece in pieces[6:]:
        put_inverses(inverses, at, [piece[:, 0, :]])
        at += 36
    order = held + rest
    for y, ref in zip(words_of(n_y), arrived):
        for k, z in enumerate(words_of(n_z)):
            at = follow(my_y, n_y, y) * n_z + follow(my_z, n_z, z)
            for side in range(2):
                v = ref[16 * k + 8 * side : 16 * k + 8 * side + 8, :]
                packets[at, :, side * rows // 2 : (side + 1) * rows // 2] = v
    local = row_iota(own, rows).astype(jnp.bfloat16)
    one_b = jnp.ones((own, rows), jnp.bfloat16)
    zero_b = jnp.zeros((own, rows), jnp.bfloat16)

    def owner_at(j):
        y, z = order[j]
        return follow(my_y, n_y, y) * n_z + follow(my_z, n_z, z)

    def member(j, ids):
        base = (owner_at(j) * own).astype(jnp.float32)
        rel = jnp.clip(ids - base, -1.0, float(own)).astype(jnp.bfloat16)
        return jnp.where(local == rel, one_b, zero_b)

    coarse[...] = jnp.zeros_like(coarse)

    def add(d, carry):
        pack = packets[d]
        ids = pack[6:7]
        parts = split3(jnp.where(row_iota(8, rows) < 6, pack, 0.0))
        for j in range(owners):
            s = dot_tt(parts, member(j, ids))
            coarse[8 * j : 8 * j + 8] = coarse[8 * j : 8 * j + 8] + (s[0:8] + (s[8:16] + s[16:24]))
        return carry

    lax.fori_loop(0, owners, add, 0, unroll=2)

    for block in range(owners // 8):
        v = [coarse[pl.ds(64 * block + k, 8, stride=8), :] for k in range(6)]
        for i in range(6):
            total = None
            for k in range(6):
                m = inverses[pl.ds(36 * 8 * block + 6 * i + k, 8, stride=36), :]
                total = m * v[k] if total is None else total + m * v[k]
            correction[pl.ds(64 * block + i, 8, stride=8), :] = total
        for i in (6, 7):
            correction[pl.ds(64 * block + i, 8, stride=8), :] = jnp.zeros_like(total)

    def ids_of(y, z):
        inside = (y >= 0) & (y < n_y) & (z >= 0) & (z < n_z)
        y = jnp.clip(y, 0, n_y - 1)
        z = jnp.clip(z, 0, n_z - 1)
        return jnp.where(inside, packets[y * n_z + z, 6:7, :], -1.0)

    upper = lax.rem(lane_iota(1, rows), dims.ny) >= dims.ny // 2

    def y_ids(z):
        return jnp.where(upper, ids_of(my_y - 1, z), ids_of(my_y + 1, z))

    beyond = [1 - my_z] if n_z == 2 else [my_z - 1, my_z + 1]
    wanted = [ids_of(my_y, my_z), y_ids(my_z)]
    wanted += [ids_of(my_y, z) for z in beyond] + [y_ids(z) for z in beyond]
    totals = [jnp.zeros((24, rows), jnp.float32) for _ in wanted]
    for j in range(owners):
        left = split3(correction[8 * j : 8 * j + 8])
        for t in range(len(wanted)):
            totals[t] = totals[t] + lax.dot_general(
                left,
                member(j, wanted[t]),
                (((1,), (0,)), ((), ())),
                preferred_element_type=jnp.float32,
            )
    totals = [s[0:8] + (s[8:16] + s[16:24]) for s in totals]
    stack[0:8] = totals[0]
    stack[8:16] = totals[1]
    if n_z == 2:
        low = my_z == 1
        for ref, at, value in ((stack, 16, totals[2]), (y_z, 0, totals[3])):
            ref[at : at + 8] = jnp.where(low, value, 0.0)
            ref[at + 8 : at + 16] = jnp.where(low, 0.0, value)
    else:
        stack[16:24], stack[24:32] = totals[2], totals[3]
        y_z[0:8], y_z[8:16] = totals[4], totals[5]


def third_kernel(dims, n_z, inverse, couplings, second, stack, y_z, *refs):
    stacks, fat, thin, refs = refs[:2], refs[2:6], refs[6:10], refs[10:]
    third, x_third, y_third = refs[:3]
    z_sends, refs = refs[3 : 3 + n_z], refs[3 + n_z :]
    field, y_field, z_field, yz_field, x_field, xy_field, xz_field = refs
    nx, ny, nz = dims.nx, dims.ny, dims.nz
    side = nx * ny // 2
    m0, m1 = mode_rows(8, nz)
    row = row_iota(8, nz)
    modes = jnp.concatenate(
        [
            jnp.where(row == 2 * c, m0, jnp.where(row == 2 * c + 1, m1, 0.0))
            for c in range(3)
        ],
        axis=1,
    )
    at = lax.rem(lane_iota(8, 3 * nz), nz)
    wide = pairs6_right(modes)
    last = pairs6_right(jnp.where(at == nz - 1, modes, 0.0))
    start = pairs6_right(jnp.where(at == 0, modes, 0.0))
    my_x, n_x = lax.axis_index("gx"), lax.axis_size("gx")
    x_low = neighbour("gx", [s[:, side:] for s in stacks], False)
    x_high = neighbour("gx", [s[:, :side] for s in stacks], True)
    x_low = jnp.where(my_x > 0, x_low, 0.0)
    x_high = jnp.where(my_x < n_x - 1, x_high, 0.0)
    x_mix = jnp.where(lane_iota(4 * 8, side) < side // 2, x_high, x_low)

    def expand(v, ends=None):
        if ends is None:
            return dot_00(pairs6(v), wide)
        return dot_00(pairs6(v), last) + dot_00(pairs6(ends), start)

    for ref, value in (
        (field, expand(stack[0:8])),
        (y_field, expand(stack[8:16])),
        (z_field, expand(stack[16:24], stack[24:32])),
        (yz_field, expand(y_z[0:8], y_z[8:16])),
        (x_field, expand(x_mix[0:8])),
        (xy_field, expand(x_mix[8:16])),
        (xz_field, expand(x_mix[16:24], x_mix[24:32])),
    ):
        for c in range(3):
            ref[c] = value[:, c * nz : (c + 1) * nz]

    def at_x(own, outer, c, x):
        if 0 <= x < nx:
            return tile(own, c, x, ny)
        return tile(outer, c, side // ny + x if x < 0 else x - nx, ny)

    def update(inv, coup, center, base, pairs):
        step = times(inv, [beside(coup, *pairs(c)) for c in range(3)])
        return [base[c] + ((1.0 - DAMPING) * center[c] + step[c]) for c in range(3)]

    for x in range(-1, nx + 1):
        center = [at_x(field, x_field, c, x) for c in range(3)]

        def pairs(c, x=x, center=center):
            y = at_x(y_field, xy_field, c, x)
            z = at_x(z_field, xz_field, c, x)
            x_pair = (at_x(field, x_field, c, x - 1), at_x(field, x_field, c, x + 1))
            return x_pair, shifted(center[c], y, y, 0), shifted(center[c], z, z, 1)

        if 0 <= x < nx:
            out = update(
                tiles(inverse, 9, x, ny),
                tiles(couplings, 6, x, ny),
                center,
                tiles(second, 3, x, ny),
                pairs,
            )
            for c in range(3):
                third[c, rows_at(dims, x), :] = out[c]
        else:
            high = x == nx
            halo = [
                neighbour("gx", [r[c * ny : (c + 1) * ny, :] for r in fat[:2]], high)
                for c in range(3, 18)
            ]
            base = [
                neighbour("gx", [r[c * ny : (c + 1) * ny, :] for r in thin[:2]], high)
                for c in range(3)
            ]
            out = update(halo[:9], halo[9:], center, base, pairs)
            for c in range(3):
                x_third[int(high), c * ny : (c + 1) * ny, :] = out[c]
    for high in (False, True):
        inner, near, far = (ny - 1, 0, 1) if high else (0, ny - 1, ny - 2)

        def line(ref, c, y):
            return ref[c, pl.ds(y, nx, stride=ny), :]

        center = [line(y_field, c, near) for c in range(3)]

        def pairs(c, center=center, inner=inner, near=near, far=far, high=high):
            low_row = xy_field[c, side - ny + near : side - ny + near + 1, :]
            high_row = xy_field[c, near : near + 1, :]
            y_pair = (line(y_field, c, far), line(field, c, inner))
            z = line(yz_field, c, near)
            return (
                shifted(center[c], low_row, high_row, 0),
                y_pair[::-1] if high else y_pair,
                shifted(center[c], z, z, 1),
            )

        halo = [
            neighbour("gy", [r[c * nx : (c + 1) * nx, :] for r in fat[2:]], high)
            for c in range(3, 18)
        ]
        base = [
            neighbour("gy", [r[c * nx : (c + 1) * nx, :] for r in thin[2:]], high)
            for c in range(3)
        ]
        out = update(halo[:9], halo[9:], center, base, pairs)
        for c in range(3):
            y_third[int(high), c * nx : (c + 1) * nx, :] = out[c]
    put_z(dims, third, z_sends)


def last_kernel(dims, inverse, couplings, first, third, x_third, y_third, *refs):
    z_recv, (out, z_halo, result, sems) = refs[:-4], refs[-4:]
    copies = []
    step = dims.nx // CHUNKS
    nx, ny = dims.nx, dims.ny

    def x_halo(c, high):
        return x_third[int(high), c * ny : (c + 1) * ny, :]

    def y_halo(c, x, high):
        return y_third[int(high), c * nx + x : c * nx + x + 1, :]

    place_z(dims, z_recv, z_halo)
    for x in range(nx):
        coup = tiles(couplings, 6, x, ny)
        center, total = sums_at(dims, x, third, x_halo, y_halo, z_halo, coup)
        change = times(tiles(inverse, 9, x, ny), total)
        at = rows_at(dims, x)
        for c in range(3):
            result[c, at, :] = first[c, at, :] + ((1.0 - DAMPING) * center[c] + change[c])
        if (x + 1) % step == 0:
            at = pl.ds((x + 1 - step) * ny, step * ny)
            copy = (result.at[:, at, :], out.at[:, at, :], sems.at[x // step])
            copies.append(pltpu.make_async_copy(*copy))
            copies[-1].start()
    for copy in copies:
        copy.wait()


def swap(value, axis, odd):
    count = lax.axis_size(axis)
    return lax.ppermute(value, axis, [(partner(i, count, odd), i) for i in range(count)])


def exchange(sends, z_sends):
    xe, xo, ye, yo = sends
    xe = swap(xe, "gx", 0)
    z_recv = [swap(v, "gz", k) for k, v in enumerate(z_sends)]
    ye, yo = swap(ye, "gy", 0), swap(yo, "gy", 1)
    xo = swap(xo, "gx", 1)
    return [xe, xo, ye, yo], z_recv


def fetch(value, word_y, word_z):
    n_y, n_z = lax.axis_size("gy"), lax.axis_size("gz")
    which = []
    for y in range(n_y):
        for z in range(n_z):
            source = follow(y, n_y, word_y) * n_z + follow(z, n_z, word_z)
            which.append((source, y * n_z + z))
    return lax.ppermute(value, ("gy", "gz"), which)


def call(body, name, out_shapes, scratch, *args, in_hbm=0, out_hbm=False):
    near = pl.BlockSpec(memory_space=pltpu.VMEM)
    far = pl.BlockSpec(memory_space=pltpu.HBM)
    return pl.pallas_call(
        body,
        name=name,
        out_shape=[jax.ShapeDtypeStruct(s, jnp.float32) for s in out_shapes],
        in_specs=[far] * in_hbm + [near] * (len(args) - in_hbm),
        out_specs=[far if out_hbm else near] * len(out_shapes),
        scratch_shapes=scratch,
        compiler_params=pltpu.CompilerParams(vmem_limit_bytes=VMEM_LIMIT),
    )(*args)


def shards(rhs, blocks, couplings, agg_ids, coarse_inv):
    _, nx, ny, nz = rhs.shape
    dims = Dims(nx, ny, nz)
    rows = nx * ny
    rhs = rhs.reshape(3, rows, nz)
    blocks = blocks.reshape(9, rows, nz)
    couplings = couplings.reshape(6, rows, nz)
    own = coarse_inv.shape[2]
    n_y, n_z = lax.axis_size("gy"), lax.axis_size("gz")
    owners = n_y * n_z
    z_count = 1 if n_z == 2 else 2
    vector = (3, rows, nz)
    part = functools.partial
    f32 = jnp.float32

    def faces(count, even, odd):
        return [(count * ny, nz)] * 2 + [(count * nx + even, nz), (count * nx + odd, nz)]

    def z_faces(extra):
        return [(8 + extra, nz)] + [(8, nz)] * (z_count - 1)

    _, rest = blocks_of(n_y, n_z)
    pieces = [fetch(coarse_inv, y, z) for y, z in rest]
    first, inverse, rhs, couplings, own_inv, ids, *sends = call(
        part(first_kernel, dims, z_count),
        "first",
        [vector, (9, rows, nz), vector, (6, rows, nz), (36, own), (1, rows)]
        + faces(18, 36, 36)
        + z_faces(36),
        [
            pltpu.VMEM((9, rows, nz), f32),
            pltpu.VMEM(coarse_inv.shape, f32),
            pltpu.VMEM(agg_ids.shape, jnp.int32),
            pltpu.SemaphoreType.DMA((2 * CHUNKS + 3,)),
        ],
        *[
            pltpu.with_memory_space_constraint(v, pltpu.HBM)
            for v in (rhs, blocks, couplings, coarse_inv, agg_ids)
        ],
        in_hbm=5,
    )
    fat, fat_z = exchange(sends[:4], sends[4:])
    second, sums, *sends = call(
        part(second_kernel, dims, z_count),
        "second",
        [vector, vector] + faces(3, 36, 0) + z_faces(72),
        [pltpu.VMEM(vector, f32)],
        inverse,
        couplings,
        first,
        *fat,
        *fat_z,
    )
    thin, thin_z = exchange(sends[:4], sends[4:])
    (packet,) = call(
        part(coarse_kernel, dims, z_count),
        "coarse",
        [(16 + 36, rows // 2)],
        [pltpu.VMEM(vector, f32)] * 2,
        rhs,
        sums,
        couplings,
        second,
        ids,
        *thin,
        *thin_z,
    )
    z_words, y_words = words_of(n_z), words_of(n_y)
    first_z = fetch(packet, (), z_words[1])
    packet = packet[:16]
    others = [fetch(packet, (), z) for z in z_words[2:]]
    packet = jnp.concatenate([packet, first_z[:16]] + others, axis=0)
    packets = [fetch(packet, y, ()) if y else packet for y in y_words]
    stack, y_z = call(
        part(solve_kernel, dims, (n_y, n_z), own),
        "solve",
        [(4 * 8, rows), (2 * 8, rows)],
        [pltpu.VMEM((owners * 8, own), f32)] * 2 + [pltpu.VMEM((owners * 36, own), f32)]
        + [pltpu.VMEM((owners, 8, rows), f32)],
        *packets,
        own_inv,
        fat[2],
        fat[3],
        fat_z[0],
        thin[2],
        thin_z[0],
        first_z,
        *pieces,
    )
    xe, xo = swap(stack, "gx", 0), swap(stack, "gx", 1)
    third, x_third, y_third, *z_sends = call(
        part(third_kernel, dims, z_count),
        "third",
        [vector, (2, 3 * ny, nz), (2, 3 * nx, nz)] + z_faces(0),
        [pltpu.VMEM(vector, f32)] * 4 + [pltpu.VMEM((3, rows // 2, nz), f32)] * 3,
        inverse,
        couplings,
        second,
        stack,
        y_z,
        xe,
        xo,
        *fat,
        *thin,
    )
    z_recv = [swap(v, "gz", k) for k, v in enumerate(z_sends)]
    (out,) = call(
        part(last_kernel, dims),
        "last",
        [vector],
        [pltpu.VMEM(vector, f32)] * 2 + [pltpu.SemaphoreType.DMA((CHUNKS,))],
        inverse,
        couplings,
        first,
        third,
        x_third,
        y_third,
        *z_recv,
        out_hbm=True,
    )
    return out.reshape(3, nx, ny, nz)


def solution(mesh):
    return jax.shard_map(
        shards,
        mesh=mesh,
        in_specs=(
            P(None, "gx", "gy", "gz"),
            P(None, "gx", "gy", "gz"),
            P(None, "gx", "gy", "gz"),
            P("gz", "gx", "gy"),
            P(None, "gx", ("gy", "gz")),
        ),
        out_specs=P(None, "gx", "gy", "gz"),
        check_vma=False,
    )
```

```python
import functools

import jax
import jax.numpy as jnp
from jax import lax
from jax.experimental import pallas as pl
from jax.experimental.pallas import tpu as pltpu
from jax.sharding import PartitionSpec as P

DAMPING = 0.8
AXES = ("gx", "gy", "gz")
VMEM_LIMIT = 12 * 1024 * 1024


def dot_tt(a, b):
    return lax.dot_general(
        a, b, (((1,), (1,)), ((), ())), preferred_element_type=jnp.float32
    )


def dot_00(a, b):
    return lax.dot_general(
        a, b, (((0,), (0,)), ((), ())), preferred_element_type=jnp.float32
    )


def parts3(v):
    high = v.astype(jnp.bfloat16)
    rest = v - high.astype(jnp.float32)
    mid = rest.astype(jnp.bfloat16)
    low = (rest - mid.astype(jnp.float32)).astype(jnp.bfloat16)
    return high, mid, low


def split3(v):
    return jnp.concatenate(parts3(v), axis=0)


def pairs6(v):
    high, mid, low = parts3(v)
    return jnp.concatenate([high, high, high, mid, mid, low], axis=0)


def pairs6_right(v):
    high, mid, low = parts3(v)
    return jnp.concatenate([high, mid, low, high, mid, high], axis=0)


def lane_iota(rows, lanes):
    return lax.broadcasted_iota(jnp.int32, (rows, lanes), 1)


def row_iota(rows, lanes):
    return lax.broadcasted_iota(jnp.int32, (rows, lanes), 0)


def mode_rows(rows, length):
    k = lane_iota(rows, length).astype(jnp.float32)
    m1 = (k - (length - 1) / 2.0) / (length / 2.0) * (3.0 / length) ** 0.5
    m0 = jnp.full((rows, length), length ** (-0.5), jnp.float32)
    return m0, m1


def is_even(axis):
    return lax.rem(lax.axis_index(axis), 2) == 0


def damped_inverse(m):
    a, b, c, d, e, f, g, h, i = m
    co_a = e * i - f * h
    co_b = f * g - d * i
    co_c = d * h - e * g
    determ = a * co_a + b * co_b + c * co_c
    scale = DAMPING / determ
    rows = [
        co_a,
        c * h - b * i,
        b * f - c * e,
        co_b,
        a * i - c * g,
        c * d - a * f,
        co_c,
        b * g - a * h,
        a * e - b * d,
    ]
    return [r * scale for r in rows]


def times(m, v):
    return [m[3 * r] * v[0] + m[3 * r + 1] * v[1] + m[3 * r + 2] * v[2] for r in range(3)]


class Dims:
    def __init__(self, nx, ny, nz):
        self.nx, self.ny, self.nz = nx, ny, nz
        self.rows = nx * ny
        self.groups = self.rows // 8


def tile(ref, c, x, size):
    return ref[c, x * size : (x + 1) * size, :]


def tiles(ref, count, x, size):
    return [tile(ref, c, x, size) for c in range(count)]


def flat_tiles(ref, start, count, size):
    return [ref[(start + c) * size : (start + c + 1) * size, :] for c in range(count)]


def face_index(axis, count):
    even = jnp.where(is_even(axis), count - 1, 0)
    return even, (count - 1) - even


def inner_odd(axis, value):
    count = lax.axis_size(axis)
    at = lax.axis_index(axis)
    return jnp.where((at > 0) & (at < count - 1), value, 0.0)


def put_faces(dims, field, sends):
    xe, xo, ye, yo = sends
    nx, ny = dims.nx, dims.ny
    x_e, x_o = face_index("gx", nx)
    y_e, y_o = face_index("gy", ny)
    for c in range(3):
        x_rows = slice(c * ny, (c + 1) * ny)
        y_rows = slice(c * nx, (c + 1) * nx)
        xe[x_rows, :] = field[c, pl.ds(pl.multiple_of(x_e * ny, ny), ny), :]
        v = field[c, pl.ds(pl.multiple_of(x_o * ny, ny), ny), :]
        xo[x_rows, :] = inner_odd("gx", v)
        ye[y_rows, :] = field[c, pl.ds(y_e, nx, stride=ny), :]
        yo[y_rows, :] = inner_odd("gy", field[c, pl.ds(y_o, nx, stride=ny), :])


def put_z(dims, field, sends):
    groups, nz = dims.groups, dims.nz
    lane = lane_iota(8, nz)
    for odd, (ref, k) in enumerate(zip(sends, face_index("gz", nz))):
        to = lax.rem(lane + nz - k, nz)
        total = []
        for c in range(3):
            face = jnp.zeros((8, nz), jnp.float32)
            for g in range(groups):
                at = c * groups + g
                face = jnp.where(to == at, pltpu.roll(field[c, 8 * g : 8 * g + 8, :], at, 1), face)
            total.append(face)
        face = pltpu.roll(total[0] + total[1] + total[2], lax.rem(nz - k, nz), 1)
        ref[0:8, :] = inner_odd("gz", face) if odd else face


def neighbour(axis, pair, high):
    e, o = pair
    even = is_even(axis)
    return jnp.where(even, e, o) if high else jnp.where(even, o, e)


def place_z(dims, recv, out):
    nz = dims.nz
    lane = lane_iota(8, nz)
    recv = [r[0:8, :] for r in recv]
    if len(recv) == 2:
        low, high = neighbour("gz", recv, False), neighbour("gz", recv, True)
    else:
        at = jnp.where(is_even("gz"), 0, nz - 1)
        moved = pltpu.roll(recv[0], at, 1)
    for c in range(3):
        for g in range(dims.groups):
            k = c * dims.groups + g
            if len(recv) == 2:
                v = jnp.where(
                    lane == nz - 1,
                    pltpu.roll(low, (nz - 1 - k) % nz, 1),
                    pltpu.roll(high, (nz - k) % nz, 1),
                )
            else:
                v = jnp.where(lane == at, pltpu.roll(moved, (nz - k) % nz, 1), 0.0)
            out[c, 8 * g : 8 * g + 8, :] = v


def shifted(v, low, high, axis):
    size = v.shape[axis]
    at = lax.broadcasted_iota(jnp.int32, v.shape, axis)
    below = pltpu.roll(jnp.where(at == size - 1, low, v), 1, axis)
    above = pltpu.roll(jnp.where(at == 0, high, v), size - 1, axis)
    return below, above


def beside(coup, x_pair, y_pair, z_pair):
    return (
        coup[0] * x_pair[0]
        + coup[1] * x_pair[1]
        + (coup[2] * y_pair[0] + coup[3] * y_pair[1])
        + (coup[4] * z_pair[0] + coup[5] * z_pair[1])
    )


def sums_at(dims, x, field, x_halo, y_halo, z_halo, coup):
    nx, ny = dims.nx, dims.ny
    center = tiles(field, 3, x, ny)
    out = []
    for c in range(3):
        low = tile(field, c, x - 1, ny) if x > 0 else x_halo(c, False)
        high = tile(field, c, x + 1, ny) if x < nx - 1 else x_halo(c, True)
        y_pair = shifted(center[c], y_halo(c, x, False), y_halo(c, x, True), 0)
        z = tile(z_halo, c, x, ny)
        z_pair = shifted(center[c], z, z, 1)
        out.append(beside(coup, (low, high), y_pair, z_pair))
    return center, out


def received(dims, recv):
    xe, xo, ye, yo = recv
    nx, ny = dims.nx, dims.ny

    def x_halo(c, high):
        pair = [r[c * ny : (c + 1) * ny, :] for r in (xe, xo)]
        return neighbour("gx", pair, high)

    def y_halo(c, x, high):
        pair = [r[c * nx + x : c * nx + x + 1, :] for r in (ye, yo)]
        return neighbour("gy", pair, high)

    return x_halo, y_halo


def rows_at(dims, x):
    return slice(x * dims.ny, (x + 1) * dims.ny)


def put_inverses(ref, start, pieces):
    for piece in pieces:
        ref[start : start + 36, :] = piece
        start += 36


CHUNKS = 4


def first_kernel(dims, n_z, *refs):
    rhs_in, blocks_in, couplings_in, coarse_inv_in, ids_in = refs[:5]
    first, inverse, rhs, couplings, own, ids, xe, xo, ye, yo = refs[5:15]
    z_sends, (blocks, coarse_inv, square, sems) = refs[15 : 15 + n_z], refs[15 + n_z :]
    step = dims.rows // CHUNKS

    def copy(k, src, dst, rows):
        return pltpu.make_async_copy(src.at[:, rows, :], dst.at[:, rows, :], sems.at[k])

    copies = []
    for k in range(CHUNKS):
        rows = pl.ds(k * step, step)
        copies.append(copy(2 * k, blocks_in, blocks, rows))
        copies.append(copy(2 * k + 1, rhs_in, rhs, rows))
    copies.append(copy(2 * CHUNKS, couplings_in, couplings, pl.ds(0, dims.rows)))
    copies.append(pltpu.make_async_copy(coarse_inv_in, coarse_inv, sems.at[2 * CHUNKS + 1]))
    copies.append(pltpu.make_async_copy(ids_in, square, sems.at[2 * CHUNKS + 2]))
    for c in copies:
        c.start()
    for x in range(dims.nx):
        if x % (dims.nx // CHUNKS) == 0:
            k = x // (dims.nx // CHUNKS)
            copies[2 * k].wait()
            copies[2 * k + 1].wait()
        inv = damped_inverse(tiles(blocks, 9, x, dims.ny))
        at = rows_at(dims, x)
        for k in range(9):
            inverse[k, at, :] = inv[k]
        v = times(inv, tiles(rhs, 3, x, dims.ny))
        for c in range(3):
            first[c, at, :] = v[c]
    for c in copies[-3:]:
        c.wait()
    put_faces(dims, first, (xe, xo, ye, yo))
    put_z(dims, first, z_sends)
    own[...] = coarse_inv[:, 0, :]
    put_inverses(ye, 3 * dims.nx, [own[...]])
    put_inverses(yo, 3 * dims.nx, [own[...]])
    put_inverses(z_sends[0], 8, [own[...]])
    ids[...] = pencil_row(dims, square[0].astype(jnp.float32))


def second_kernel(dims, n_z, inverse, couplings, first, *refs):
    recv, z_recv, refs = refs[:4], refs[4 : 4 + n_z], refs[4 + n_z :]
    second, sums, *sends = refs[:6]
    z_sends, z_halo = refs[6:-1], refs[-1]
    x_halo, y_halo = received(dims, recv)
    place_z(dims, z_recv, z_halo)
    for x in range(dims.nx):
        coup = tiles(couplings, 6, x, dims.ny)
        center, total = sums_at(dims, x, first, x_halo, y_halo, z_halo, coup)
        step = times(tiles(inverse, 9, x, dims.ny), total)
        at = rows_at(dims, x)
        for c in range(3):
            sums[c, at, :] = total[c]
            second[c, at, :] = (2.0 - DAMPING) * center[c] + step[c]
    put_faces(dims, second, sends)
    put_z(dims, second, z_sends)
    even_block, odd_block = [r[3 * dims.nx : 3 * dims.nx + 36, :] for r in recv[2:]]
    put_inverses(sends[2], 3 * dims.nx, [odd_block])
    put_inverses(z_sends[0], 8, [even_block, odd_block])


def coarse_kernel(dims, n_z, rhs, sums, couplings, second, ids, *refs):
    half = dims.rows // 2
    recv, z_recv, refs = refs[:4], refs[4 : 4 + n_z], refs[4 + n_z :]
    packet, resid, z_halo = refs
    x_halo, y_halo = received(dims, recv)
    place_z(dims, z_recv, z_halo)
    rest = 1.0 - DAMPING * (2.0 - DAMPING)
    for x in range(dims.nx):
        coup = tiles(couplings, 6, x, dims.ny)
        _, total = sums_at(dims, x, second, x_halo, y_halo, z_halo, coup)
        at = rows_at(dims, x)
        for c in range(3):
            resid[c, at, :] = rest * rhs[c, at, :] + (total[c] - DAMPING * sums[c, at, :])
    m0, m1 = mode_rows(8, dims.nz)
    row = row_iota(8, dims.nz)
    modes = split3(jnp.where(row == 0, m0, jnp.where(row == 1, m1, 0.0)))
    for c in range(3):
        s = sum(dot_tt(modes, part) for part in parts3(resid[c]))
        s = (s[0:8] + (s[8:16] + s[16:24]))[0:2]
        packet[2 * c : 2 * c + 2, :] = s[:, :half]
        packet[8 + 2 * c : 10 + 2 * c, :] = s[:, half:]
    for k in range(2):
        packet[8 * k + 6 : 8 * k + 7, :] = ids[:, k * half : (k + 1) * half]
        packet[8 * k + 7 : 8 * k + 8, :] = jnp.zeros((1, half), jnp.float32)
    put_inverses(packet, 16, [recv[2][3 * dims.nx : 3 * dims.nx + 36, :]])


def pencil_row(dims, square):
    nx, ny, rows = dims.nx, dims.ny, dims.rows
    lane = lane_iota(ny, rows)
    spread = jnp.where(lax.rem(lane, ny) == row_iota(ny, rows), 1.0, 0.0)
    wide = lax.dot_general(
        square,
        spread,
        (((1,), (0,)), ((), ())),
        precision=lax.Precision.HIGHEST,
        preferred_element_type=jnp.float32,
    )
    lane = lane_iota(nx, rows)
    keep = lax.div(lane, ny) == row_iota(nx, rows)
    return jnp.sum(jnp.where(keep, wide, 0.0), axis=0, keepdims=True)


def partner(index, count, odd):
    if odd:
        return ((index + 1) % count ^ 1) - 1 + (((index + 1) % count ^ 1) == 0) * count
    return index ^ 1


def follow(index, count, word):
    for odd in word:
        index = partner(index, count, odd)
    return index


def words_of(count):
    words, seen = [], set()
    for length in range(count):
        for start in (False, True):
            word = tuple(bool(start) ^ bool(k % 2) for k in range(length))
            to = follow(0, count, word)
            if to not in seen:
                seen.add(to)
                words.append(word)
    return words


def blocks_of(n_y, n_z):
    e, o, none = (False,), (True,), ()
    held = [(none, none), (e, none), (o, none), (none, e), (e, e), (o, e), (e + o, none), (e + o, e)]
    found = {(follow(0, n_y, y), follow(0, n_z, z)) for y, z in held}
    rest = []
    for y in words_of(n_y):
        for z in words_of(n_z):
            at = (follow(0, n_y, y), follow(0, n_z, z))
            if at not in found:
                found.add(at)
                rest.append((y, z))
    return held, rest


def solve_kernel(dims, sizes, own, *refs):
    n_y, n_z = sizes
    owners = n_y * n_z
    rows = dims.rows
    my_y, my_z = lax.axis_index("gy"), lax.axis_index("gz")
    arrived, coarse_inv, refs = refs[:n_y], refs[n_y], refs[n_y + 1 :]
    held, rest = blocks_of(n_y, n_z)
    pieces, refs = refs[: 6 + len(rest)], refs[6 + len(rest) :]
    stack, beyond_out, coarse, correction, inverses, packets = refs
    put_inverses(inverses, 0, [coarse_inv[...]])
    at = 36
    fat_ye, fat_yo, fat_z, thin_ye, thin_z, first_z = pieces[:6]
    for ref, start, count in (
        (fat_ye, 3 * dims.nx, 36),
        (fat_yo, 3 * dims.nx, 36),
        (fat_z, 8, 36),
        (thin_z, 8, 72),
        (thin_ye, 3 * dims.nx, 36),
        (first_z, 16, 36),
    ):
        inverses[at : at + count, :] = ref[start : start + count, :]
        at += count
    for piece in pieces[6:]:
        put_inverses(inverses, at, [piece[:, 0, :]])
        at += 36
    order = held + rest
    for y, ref in zip(words_of(n_y), arrived):
        for k, z in enumerate(words_of(n_z)):
            at = follow(my_y, n_y, y) * n_z + follow(my_z, n_z, z)
            for side in range(2):
                v = ref[16 * k + 8 * side : 16 * k + 8 * side + 8, :]
                packets[at, :, side * rows // 2 : (side + 1) * rows // 2] = v
    local = row_iota(own, rows).astype(jnp.bfloat16)
    one_b = jnp.ones((own, rows), jnp.bfloat16)
    zero_b = jnp.zeros((own, rows), jnp.bfloat16)

    def owner_at(j):
        y, z = order[j]
        return follow(my_y, n_y, y) * n_z + follow(my_z, n_z, z)

    def member(j, ids):
        base = (owner_at(j) * own).astype(jnp.float32)
        rel = jnp.clip(ids - base, -1.0, float(own)).astype(jnp.bfloat16)
        return jnp.where(local == rel, one_b, zero_b)

    coarse[...] = jnp.zeros_like(coarse)

    def add(d, carry):
        pack = packets[d]
        ids = pack[6:7]
        parts = split3(jnp.where(row_iota(8, rows) < 6, pack, 0.0))
        for j in range(owners):
            s = dot_tt(parts, member(j, ids))
            coarse[8 * j : 8 * j + 8] = coarse[8 * j : 8 * j + 8] + (s[0:8] + (s[8:16] + s[16:24]))
        return carry

    lax.fori_loop(0, owners, add, 0, unroll=2)

    for block in range(owners // 8):
        v = [coarse[pl.ds(64 * block + k, 8, stride=8), :] for k in range(6)]
        for i in range(6):
            total = None
            for k in range(6):
                m = inverses[pl.ds(36 * 8 * block + 6 * i + k, 8, stride=36), :]
                total = m * v[k] if total is None else total + m * v[k]
            correction[pl.ds(64 * block + i, 8, stride=8), :] = total
        for i in (6, 7):
            correction[pl.ds(64 * block + i, 8, stride=8), :] = jnp.zeros_like(total)

    def ids_of(y, z):
        inside = (y >= 0) & (y < n_y) & (z >= 0) & (z < n_z)
        y = jnp.clip(y, 0, n_y - 1)
        z = jnp.clip(z, 0, n_z - 1)
        return jnp.where(inside, packets[y * n_z + z, 6:7, :], -1.0)

    upper = lax.rem(lane_iota(1, rows), dims.ny) >= dims.ny // 2

    def y_ids(z):
        return jnp.where(upper, ids_of(my_y - 1, z), ids_of(my_y + 1, z))

    beyond = [1 - my_z] if n_z == 2 else [my_z - 1, my_z + 1]
    wanted = [ids_of(my_y, my_z), y_ids(my_z)]
    wanted += [ids_of(my_y, z) for z in beyond]
    totals = [jnp.zeros((24, rows), jnp.float32) for _ in wanted]
    for j in range(owners):
        left = split3(correction[8 * j : 8 * j + 8])
        for t in range(len(wanted)):
            totals[t] = totals[t] + lax.dot_general(
                left,
                member(j, wanted[t]),
                (((1,), (0,)), ((), ())),
                preferred_element_type=jnp.float32,
            )
    totals = [s[0:8] + (s[8:16] + s[16:24]) for s in totals]
    stack[...] = totals[0]
    beyond_out[0:8] = totals[1]
    if n_z == 2:
        beyond_out[8:16] = jnp.where(my_z == 1, totals[2], 0.0)
        beyond_out[16:24] = jnp.where(my_z == 0, totals[2], 0.0)
    else:
        beyond_out[8:16], beyond_out[16:24] = totals[2], totals[3]


def third_kernel(dims, n_z, inverse, couplings, second, stack, beyond, *refs):
    stacks, third, sends = refs[:2], refs[2], refs[3:7]
    z_sends, (field, y_field, z_field) = refs[7 : 7 + n_z], refs[7 + n_z :]
    nx, ny, nz = dims.nx, dims.ny, dims.nz
    side = nx * ny // 2
    m0, m1 = mode_rows(8, nz)
    row = row_iota(8, nz)
    modes = jnp.concatenate(
        [
            jnp.where(row == 2 * c, m0, jnp.where(row == 2 * c + 1, m1, 0.0))
            for c in range(3)
        ],
        axis=1,
    )
    at = lax.rem(lane_iota(8, 3 * nz), nz)
    wide = pairs6_right(modes)
    last = pairs6_right(jnp.where(at == nz - 1, modes, 0.0))
    start = pairs6_right(jnp.where(at == 0, modes, 0.0))
    my_x, n_x = lax.axis_index("gx"), lax.axis_size("gx")
    x_low = neighbour("gx", [s[:, side:] for s in stacks], False)
    x_high = neighbour("gx", [s[:, :side] for s in stacks], True)
    x_low = jnp.where(my_x > 0, x_low, 0.0)
    x_high = jnp.where(my_x < n_x - 1, x_high, 0.0)
    x_mix = jnp.where(lane_iota(8, side) < side // 2, x_high, x_low)
    x_field = dot_00(pairs6(x_mix), wide)
    for ref, value in (
        (field, dot_00(pairs6(stack[...]), wide)),
        (y_field, dot_00(pairs6(beyond[0:8]), wide)),
        (z_field, dot_00(pairs6(beyond[8:16]), last) + dot_00(pairs6(beyond[16:24]), start)),
    ):
        for c in range(3):
            ref[c] = value[:, c * nz : (c + 1) * nz]

    def x_halo(c, high):
        v = x_field[:, c * nz : (c + 1) * nz]
        return v[0:ny] if high else v[side - ny : side]

    def y_halo(c, x, high):
        return tile(y_field, c, x, ny)

    for x in range(nx):
        coup = tiles(couplings, 6, x, ny)
        center, total = sums_at(dims, x, field, x_halo, y_halo, z_field, coup)
        change = times(tiles(inverse, 9, x, ny), total)
        at = rows_at(dims, x)
        for c in range(3):
            third[c, at, :] = second[c, at, :] + ((1.0 - DAMPING) * center[c] + change[c])
    put_faces(dims, third, sends)
    put_z(dims, third, z_sends)


def last_kernel(dims, n_z, inverse, couplings, first, third, *refs):
    recv, z_recv, (out, z_halo, result, sems) = refs[:4], refs[4 : 4 + n_z], refs[4 + n_z :]
    nx, ny = dims.nx, dims.ny
    copies = []
    step = nx // CHUNKS
    x_halo, y_halo = received(dims, recv)
    place_z(dims, z_recv, z_halo)
    for x in range(nx):
        coup = tiles(couplings, 6, x, ny)
        center, total = sums_at(dims, x, third, x_halo, y_halo, z_halo, coup)
        change = times(tiles(inverse, 9, x, ny), total)
        at = rows_at(dims, x)
        for c in range(3):
            result[c, at, :] = first[c, at, :] + ((1.0 - DAMPING) * center[c] + change[c])
        if (x + 1) % step == 0:
            at = pl.ds((x + 1 - step) * ny, step * ny)
            copy = (result.at[:, at, :], out.at[:, at, :], sems.at[x // step])
            copies.append(pltpu.make_async_copy(*copy))
            copies[-1].start()
    for copy in copies:
        copy.wait()


def swap(value, axis, odd):
    count = lax.axis_size(axis)
    return lax.ppermute(value, axis, [(partner(i, count, odd), i) for i in range(count)])


def swap_inner(value, axis, spare):
    count, other = lax.axis_size(axis), lax.axis_size(spare)
    which = []
    for i in range(count):
        for k in range(other):
            inside = 0 < i < count - 1
            source = (partner(i, count, True), k) if inside else (i, partner(k, other, False))
            which.append((source[0] * other + source[1], i * other + k))
    return lax.ppermute(value, (axis, spare), which)


def exchange(sends, z_sends, ring):
    xe, xo, ye, yo = sends
    xe = swap(xe, "gx", 0)
    z_recv = [swap(v, "gz", k) for k, v in enumerate(z_sends)]
    ye = swap(ye, "gy", 0)
    yo = swap(yo, "gy", 1) if ring else swap_inner(yo, "gy", "gz")
    xo = swap(xo, "gx", 1)
    return [xe, xo, ye, yo], z_recv


def fetch(value, word_y, word_z):
    n_y, n_z = lax.axis_size("gy"), lax.axis_size("gz")
    which = []
    for y in range(n_y):
        for z in range(n_z):
            source = follow(y, n_y, word_y) * n_z + follow(z, n_z, word_z)
            which.append((source, y * n_z + z))
    return lax.ppermute(value, ("gy", "gz"), which)


def call(body, name, out_shapes, scratch, *args, in_hbm=0, out_hbm=False):
    near = pl.BlockSpec(memory_space=pltpu.VMEM)
    far = pl.BlockSpec(memory_space=pltpu.HBM)
    return pl.pallas_call(
        body,
        name=name,
        out_shape=[jax.ShapeDtypeStruct(s, jnp.float32) for s in out_shapes],
        in_specs=[far] * in_hbm + [near] * (len(args) - in_hbm),
        out_specs=[far if out_hbm else near] * len(out_shapes),
        scratch_shapes=scratch,
        compiler_params=pltpu.CompilerParams(vmem_limit_bytes=VMEM_LIMIT),
    )(*args)


def shards(rhs, blocks, couplings, agg_ids, coarse_inv):
    _, nx, ny, nz = rhs.shape
    dims = Dims(nx, ny, nz)
    rows = nx * ny
    rhs = rhs.reshape(3, rows, nz)
    blocks = blocks.reshape(9, rows, nz)
    couplings = couplings.reshape(6, rows, nz)
    own = coarse_inv.shape[2]
    n_y, n_z = lax.axis_size("gy"), lax.axis_size("gz")
    owners = n_y * n_z
    z_count = 1 if n_z == 2 else 2
    vector = (3, rows, nz)
    part = functools.partial
    f32 = jnp.float32

    def faces(count, even, odd):
        return [(count * ny, nz)] * 2 + [(count * nx + even, nz), (count * nx + odd, nz)]

    def z_faces(extra):
        return [(8 + extra, nz)] + [(8, nz)] * (z_count - 1)

    _, rest = blocks_of(n_y, n_z)
    pieces = [fetch(coarse_inv, y, z) for y, z in rest]
    first, inverse, rhs, couplings, own_inv, ids, *sends = call(
        part(first_kernel, dims, z_count),
        "first",
        [vector, (9, rows, nz), vector, (6, rows, nz), (36, own), (1, rows)]
        + faces(3, 36, 36)
        + z_faces(36),
        [
            pltpu.VMEM((9, rows, nz), f32),
            pltpu.VMEM(coarse_inv.shape, f32),
            pltpu.VMEM(agg_ids.shape, jnp.int32),
            pltpu.SemaphoreType.DMA((2 * CHUNKS + 3,)),
        ],
        *[
            pltpu.with_memory_space_constraint(v, pltpu.HBM)
            for v in (rhs, blocks, couplings, coarse_inv, agg_ids)
        ],
        in_hbm=5,
    )
    fat, fat_z = exchange(sends[:4], sends[4:], True)
    second, sums, *sends = call(
        part(second_kernel, dims, z_count),
        "second",
        [vector, vector] + faces(3, 36, 0) + z_faces(72),
        [pltpu.VMEM(vector, f32)],
        inverse,
        couplings,
        first,
        *fat,
        *fat_z,
    )
    thin, thin_z = exchange(sends[:4], sends[4:], False)
    (packet,) = call(
        part(coarse_kernel, dims, z_count),
        "coarse",
        [(16 + 36, rows // 2)],
        [pltpu.VMEM(vector, f32)] * 2,
        rhs,
        sums,
        couplings,
        second,
        ids,
        *thin,
        *thin_z,
    )
    z_words, y_words = words_of(n_z), words_of(n_y)
    first_z = fetch(packet, (), z_words[1])
    packet = packet[:16]
    others = [fetch(packet, (), z) for z in z_words[2:]]
    packet = jnp.concatenate([packet, first_z[:16]] + others, axis=0)
    packets = [fetch(packet, y, ()) if y else packet for y in y_words]
    stack, beyond = call(
        part(solve_kernel, dims, (n_y, n_z), own),
        "solve",
        [(8, rows), (24, rows)],
        [pltpu.VMEM((owners * 8, own), f32)] * 2 + [pltpu.VMEM((owners * 36, own), f32)]
        + [pltpu.VMEM((owners, 8, rows), f32)],
        *packets,
        own_inv,
        fat[2],
        fat[3],
        fat_z[0],
        thin[2],
        thin_z[0],
        first_z,
        *pieces,
    )
    xe, xo = swap(stack, "gx", 0), swap(stack, "gx", 1)
    third, *sends = call(
        part(third_kernel, dims, z_count),
        "third",
        [vector] + faces(3, 0, 0) + z_faces(0),
        [pltpu.VMEM(vector, f32)] * 3,
        inverse,
        couplings,
        second,
        stack,
        beyond,
        xe,
        xo,
    )
    recv, z_recv = exchange(sends[:4], sends[4:], False)
    (out,) = call(
        part(last_kernel, dims, z_count),
        "last",
        [vector],
        [pltpu.VMEM(vector, f32)] * 2 + [pltpu.SemaphoreType.DMA((CHUNKS,))],
        inverse,
        couplings,
        first,
        third,
        *recv,
        *z_recv,
        out_hbm=True,
    )
    return out.reshape(3, nx, ny, nz)


def solution(mesh):
    return jax.shard_map(
        shards,
        mesh=mesh,
        in_specs=(
            P(None, "gx", "gy", "gz"),
            P(None, "gx", "gy", "gz"),
            P(None, "gx", "gy", "gz"),
            P("gz", "gx", "gy"),
            P(None, "gx", ("gy", "gz")),
        ),
        out_specs=P(None, "gx", "gy", "gz"),
        check_vma=False,
    )
```

```python
import functools

import jax
import jax.numpy as jnp
from jax import lax
from jax.experimental import pallas as pl
from jax.experimental.pallas import tpu as pltpu
from jax.sharding import PartitionSpec as P

DAMPING = 0.8
AXES = ("gx", "gy", "gz")
VMEM_LIMIT = 12 * 1024 * 1024


def dot_tt(a, b):
    return lax.dot_general(
        a, b, (((1,), (1,)), ((), ())), preferred_element_type=jnp.float32
    )


def dot_00(a, b):
    return lax.dot_general(
        a, b, (((0,), (0,)), ((), ())), preferred_element_type=jnp.float32
    )


def parts3(v):
    high = v.astype(jnp.bfloat16)
    rest = v - high.astype(jnp.float32)
    mid = rest.astype(jnp.bfloat16)
    low = (rest - mid.astype(jnp.float32)).astype(jnp.bfloat16)
    return high, mid, low


def split3(v):
    return jnp.concatenate(parts3(v), axis=0)


def pairs6(v):
    high, mid, low = parts3(v)
    return jnp.concatenate([high, high, high, mid, mid, low], axis=0)


def pairs6_right(v):
    high, mid, low = parts3(v)
    return jnp.concatenate([high, mid, low, high, mid, high], axis=0)


def lane_iota(rows, lanes):
    return lax.broadcasted_iota(jnp.int32, (rows, lanes), 1)


def row_iota(rows, lanes):
    return lax.broadcasted_iota(jnp.int32, (rows, lanes), 0)


def mode_rows(rows, length):
    k = lane_iota(rows, length).astype(jnp.float32)
    m1 = (k - (length - 1) / 2.0) / (length / 2.0) * (3.0 / length) ** 0.5
    m0 = jnp.full((rows, length), length ** (-0.5), jnp.float32)
    return m0, m1


def is_even(axis):
    return lax.rem(lax.axis_index(axis), 2) == 0


def damped_inverse(m):
    a, b, c, d, e, f, g, h, i = m
    co_a = e * i - f * h
    co_b = f * g - d * i
    co_c = d * h - e * g
    determ = a * co_a + b * co_b + c * co_c
    scale = DAMPING / determ
    rows = [
        co_a,
        c * h - b * i,
        b * f - c * e,
        co_b,
        a * i - c * g,
        c * d - a * f,
        co_c,
        b * g - a * h,
        a * e - b * d,
    ]
    return [r * scale for r in rows]


def times(m, v):
    return [m[3 * r] * v[0] + m[3 * r + 1] * v[1] + m[3 * r + 2] * v[2] for r in range(3)]


class Dims:
    def __init__(self, nx, ny, nz):
        self.nx, self.ny, self.nz = nx, ny, nz
        self.rows = nx * ny
        self.groups = self.rows // 8


def tile(ref, c, x, size):
    return ref[c, x * size : (x + 1) * size, :]


def tiles(ref, count, x, size):
    return [tile(ref, c, x, size) for c in range(count)]


def flat_tiles(ref, start, count, size):
    return [ref[(start + c) * size : (start + c + 1) * size, :] for c in range(count)]


def face_index(axis, count):
    even = jnp.where(is_even(axis), count - 1, 0)
    return even, (count - 1) - even


def inner_odd(axis, value):
    count = lax.axis_size(axis)
    at = lax.axis_index(axis)
    return jnp.where((at > 0) & (at < count - 1), value, 0.0)


def put_x(dims, field, sends):
    ny = dims.ny
    for odd, (ref, x) in enumerate(zip(sends, face_index("gx", dims.nx))):
        for c in range(3):
            v = field[c, pl.ds(pl.multiple_of(x * ny, ny), ny), :]
            ref[c * ny : (c + 1) * ny, :] = inner_odd("gx", v) if odd else v


def put_faces(dims, field, sends):
    nx, ny = dims.nx, dims.ny
    put_x(dims, field, sends[:2])
    for odd, (ref, y) in enumerate(zip(sends[2:], face_index("gy", ny))):
        for c in range(3):
            v = field[c, pl.ds(y, nx, stride=ny), :]
            ref[c * nx : (c + 1) * nx, :] = inner_odd("gy", v) if odd else v


def pack_z(dims, planes, k):
    groups, nz = dims.groups, dims.nz
    to = lax.rem(lane_iota(8, nz) + nz - k, nz)
    total = None
    for c, plane in enumerate(planes):
        face = jnp.zeros((8, nz), jnp.float32)
        for g in range(groups):
            at = c * groups + g
            face = jnp.where(to == at, pltpu.roll(plane[8 * g : 8 * g + 8, :], at, 1), face)
        total = face if total is None else total + face
    return pltpu.roll(total, lax.rem(nz - k, nz), 1)


def put_z(dims, field, sends, couplings=None):
    for odd, (ref, k) in enumerate(zip(sends, face_index("gz", dims.nz))):
        planes = [field.at[c] for c in range(3)]
        if couplings is not None:
            planes.append(couplings.at[jnp.where(k > 0, 5, 4)])
        face = pack_z(dims, planes, k)
        ref[0:8, :] = inner_odd("gz", face) if odd else face


def neighbour(axis, pair, high):
    e, o = pair
    even = is_even(axis)
    return jnp.where(even, e, o) if high else jnp.where(even, o, e)


def place_z(dims, recv, out):
    nz = dims.nz
    lane = lane_iota(8, nz)
    recv = [r[0:8, :] for r in recv]
    if len(recv) == 2:
        low, high = neighbour("gz", recv, False), neighbour("gz", recv, True)
    else:
        at = jnp.where(is_even("gz"), 0, nz - 1)
        moved = pltpu.roll(recv[0], at, 1)
    for c in range(3):
        for g in range(dims.groups):
            k = c * dims.groups + g
            if len(recv) == 2:
                v = jnp.where(
                    lane == nz - 1,
                    pltpu.roll(low, (nz - 1 - k) % nz, 1),
                    pltpu.roll(high, (nz - k) % nz, 1),
                )
            else:
                v = jnp.where(lane == at, pltpu.roll(moved, (nz - k) % nz, 1), 0.0)
            out[c, 8 * g : 8 * g + 8, :] = v


def shifted(v, low, high, axis):
    size = v.shape[axis]
    at = lax.broadcasted_iota(jnp.int32, v.shape, axis)
    below = pltpu.roll(jnp.where(at == size - 1, low, v), 1, axis)
    above = pltpu.roll(jnp.where(at == 0, high, v), size - 1, axis)
    return below, above


def beside(coup, x_pair, y_pair, z_pair):
    return (
        coup[0] * x_pair[0]
        + coup[1] * x_pair[1]
        + (coup[2] * y_pair[0] + coup[3] * y_pair[1])
        + (coup[4] * z_pair[0] + coup[5] * z_pair[1])
    )


def sums_at(dims, x, field, x_halo, y_halo, z_halo, coup):
    nx, ny = dims.nx, dims.ny
    center = tiles(field, 3, x, ny)
    out = []
    for c in range(3):
        low = tile(field, c, x - 1, ny) if x > 0 else x_halo(c, False)
        high = tile(field, c, x + 1, ny) if x < nx - 1 else x_halo(c, True)
        y_pair = shifted(center[c], y_halo(c, x, False), y_halo(c, x, True), 0)
        z = tile(z_halo, c, x, ny)
        z_pair = shifted(center[c], z, z, 1)
        out.append(beside(coup, (low, high), y_pair, z_pair))
    return center, out


def received(dims, recv):
    xe, xo, ye, yo = recv
    nx, ny = dims.nx, dims.ny

    def x_halo(c, high):
        pair = [r[c * ny : (c + 1) * ny, :] for r in (xe, xo)]
        return neighbour("gx", pair, high)

    def y_halo(c, x, high):
        pair = [r[c * nx + x : c * nx + x + 1, :] for r in (ye, yo)]
        return neighbour("gy", pair, high)

    return x_halo, y_halo


def rows_at(dims, x):
    return slice(x * dims.ny, (x + 1) * dims.ny)


def put_inverses(ref, start, pieces):
    for piece in pieces:
        ref[start : start + 36, :] = piece
        start += 36


CHUNKS = 4


def first_kernel(dims, n_z, *refs):
    rhs_in, blocks_in, couplings_in, coarse_inv_in, ids_in = refs[:5]
    first, inverse, rhs, couplings, own, ids, xe, xo, ye, yo = refs[5:15]
    z_sends, (blocks, coarse_inv, square, sems) = refs[15 : 15 + n_z], refs[15 + n_z :]
    step = dims.rows // CHUNKS

    def copy(k, src, dst, rows):
        return pltpu.make_async_copy(src.at[:, rows, :], dst.at[:, rows, :], sems.at[k])

    copies = []
    for k in range(CHUNKS):
        rows = pl.ds(k * step, step)
        copies.append(copy(2 * k, blocks_in, blocks, rows))
        copies.append(copy(2 * k + 1, rhs_in, rhs, rows))
    copies.append(copy(2 * CHUNKS, couplings_in, couplings, pl.ds(0, dims.rows)))
    copies.append(pltpu.make_async_copy(coarse_inv_in, coarse_inv, sems.at[2 * CHUNKS + 1]))
    copies.append(pltpu.make_async_copy(ids_in, square, sems.at[2 * CHUNKS + 2]))
    for c in copies:
        c.start()
    for x in range(dims.nx):
        if x % (dims.nx // CHUNKS) == 0:
            k = x // (dims.nx // CHUNKS)
            copies[2 * k].wait()
            copies[2 * k + 1].wait()
        inv = damped_inverse(tiles(blocks, 9, x, dims.ny))
        at = rows_at(dims, x)
        for k in range(9):
            inverse[k, at, :] = inv[k]
        v = times(inv, tiles(rhs, 3, x, dims.ny))
        for c in range(3):
            first[c, at, :] = v[c]
    for c in copies[-3:]:
        c.wait()
    put_faces(dims, first, (xe, xo, ye, yo))
    put_z(dims, first, z_sends, couplings)
    for odd, (ref, y) in enumerate(zip((ye, yo), face_index("gy", dims.ny))):
        v = couplings[jnp.where(y > 0, 3, 2), pl.ds(y, dims.nx, stride=dims.ny), :]
        ref[3 * dims.nx : 4 * dims.nx, :] = inner_odd("gy", v) if odd else v
    own[...] = coarse_inv[:, 0, :]
    put_inverses(ye, 4 * dims.nx, [own[...]])
    put_inverses(yo, 4 * dims.nx, [own[...]])
    put_inverses(z_sends[0], 8, [own[...]])
    ids[...] = pencil_row(dims, square[0].astype(jnp.float32))


def second_kernel(dims, n_z, inverse, couplings, first, *refs):
    recv, z_recv, refs = refs[:4], refs[4 : 4 + n_z], refs[4 + n_z :]
    second, sums, *sends = refs[:4]
    z_halo = refs[4]
    x_halo, y_halo = received(dims, recv)
    place_z(dims, z_recv, z_halo)
    for x in range(dims.nx):
        coup = tiles(couplings, 6, x, dims.ny)
        center, total = sums_at(dims, x, first, x_halo, y_halo, z_halo, coup)
        step = times(tiles(inverse, 9, x, dims.ny), total)
        at = rows_at(dims, x)
        for c in range(3):
            sums[c, at, :] = total[c]
            second[c, at, :] = (2.0 - DAMPING) * center[c] + step[c]
    put_x(dims, second, sends)


def coarse_kernel(dims, n_z, rhs, sums, couplings, second, ids, *refs):
    nx, ny, nz, rows = dims.nx, dims.ny, dims.nz, dims.rows
    half = rows // 2
    (xe, xo, ye, yo), z_recv, refs = refs[:4], refs[4 : 4 + n_z], refs[4 + n_z :]
    packet, z_more, (resid, wide) = refs[0], refs[1:n_z], refs[n_z:]

    def x_halo(c, high):
        return neighbour("gx", [r[c * ny : (c + 1) * ny, :] for r in (xe, xo)], high)

    rest = 1.0 - DAMPING * (2.0 - DAMPING)
    row = row_iota(ny, nz)
    lane = lane_iota(ny, nz)
    for x in range(nx):
        coup = tiles(couplings, 6, x, ny)
        coup[2] = jnp.where(row == 0, 0.0, coup[2])
        coup[3] = jnp.where(row == ny - 1, 0.0, coup[3])
        coup[4] = jnp.where(lane == 0, 0.0, coup[4])
        coup[5] = jnp.where(lane == nz - 1, 0.0, coup[5])
        at = rows_at(dims, x)
        for c in range(3):
            v = tile(second, c, x, ny)
            low = tile(second, c, x - 1, ny) if x > 0 else x_halo(c, False)
            high = tile(second, c, x + 1, ny) if x < nx - 1 else x_halo(c, True)
            y_pair = (pltpu.roll(v, 1, 0), pltpu.roll(v, ny - 1, 0))
            z_pair = (pltpu.roll(v, 1, 1), pltpu.roll(v, nz - 1, 1))
            total = beside(coup, (low, high), y_pair, z_pair)
            resid[c, at, :] = rest * rhs[c, at, :] + (total - DAMPING * sums[c, at, :])
    m0, m1 = mode_rows(8, nz)
    row = row_iota(8, nz)
    modes = split3(jnp.where(row == 0, m0, jnp.where(row == 1, m1, 0.0)))

    def mode_sums(v):
        s = sum(dot_tt(modes, part) for part in parts3(v))
        return s[0:8] + (s[8:16] + s[16:24])

    for c in range(3):
        s = mode_sums(resid[c])
        packet[2 * c : 2 * c + 2, :] = s[0:2, :half]
        packet[8 + 2 * c : 10 + 2 * c, :] = s[0:2, half:]
    toward = [
        neighbour("gy", [r[3 * nx : 4 * nx, :] for r in (ye, yo)], high) for high in (False, True)
    ]
    wide[...] = jnp.zeros_like(wide)
    for c in range(3):
        for side, y in enumerate((0, ny - 1)):
            at = (2 * c + side) * nx
            wide[at : at + nx, :] = toward[side] * second[c, pl.ds(y, nx, stride=ny), :]
    s = mode_sums(wide[...])
    for k in range(2):
        packet[8 * k + 6 : 8 * k + 7, :] = ids[:, k * half : (k + 1) * half]
        packet[8 * k + 7 : 8 * k + 8, :] = s[k : k + 1, :]
    groups = dims.groups
    lane = lane_iota(nz, 3 * rows)
    c_of, p_of = lax.div(lane, rows), lax.rem(lane, rows)
    spread = jnp.where(row_iota(nz, 3 * rows) == c_of * groups + lax.div(p_of, 8), 1.0, 0.0)
    spread = spread.astype(jnp.bfloat16)
    keep = lax.rem(lane_iota(8, 3 * rows), 8) == row_iota(8, 3 * rows)
    steps = [(packet, 16), *[(ref, 0) for ref in z_more]]
    for (ref, at), recv, k in zip(steps, z_recv, face_index("gz", nz)):
        face = pack_z(dims, [second.at[c] for c in range(3)], k)
        beyond = recv[0:8, :]
        coup = jnp.zeros_like(beyond)
        lane = lane_iota(8, nz)
        for c in range(3):
            inside = (lane >= c * groups) & (lane < (c + 1) * groups)
            coup = jnp.where(inside, pltpu.roll(beyond, (nz - (3 - c) * groups) % nz, 1), coup)
        s = lax.dot_general(
            split3(coup * face),
            spread,
            (((1,), (0,)), ((), ())),
            preferred_element_type=jnp.float32,
        )
        s = jnp.where(keep, s[0:8] + (s[8:16] + s[16:24]), 0.0)
        s = jnp.sum(s, axis=0, keepdims=True)
        mode = ((nz - 1 - k).astype(jnp.float32) - (nz - 1) / 2.0) / (nz / 2.0) * (3.0 / nz) ** 0.5
        ref[at : at + 16, :] = jnp.zeros((16, half), jnp.float32)
        for c in range(3):
            for side in range(2):
                v = s[:, c * rows + side * half : c * rows + (side + 1) * half]
                to = at + 8 * side + 2 * c
                ref[to : to + 1, :] = v * nz ** (-0.5)
                ref[to + 1 : to + 2, :] = v * mode
    put_inverses(packet, 32, [r[4 * nx : 4 * nx + 36, :] for r in (ye, yo)])


def pencil_row(dims, square):
    nx, ny, rows = dims.nx, dims.ny, dims.rows
    lane = lane_iota(ny, rows)
    spread = jnp.where(lax.rem(lane, ny) == row_iota(ny, rows), 1.0, 0.0)
    wide = lax.dot_general(
        square,
        spread,
        (((1,), (0,)), ((), ())),
        precision=lax.Precision.HIGHEST,
        preferred_element_type=jnp.float32,
    )
    lane = lane_iota(nx, rows)
    keep = lax.div(lane, ny) == row_iota(nx, rows)
    return jnp.sum(jnp.where(keep, wide, 0.0), axis=0, keepdims=True)


def partner(index, count, odd):
    if odd:
        return ((index + 1) % count ^ 1) - 1 + (((index + 1) % count ^ 1) == 0) * count
    return index ^ 1


def follow(index, count, word):
    for odd in word:
        index = partner(index, count, odd)
    return index


def words_of(count):
    words, seen = [], set()
    for length in range(count):
        for start in (False, True):
            word = tuple(bool(start) ^ bool(k % 2) for k in range(length))
            to = follow(0, count, word)
            if to not in seen:
                seen.add(to)
                words.append(word)
    return words


def blocks_of(n_y, n_z):
    e, o, none = (False,), (True,), ()
    held = [(none, none), (e, none), (o, none), (none, e), (e, e), (o, e), (e + o, none), (e + o, e)]
    found = {(follow(0, n_y, y), follow(0, n_z, z)) for y, z in held}
    rest = []
    for y in words_of(n_y):
        for z in words_of(n_z):
            at = (follow(0, n_y, y), follow(0, n_z, z))
            if at not in found:
                found.add(at)
                rest.append((y, z))
    return held, rest


def add_beside(dims, sizes, packets):
    n_y, n_z = sizes
    owners = n_y * n_z
    nx, ny, nz, rows = dims.nx, dims.ny, dims.nz, dims.rows
    half = rows // 2
    lane = lane_iota(half, 3 * rows)
    row = row_iota(half, 3 * rows)
    c, p = lax.div(lane, rows), lax.rem(lane, rows)
    x, y = lax.div(p, ny), lax.rem(p, ny)
    low, high = row == 2 * c * nx + x, row == (2 * c + 1) * nx + x
    spread = jnp.where(((y == ny - 1) & low) | ((y == 0) & high), 1.0, 0.0).astype(jnp.bfloat16)
    y = lax.rem(lane_iota(owners, 3 * rows), ny)
    for m in range(2):
        parts = parts3(packets[m][pl.ds(7, owners, stride=8), :])
        s = sum(
            lax.dot_general(
                part, spread, (((1,), (0,)), ((), ())), preferred_element_type=jnp.float32
            )
            for part in parts
        )
        above, below = pltpu.roll(s, owners - n_z, 0), pltpu.roll(s, n_z, 0)
        s = jnp.where(y == ny - 1, above, jnp.where(y == 0, below, 0.0))
        for c in range(3):
            at = pl.ds(2 * c + m, owners, stride=8)
            for side in range(2):
                v = s[:, c * rows + side * half : c * rows + (side + 1) * half]
                packets[side][at, :] = packets[side][at, :] + v


def solve_kernel(dims, sizes, own, *refs):
    n_y, n_z = sizes
    owners = n_y * n_z
    rows = dims.rows
    my_y, my_z = lax.axis_index("gy"), lax.axis_index("gz")
    arrived, coarse_inv, refs = refs[:n_y], refs[n_y], refs[n_y + 1 :]
    held, rest = blocks_of(n_y, n_z)
    pieces, refs = refs[: 5 + len(rest)], refs[5 + len(rest) :]
    stack, beyond_out, coarse, correction, inverses, *packets = refs
    put_inverses(inverses, 0, [coarse_inv[...]])
    at = 36
    ye, yo, z, more_z, more_e = pieces[:5]
    for ref, start, count in (
        (ye, 4 * dims.nx, 36),
        (yo, 4 * dims.nx, 36),
        (z, 8, 36),
        (more_z, 32, 72),
        (more_e, 16 * n_z, 72),
    ):
        inverses[at : at + count, :] = ref[start : start + count, :]
        at += count
    for piece in pieces[5:]:
        put_inverses(inverses, at, [piece[:, 0, :]])
        at += 36
    order = held + rest
    for y, ref in zip(words_of(n_y), arrived):
        for k, z in enumerate(words_of(n_z)):
            at = follow(my_y, n_y, y) * n_z + follow(my_z, n_z, z)
            at = pl.ds(pl.multiple_of(8 * at, 8), 8)
            for side in range(2):
                packets[side][at, :] = ref[16 * k + 8 * side : 16 * k + 8 * side + 8, :]
    add_beside(dims, sizes, packets)

    def packet_of(d):
        at = pl.ds(pl.multiple_of(8 * d, 8), 8)
        return jnp.concatenate([packets[0][at, :], packets[1][at, :]], axis=1)

    local = row_iota(own, rows).astype(jnp.bfloat16)
    one_b = jnp.ones((own, rows), jnp.bfloat16)
    zero_b = jnp.zeros((own, rows), jnp.bfloat16)

    def owner_at(j):
        y, z = order[j]
        return follow(my_y, n_y, y) * n_z + follow(my_z, n_z, z)

    def member(j, ids):
        base = (owner_at(j) * own).astype(jnp.float32)
        rel = jnp.clip(ids - base, -1.0, float(own)).astype(jnp.bfloat16)
        return jnp.where(local == rel, one_b, zero_b)

    coarse[...] = jnp.zeros_like(coarse)

    def add(d, carry):
        pack = packet_of(d)
        ids = pack[6:7]
        parts = split3(jnp.where(row_iota(8, rows) < 6, pack, 0.0))
        for j in range(owners):
            s = dot_tt(parts, member(j, ids))
            coarse[8 * j : 8 * j + 8] = coarse[8 * j : 8 * j + 8] + (s[0:8] + (s[8:16] + s[16:24]))
        return carry

    lax.fori_loop(0, owners, add, 0, unroll=2)

    for block in range(owners // 8):
        v = [coarse[pl.ds(64 * block + k, 8, stride=8), :] for k in range(6)]
        for i in range(6):
            total = None
            for k in range(6):
                m = inverses[pl.ds(36 * 8 * block + 6 * i + k, 8, stride=36), :]
                total = m * v[k] if total is None else total + m * v[k]
            correction[pl.ds(64 * block + i, 8, stride=8), :] = total
        for i in (6, 7):
            correction[pl.ds(64 * block + i, 8, stride=8), :] = jnp.zeros_like(total)

    def ids_of(y, z):
        inside = (y >= 0) & (y < n_y) & (z >= 0) & (z < n_z)
        y = jnp.clip(y, 0, n_y - 1)
        z = jnp.clip(z, 0, n_z - 1)
        return jnp.where(inside, packet_of(y * n_z + z)[6:7], -1.0)

    upper = lax.rem(lane_iota(1, rows), dims.ny) >= dims.ny // 2

    def y_ids(z):
        return jnp.where(upper, ids_of(my_y - 1, z), ids_of(my_y + 1, z))

    beyond = [1 - my_z] if n_z == 2 else [my_z - 1, my_z + 1]
    wanted = [ids_of(my_y, my_z), y_ids(my_z)]
    wanted += [ids_of(my_y, z) for z in beyond]
    totals = [jnp.zeros((24, rows), jnp.float32) for _ in wanted]
    for j in range(owners):
        left = split3(correction[8 * j : 8 * j + 8])
        for t in range(len(wanted)):
            totals[t] = totals[t] + lax.dot_general(
                left,
                member(j, wanted[t]),
                (((1,), (0,)), ((), ())),
                preferred_element_type=jnp.float32,
            )
    totals = [s[0:8] + (s[8:16] + s[16:24]) for s in totals]
    stack[...] = totals[0]
    beyond_out[0:8] = totals[1]
    if n_z == 2:
        beyond_out[8:16] = jnp.where(my_z == 1, totals[2], 0.0)
        beyond_out[16:24] = jnp.where(my_z == 0, totals[2], 0.0)
    else:
        beyond_out[8:16], beyond_out[16:24] = totals[2], totals[3]


def third_kernel(dims, n_z, inverse, couplings, second, stack, beyond, *refs):
    stacks, third, sends = refs[:2], refs[2], refs[3:7]
    z_sends, (field, y_field, z_field) = refs[7 : 7 + n_z], refs[7 + n_z :]
    nx, ny, nz = dims.nx, dims.ny, dims.nz
    side = nx * ny // 2
    m0, m1 = mode_rows(8, nz)
    row = row_iota(8, nz)
    modes = jnp.concatenate(
        [
            jnp.where(row == 2 * c, m0, jnp.where(row == 2 * c + 1, m1, 0.0))
            for c in range(3)
        ],
        axis=1,
    )
    at = lax.rem(lane_iota(8, 3 * nz), nz)
    wide = pairs6_right(modes)
    last = pairs6_right(jnp.where(at == nz - 1, modes, 0.0))
    start = pairs6_right(jnp.where(at == 0, modes, 0.0))
    my_x, n_x = lax.axis_index("gx"), lax.axis_size("gx")
    x_low = neighbour("gx", [s[:, side:] for s in stacks], False)
    x_high = neighbour("gx", [s[:, :side] for s in stacks], True)
    x_low = jnp.where(my_x > 0, x_low, 0.0)
    x_high = jnp.where(my_x < n_x - 1, x_high, 0.0)
    x_mix = jnp.where(lane_iota(8, side) < side // 2, x_high, x_low)
    x_field = dot_00(pairs6(x_mix), wide)
    for ref, value in (
        (field, dot_00(pairs6(stack[...]), wide)),
        (y_field, dot_00(pairs6(beyond[0:8]), wide)),
        (z_field, dot_00(pairs6(beyond[8:16]), last) + dot_00(pairs6(beyond[16:24]), start)),
    ):
        for c in range(3):
            ref[c] = value[:, c * nz : (c + 1) * nz]

    def x_halo(c, high):
        v = x_field[:, c * nz : (c + 1) * nz]
        return v[0:ny] if high else v[side - ny : side]

    def y_halo(c, x, high):
        return tile(y_field, c, x, ny)

    for x in range(nx):
        coup = tiles(couplings, 6, x, ny)
        center, total = sums_at(dims, x, field, x_halo, y_halo, z_field, coup)
        change = times(tiles(inverse, 9, x, ny), total)
        at = rows_at(dims, x)
        for c in range(3):
            third[c, at, :] = second[c, at, :] + ((1.0 - DAMPING) * center[c] + change[c])
    put_faces(dims, third, sends)
    put_z(dims, third, z_sends)


def last_kernel(dims, n_z, inverse, couplings, first, third, *refs):
    recv, z_recv, (out, z_halo, result, sems) = refs[:4], refs[4 : 4 + n_z], refs[4 + n_z :]
    nx, ny = dims.nx, dims.ny
    copies = []
    step = nx // CHUNKS
    x_halo, y_halo = received(dims, recv)
    place_z(dims, z_recv, z_halo)
    for x in range(nx):
        coup = tiles(couplings, 6, x, ny)
        center, total = sums_at(dims, x, third, x_halo, y_halo, z_halo, coup)
        change = times(tiles(inverse, 9, x, ny), total)
        at = rows_at(dims, x)
        for c in range(3):
            result[c, at, :] = first[c, at, :] + ((1.0 - DAMPING) * center[c] + change[c])
        if (x + 1) % step == 0:
            at = pl.ds((x + 1 - step) * ny, step * ny)
            copy = (result.at[:, at, :], out.at[:, at, :], sems.at[x // step])
            copies.append(pltpu.make_async_copy(*copy))
            copies[-1].start()
    for copy in copies:
        copy.wait()


def swap(value, axis, odd):
    count = lax.axis_size(axis)
    return lax.ppermute(value, axis, [(partner(i, count, odd), i) for i in range(count)])


def swap_inner(value, axis, spare):
    count, other = lax.axis_size(axis), lax.axis_size(spare)
    which = []
    for i in range(count):
        for k in range(other):
            inside = 0 < i < count - 1
            source = (partner(i, count, True), k) if inside else (i, partner(k, other, False))
            which.append((source[0] * other + source[1], i * other + k))
    return lax.ppermute(value, (axis, spare), which)


def exchange(sends, z_sends, ring):
    xe, xo, ye, yo = sends
    xe = swap(xe, "gx", 0)
    z_recv = [swap(v, "gz", k) for k, v in enumerate(z_sends)]
    ye = swap(ye, "gy", 0)
    yo = swap(yo, "gy", 1) if ring else swap_inner(yo, "gy", "gz")
    xo = swap(xo, "gx", 1)
    return [xe, xo, ye, yo], z_recv


def fetch(value, word_y, word_z):
    n_y, n_z = lax.axis_size("gy"), lax.axis_size("gz")
    which = []
    for y in range(n_y):
        for z in range(n_z):
            source = follow(y, n_y, word_y) * n_z + follow(z, n_z, word_z)
            which.append((source, y * n_z + z))
    return lax.ppermute(value, ("gy", "gz"), which)


def call(body, name, out_shapes, scratch, *args, in_hbm=0, out_hbm=False):
    near = pl.BlockSpec(memory_space=pltpu.VMEM)
    far = pl.BlockSpec(memory_space=pltpu.HBM)
    return pl.pallas_call(
        body,
        name=name,
        out_shape=[jax.ShapeDtypeStruct(s, jnp.float32) for s in out_shapes],
        in_specs=[far] * in_hbm + [near] * (len(args) - in_hbm),
        out_specs=[far if out_hbm else near] * len(out_shapes),
        scratch_shapes=scratch,
        compiler_params=pltpu.CompilerParams(vmem_limit_bytes=VMEM_LIMIT),
    )(*args)


def shards(rhs, blocks, couplings, agg_ids, coarse_inv):
    _, nx, ny, nz = rhs.shape
    dims = Dims(nx, ny, nz)
    rows = nx * ny
    rhs = rhs.reshape(3, rows, nz)
    blocks = blocks.reshape(9, rows, nz)
    couplings = couplings.reshape(6, rows, nz)
    own = coarse_inv.shape[2]
    n_y, n_z = lax.axis_size("gy"), lax.axis_size("gz")
    owners = n_y * n_z
    z_count = 1 if n_z == 2 else 2
    vector = (3, rows, nz)
    part = functools.partial
    f32 = jnp.float32

    def faces(count, even, odd):
        return [(count * ny, nz)] * 2 + [(count * nx + even, nz), (count * nx + odd, nz)]

    def z_faces(extra):
        return [(8 + extra, nz)] + [(8, nz)] * (z_count - 1)

    _, rest = blocks_of(n_y, n_z)
    pieces = [fetch(coarse_inv, y, z) for y, z in rest]
    first, inverse, rhs, couplings, own_inv, ids, *sends = call(
        part(first_kernel, dims, z_count),
        "first",
        [vector, (9, rows, nz), vector, (6, rows, nz), (36, own), (1, rows)]
        + faces(3, nx + 36, nx + 36)
        + z_faces(36),
        [
            pltpu.VMEM((9, rows, nz), f32),
            pltpu.VMEM(coarse_inv.shape, f32),
            pltpu.VMEM(agg_ids.shape, jnp.int32),
            pltpu.SemaphoreType.DMA((2 * CHUNKS + 3,)),
        ],
        *[
            pltpu.with_memory_space_constraint(v, pltpu.HBM)
            for v in (rhs, blocks, couplings, coarse_inv, agg_ids)
        ],
        in_hbm=5,
    )
    fat, fat_z = exchange(sends[:4], sends[4:], True)
    second, sums, *sends = call(
        part(second_kernel, dims, z_count),
        "second",
        [vector, vector] + faces(3, 0, 0)[:2],
        [pltpu.VMEM(vector, f32)],
        inverse,
        couplings,
        first,
        *fat,
        *fat_z,
    )
    second_x = [swap(sends[0], "gx", 0), swap(sends[1], "gx", 1)]
    half = rows // 2
    packet, *z_more = call(
        part(coarse_kernel, dims, z_count),
        "coarse",
        [(32 + 72, half)] + [(16, half)] * (z_count - 1),
        [pltpu.VMEM(vector, f32), pltpu.VMEM((half, nz), f32)],
        rhs,
        sums,
        couplings,
        second,
        ids,
        *second_x,
        *fat[2:],
        *fat_z,
    )
    z_words, y_words = words_of(n_z), words_of(n_y)
    if n_z == 2:
        more_z = fetch(packet, (), z_words[1])
        mine = packet[:16] + more_z[16:32]
        theirs = more_z[:16] + packet[16:32]
        joined = jnp.concatenate([mine, theirs], axis=0)
    else:
        mine = packet[:16] + swap(packet[16:32], "gz", 0) + swap(z_more[0], "gz", 1)
        more_z = fetch(jnp.concatenate([mine, packet[16:]], axis=0), (), z_words[1])
        others = [fetch(mine, (), z) for z in z_words[2:]]
        joined = jnp.concatenate([mine, more_z[:16]] + others, axis=0)
    with_more = jnp.concatenate([joined, packet[68:], more_z[68:]], axis=0)
    packets = [joined, fetch(with_more, y_words[1], ())]
    packets += [fetch(joined, y, ()) for y in y_words[2:]]
    stack, beyond = call(
        part(solve_kernel, dims, (n_y, n_z), own),
        "solve",
        [(8, rows), (24, rows)],
        [pltpu.VMEM((owners * 8, own), f32)] * 2 + [pltpu.VMEM((owners * 36, own), f32)]
        + [pltpu.VMEM((owners * 8, half), f32)] * 2,
        *packets,
        own_inv,
        fat[2],
        fat[3],
        fat_z[0],
        more_z,
        packets[1],
        *pieces,
    )
    xe, xo = swap(stack, "gx", 0), swap(stack, "gx", 1)
    third, *sends = call(
        part(third_kernel, dims, z_count),
        "third",
        [vector] + faces(3, 0, 0) + z_faces(0),
        [pltpu.VMEM(vector, f32)] * 3,
        inverse,
        couplings,
        second,
        stack,
        beyond,
        xe,
        xo,
    )
    recv, z_recv = exchange(sends[:4], sends[4:], False)
    (out,) = call(
        part(last_kernel, dims, z_count),
        "last",
        [vector],
        [pltpu.VMEM(vector, f32)] * 2 + [pltpu.SemaphoreType.DMA((CHUNKS,))],
        inverse,
        couplings,
        first,
        third,
        *recv,
        *z_recv,
        out_hbm=True,
    )
    return out.reshape(3, nx, ny, nz)


def solution(mesh):
    return jax.shard_map(
        shards,
        mesh=mesh,
        in_specs=(
            P(None, "gx", "gy", "gz"),
            P(None, "gx", "gy", "gz"),
            P(None, "gx", "gy", "gz"),
            P("gz", "gx", "gy"),
            P(None, "gx", ("gy", "gz")),
        ),
        out_specs=P(None, "gx", "gy", "gz"),
        check_vma=False,
    )
```

```python
import functools

import jax
import jax.numpy as jnp
from jax import lax
from jax.experimental import pallas as pl
from jax.experimental.pallas import tpu as pltpu
from jax.sharding import PartitionSpec as P


DAMPING = 0.8
VMEM_LIMIT = 12 * 1024 * 1024
EO = (False, True)


def dot_tt(a, b):
    return lax.dot_general(
        a, b, (((1,), (1,)), ((), ())), preferred_element_type=jnp.float32
    )


def dot_00(a, b):
    return lax.dot_general(
        a, b, (((0,), (0,)), ((), ())), preferred_element_type=jnp.float32
    )


def parts3(v):
    high = v.astype(jnp.bfloat16)
    rest = v - high.astype(jnp.float32)
    mid = rest.astype(jnp.bfloat16)
    low = (rest - mid.astype(jnp.float32)).astype(jnp.bfloat16)
    return high, mid, low


def split3(v):
    return jnp.concatenate(parts3(v), axis=0)


def pairs6(v):
    high, mid, low = parts3(v)
    return jnp.concatenate([high, high, high, mid, mid, low], axis=0)


def pairs6_right(v):
    high, mid, low = parts3(v)
    return jnp.concatenate([high, mid, low, high, mid, high], axis=0)


def lane_iota(rows, lanes):
    return lax.broadcasted_iota(jnp.int32, (rows, lanes), 1)


def row_iota(rows, lanes):
    return lax.broadcasted_iota(jnp.int32, (rows, lanes), 0)


def mode_rows(rows, length):
    k = lane_iota(rows, length).astype(jnp.float32)
    m1 = (k - (length - 1) / 2.0) / (length / 2.0) * (3.0 / length) ** 0.5
    m0 = jnp.full((rows, length), length ** (-0.5), jnp.float32)
    return m0, m1


def is_even(axis):
    return lax.rem(lax.axis_index(axis), 2) == 0


def damped_inverse(m):
    a, b, c, d, e, f, g, h, i = m
    co_a = e * i - f * h
    co_b = f * g - d * i
    co_c = d * h - e * g
    determ = a * co_a + b * co_b + c * co_c
    scale = DAMPING / determ
    rows = [
        co_a,
        c * h - b * i,
        b * f - c * e,
        co_b,
        a * i - c * g,
        c * d - a * f,
        co_c,
        b * g - a * h,
        a * e - b * d,
    ]
    return [r * scale for r in rows]


def times(m, v):
    return [m[3 * r] * v[0] + m[3 * r + 1] * v[1] + m[3 * r + 2] * v[2] for r in range(3)]


class Dims:
    def __init__(self, nx, ny, nz):
        self.nx, self.ny, self.nz = nx, ny, nz
        self.rows = nx * ny
        self.groups = self.rows // 8


def tile(ref, c, x, size):
    return ref[c, x * size : (x + 1) * size, :]


def tiles(ref, count, x, size):
    return [tile(ref, c, x, size) for c in range(count)]


def face_index(axis, count):
    even = jnp.where(is_even(axis), count - 1, 0)
    return even, (count - 1) - even


def inner_odd(axis, value):
    count = lax.axis_size(axis)
    at = lax.axis_index(axis)
    return jnp.where((at > 0) & (at < count - 1), value, 0.0)


def put_x(dims, field, sends):
    ny = dims.ny
    for odd, (ref, x) in enumerate(zip(sends, face_index("gx", dims.nx))):
        for c in range(3):
            v = field[c, pl.ds(pl.multiple_of(x * ny, ny), ny), :]
            ref[c * ny : (c + 1) * ny, :] = inner_odd("gx", v) if odd else v


def put_faces(dims, field, sends):
    nx, ny = dims.nx, dims.ny
    put_x(dims, field, sends[:2])
    for odd, (ref, y) in enumerate(zip(sends[2:], face_index("gy", ny))):
        for c in range(3):
            v = field[c, pl.ds(y, nx, stride=ny), :]
            ref[c * nx : (c + 1) * nx, :] = inner_odd("gy", v) if odd else v


def pack_z(dims, planes, k):
    groups, nz = dims.groups, dims.nz
    to = lax.rem(lane_iota(8, nz) + nz - k, nz)
    total = None
    for c, plane in enumerate(planes):
        face = jnp.zeros((8, nz), jnp.float32)
        for g in range(groups):
            at = c * groups + g
            face = jnp.where(to == at, pltpu.roll(plane[8 * g : 8 * g + 8, :], at, 1), face)
        total = face if total is None else total + face
    return pltpu.roll(total, lax.rem(nz - k, nz), 1)


def put_z(dims, field, sends, couplings=None):
    for odd, (ref, k) in enumerate(zip(sends, face_index("gz", dims.nz))):
        planes = [field.at[c] for c in range(3)]
        if couplings is not None:
            planes.append(couplings.at[jnp.where(k > 0, 5, 4)])
        face = pack_z(dims, planes, k)
        ref[0:8, :] = inner_odd("gz", face) if odd else face


def neighbour(axis, pair, high):
    e, o = pair
    even = is_even(axis)
    return jnp.where(even, e, o) if high else jnp.where(even, o, e)


def place_z(dims, recv, out):
    nz = dims.nz
    lane = lane_iota(8, nz)
    recv = [r[0:8, :] for r in recv]
    if len(recv) == 2:
        low, high = neighbour("gz", recv, False), neighbour("gz", recv, True)
    else:
        at = jnp.where(is_even("gz"), 0, nz - 1)
        moved = pltpu.roll(recv[0], at, 1)
    for c in range(3):
        for g in range(dims.groups):
            k = c * dims.groups + g
            if len(recv) == 2:
                v = jnp.where(
                    lane == nz - 1,
                    pltpu.roll(low, (nz - 1 - k) % nz, 1),
                    pltpu.roll(high, (nz - k) % nz, 1),
                )
            else:
                v = jnp.where(lane == at, pltpu.roll(moved, (nz - k) % nz, 1), 0.0)
            out[c, 8 * g : 8 * g + 8, :] = v


def shifted(v, low, high, axis):
    size = v.shape[axis]
    at = lax.broadcasted_iota(jnp.int32, v.shape, axis)
    below = pltpu.roll(jnp.where(at == size - 1, low, v), 1, axis)
    above = pltpu.roll(jnp.where(at == 0, high, v), size - 1, axis)
    return below, above


def beside(coup, x_pair, y_pair, z_pair):
    return (
        coup[0] * x_pair[0]
        + coup[1] * x_pair[1]
        + (coup[2] * y_pair[0] + coup[3] * y_pair[1])
        + (coup[4] * z_pair[0] + coup[5] * z_pair[1])
    )


def sums_at(dims, x, field, x_halo, y_halo, z_halo, coup):
    nx, ny = dims.nx, dims.ny
    center = tiles(field, 3, x, ny)
    out = []
    for c in range(3):
        low = tile(field, c, x - 1, ny) if x > 0 else x_halo(c, False)
        high = tile(field, c, x + 1, ny) if x < nx - 1 else x_halo(c, True)
        y_pair = shifted(center[c], y_halo(c, x, False), y_halo(c, x, True), 0)
        z = tile(z_halo, c, x, ny)
        z_pair = shifted(center[c], z, z, 1)
        out.append(beside(coup, (low, high), y_pair, z_pair))
    return center, out


def received(dims, recv):
    xe, xo, ye, yo = recv
    nx, ny = dims.nx, dims.ny

    def x_halo(c, high):
        pair = [r[c * ny : (c + 1) * ny, :] for r in (xe, xo)]
        return neighbour("gx", pair, high)

    def y_halo(c, x, high):
        pair = [r[c * nx + x : c * nx + x + 1, :] for r in (ye, yo)]
        return neighbour("gy", pair, high)

    return x_halo, y_halo


def rows_at(dims, x):
    return slice(x * dims.ny, (x + 1) * dims.ny)


def put_inverses(ref, start, pieces):
    for piece in pieces:
        ref[start : start + 36, :] = piece
        start += 36


def put_tables(dims, spread_y, spread_z):
    nx, ny, rows = dims.nx, dims.ny, dims.rows
    half = rows // 2
    for c in range(3):
        row, p = row_iota(half, rows), lane_iota(half, rows)
        x, y = lax.div(p, ny), lax.rem(p, ny)
        low, high = row == 2 * c * nx + x, row == (2 * c + 1) * nx + x
        at = slice(c * rows, (c + 1) * rows)
        hit = ((y == ny - 1) & low) | ((y == 0) & high)
        spread_y[:, at] = jnp.where(hit, 1.0, 0.0).astype(jnp.bfloat16)
        hit = row == c * dims.groups + lax.div(p, 8)
        spread_z[:, at] = jnp.where(hit, 1.0, 0.0).astype(jnp.bfloat16)


CHUNKS = 4


def first_kernel(dims, n_z, *refs):
    rhs_in, blocks_in, couplings_in, coarse_inv_in, ids_in = refs[:5]
    first, inverse, rhs, couplings, own, ids, spread_y, spread_z, xe, xo, ye, yo = refs[5:17]
    z_sends, (blocks, coarse_inv, square, sems) = refs[17 : 17 + n_z], refs[17 + n_z :]
    step = dims.rows // CHUNKS

    def copy(k, src, dst, rows):
        return pltpu.make_async_copy(src.at[:, rows, :], dst.at[:, rows, :], sems.at[k])

    copies = []
    for k in range(CHUNKS):
        rows = pl.ds(k * step, step)
        copies.append(copy(2 * k, blocks_in, blocks, rows))
        copies.append(copy(2 * k + 1, rhs_in, rhs, rows))
    copies.append(copy(2 * CHUNKS, couplings_in, couplings, pl.ds(0, dims.rows)))
    copies.append(pltpu.make_async_copy(coarse_inv_in, coarse_inv, sems.at[2 * CHUNKS + 1]))
    copies.append(pltpu.make_async_copy(ids_in, square, sems.at[2 * CHUNKS + 2]))
    for c in copies:
        c.start()
    put_tables(dims, spread_y, spread_z)
    for x in range(dims.nx):
        if x % (dims.nx // CHUNKS) == 0:
            k = x // (dims.nx // CHUNKS)
            copies[2 * k].wait()
            copies[2 * k + 1].wait()
        inv = damped_inverse(tiles(blocks, 9, x, dims.ny))
        at = rows_at(dims, x)
        for k in range(9):
            inverse[k, at, :] = inv[k]
        v = times(inv, tiles(rhs, 3, x, dims.ny))
        for c in range(3):
            first[c, at, :] = v[c]
    for c in copies[-3:]:
        c.wait()
    put_faces(dims, first, (xe, xo, ye, yo))
    put_z(dims, first, z_sends, couplings)
    for odd, (ref, y) in enumerate(zip((ye, yo), face_index("gy", dims.ny))):
        v = couplings[jnp.where(y > 0, 3, 2), pl.ds(y, dims.nx, stride=dims.ny), :]
        ref[3 * dims.nx : 4 * dims.nx, :] = inner_odd("gy", v) if odd else v
    own[...] = coarse_inv[:, 0, :]
    put_inverses(ye, 4 * dims.nx, [own[...]])
    put_inverses(z_sends[0], 8, [own[...]])
    ids[...] = pencil_row(dims, square[0].astype(jnp.float32))


def second_kernel(dims, n_z, inverse, couplings, first, own, *refs):
    recv, z_recv, refs = refs[:4], refs[4 : 4 + n_z], refs[4 + n_z :]
    second, sums, *sends = refs[:4]
    inverses, z_halo = refs[4:]
    e_block = recv[2][4 * dims.nx : 4 * dims.nx + 36, :]
    put_inverses(inverses, 0, [own[...], z_recv[0][8:44, :], e_block])
    x_halo, y_halo = received(dims, recv)
    place_z(dims, z_recv, z_halo)
    for x in range(dims.nx):
        coup = tiles(couplings, 6, x, dims.ny)
        center, total = sums_at(dims, x, first, x_halo, y_halo, z_halo, coup)
        step = times(tiles(inverse, 9, x, dims.ny), total)
        at = rows_at(dims, x)
        for c in range(3):
            sums[c, at, :] = total[c]
            second[c, at, :] = (2.0 - DAMPING) * center[c] + step[c]
    put_x(dims, second, sends)


def coarse_kernel(dims, n_z, rhs, sums, couplings, second, ids, spread, *refs):
    nx, ny, nz, rows = dims.nx, dims.ny, dims.nz, dims.rows
    half = rows // 2
    (xe, xo, ye, yo), z_recv, refs = refs[:4], refs[4 : 4 + n_z], refs[4 + n_z :]
    packet, z_more, (resid, wide) = refs[0], refs[1:n_z], refs[n_z:]

    def x_halo(c, high):
        return neighbour("gx", [r[c * ny : (c + 1) * ny, :] for r in (xe, xo)], high)

    rest = 1.0 - DAMPING * (2.0 - DAMPING)
    row = row_iota(ny, nz)
    lane = lane_iota(ny, nz)
    for x in range(nx):
        coup = tiles(couplings, 6, x, ny)
        coup[2] = jnp.where(row == 0, 0.0, coup[2])
        coup[3] = jnp.where(row == ny - 1, 0.0, coup[3])
        coup[4] = jnp.where(lane == 0, 0.0, coup[4])
        coup[5] = jnp.where(lane == nz - 1, 0.0, coup[5])
        at = rows_at(dims, x)
        for c in range(3):
            v = tile(second, c, x, ny)
            low = tile(second, c, x - 1, ny) if x > 0 else x_halo(c, False)
            high = tile(second, c, x + 1, ny) if x < nx - 1 else x_halo(c, True)
            y_pair = (pltpu.roll(v, 1, 0), pltpu.roll(v, ny - 1, 0))
            z_pair = (pltpu.roll(v, 1, 1), pltpu.roll(v, nz - 1, 1))
            total = beside(coup, (low, high), y_pair, z_pair)
            resid[c, at, :] = rest * rhs[c, at, :] + (total - DAMPING * sums[c, at, :])
    m0, m1 = mode_rows(8, nz)
    row = row_iota(8, nz)
    modes = split3(jnp.where(row == 0, m0, jnp.where(row == 1, m1, 0.0)))

    def mode_sums(v):
        s = sum(dot_tt(modes, part) for part in parts3(v))
        return s[0:8] + (s[8:16] + s[16:24])

    for c in range(3):
        s = mode_sums(resid[c])
        packet[2 * c : 2 * c + 2, :] = s[0:2, :half]
        packet[8 + 2 * c : 10 + 2 * c, :] = s[0:2, half:]
    toward = [
        neighbour("gy", [r[3 * nx : 4 * nx, :] for r in (ye, yo)], high) for high in (False, True)
    ]
    wide[...] = jnp.zeros_like(wide)
    for c in range(3):
        for side, y in enumerate((0, ny - 1)):
            at = (2 * c + side) * nx
            wide[at : at + nx, :] = toward[side] * second[c, pl.ds(y, nx, stride=ny), :]
    s = mode_sums(wide[...])
    for k in range(2):
        packet[8 * k + 6 : 8 * k + 7, :] = ids[:, k * half : (k + 1) * half]
        packet[8 * k + 7 : 8 * k + 8, :] = s[k : k + 1, :]
    groups = dims.groups
    keep = lax.rem(lane_iota(8, 3 * rows), 8) == row_iota(8, 3 * rows)
    steps = [(packet, 16), *[(ref, 0) for ref in z_more]]
    for (ref, at), recv, k in zip(steps, z_recv, face_index("gz", nz)):
        face = pack_z(dims, [second.at[c] for c in range(3)], k)
        beyond = recv[0:8, :]
        coup = jnp.zeros_like(beyond)
        lane = lane_iota(8, nz)
        for c in range(3):
            inside = (lane >= c * groups) & (lane < (c + 1) * groups)
            coup = jnp.where(inside, pltpu.roll(beyond, (nz - (3 - c) * groups) % nz, 1), coup)
        s = lax.dot_general(
            split3(coup * face),
            spread[...],
            (((1,), (0,)), ((), ())),
            preferred_element_type=jnp.float32,
        )
        s = jnp.where(keep, s[0:8] + (s[8:16] + s[16:24]), 0.0)
        s = jnp.sum(s, axis=0, keepdims=True)
        mode = ((nz - 1 - k).astype(jnp.float32) - (nz - 1) / 2.0) / (nz / 2.0) * (3.0 / nz) ** 0.5
        ref[at : at + 16, :] = jnp.zeros((16, half), jnp.float32)
        for c in range(3):
            for side in range(2):
                v = s[:, c * rows + side * half : c * rows + (side + 1) * half]
                to = at + 8 * side + 2 * c
                ref[to : to + 1, :] = v * nz ** (-0.5)
                ref[to + 1 : to + 2, :] = v * mode


def pencil_row(dims, square):
    nx, ny, rows = dims.nx, dims.ny, dims.rows
    lane = lane_iota(ny, rows)
    spread = jnp.where(lax.rem(lane, ny) == row_iota(ny, rows), 1.0, 0.0)
    wide = lax.dot_general(
        square,
        spread,
        (((1,), (0,)), ((), ())),
        precision=lax.Precision.HIGHEST,
        preferred_element_type=jnp.float32,
    )
    lane = lane_iota(nx, rows)
    keep = lax.div(lane, ny) == row_iota(nx, rows)
    return jnp.sum(jnp.where(keep, wide, 0.0), axis=0, keepdims=True)


def partner(index, count, odd):
    if odd:
        return ((index + 1) % count ^ 1) - 1 + (((index + 1) % count ^ 1) == 0) * count
    return index ^ 1


def follow(index, count, word):
    for odd in word:
        index = partner(index, count, odd)
    return index


def words_of(count):
    words, seen = [], set()
    for length in range(count):
        for start in (False, True):
            word = tuple(bool(start) ^ bool(k % 2) for k in range(length))
            to = follow(0, count, word)
            if to not in seen:
                seen.add(to)
                words.append(word)
    return words


def blocks_of(n_y, n_z):
    e, o, none = (False,), (True,), ()
    held = [(none, none), (e, none), (none, e), (EO, none), (EO, e), (EO + e, none), (e, e), (o, e)]
    found = {(follow(0, n_y, y), follow(0, n_z, z)) for y, z in held}
    rest = []
    for y in words_of(n_y):
        for z in words_of(n_z):
            at = (follow(0, n_y, y), follow(0, n_z, z))
            if at not in found:
                found.add(at)
                rest.append((y, z))
    return held, rest


def add_beside(dims, sizes, packets, spread):
    n_y, n_z = sizes
    owners = n_y * n_z
    ny, rows = dims.ny, dims.rows
    half = rows // 2
    y = lax.rem(lane_iota(owners, 3 * rows), ny)
    for m in range(2):
        parts = parts3(packets[m][pl.ds(7, owners, stride=8), :])
        s = sum(
            lax.dot_general(
                part, spread[...], (((1,), (0,)), ((), ())), preferred_element_type=jnp.float32
            )
            for part in parts
        )
        above, below = pltpu.roll(s, owners - n_z, 0), pltpu.roll(s, n_z, 0)
        s = jnp.where(y == ny - 1, above, jnp.where(y == 0, below, 0.0))
        for c in range(3):
            at = pl.ds(2 * c + m, owners, stride=8)
            for side in range(2):
                v = s[:, c * rows + side * half : c * rows + (side + 1) * half]
                packets[side][at, :] = packets[side][at, :] + v


def solve_kernel(dims, sizes, own, *refs):
    n_y, n_z = sizes
    owners = n_y * n_z
    rows = dims.rows
    my_y, my_z = lax.axis_index("gy"), lax.axis_index("gz")
    arrived, coarse_inv, spread, refs = refs[:n_y], refs[n_y], refs[n_y + 1], refs[n_y + 2 :]
    held, rest = blocks_of(n_y, n_z)
    pieces, refs = refs[: 4 + len(rest)], refs[4 + len(rest) :]
    stack, beyond_out, coarse, correction, inverses, low_half, high_half, parts, members = refs
    packets = (low_half, high_half)
    put_inverses(inverses, 0, [coarse_inv[...]])
    at = 36
    ye, z, far, more_e = pieces[:4]
    for ref, start, count in (
        (ye, 4 * dims.nx, 36),
        (z, 8, 36),
        (far, 0, 108),
        (more_e, 16 * n_z, 72),
    ):
        inverses[at : at + count, :] = ref[start : start + count, :]
        at += count
    for piece in pieces[4:]:
        put_inverses(inverses, at, [piece[:, 0, :]])
        at += 36
    order = held + rest
    for y, ref in zip(words_of(n_y), arrived):
        for k, z in enumerate(words_of(n_z)):
            at = follow(my_y, n_y, y) * n_z + follow(my_z, n_z, z)
            at = pl.ds(pl.multiple_of(8 * at, 8), 8)
            for side in range(2):
                packets[side][at, :] = ref[16 * k + 8 * side : 16 * k + 8 * side + 8, :]
    add_beside(dims, sizes, packets, spread)

    def packet_of(d):
        at = pl.ds(pl.multiple_of(8 * d, 8), 8)
        return jnp.concatenate([packets[0][at, :], packets[1][at, :]], axis=1)

    local = row_iota(own, rows).astype(jnp.bfloat16)
    one_b = jnp.ones((own, rows), jnp.bfloat16)
    zero_b = jnp.zeros((own, rows), jnp.bfloat16)

    def owner_at(j):
        y, z = order[j]
        return follow(my_y, n_y, y) * n_z + follow(my_z, n_z, z)

    def member(j, ids):
        base = (owner_at(j) * own).astype(jnp.float32)
        rel = jnp.clip(ids - base, -1.0, float(own)).astype(jnp.bfloat16)
        return jnp.where(local == rel, one_b, zero_b)

    for d in range(owners):
        pack = packet_of(d)
        parts[:, d * rows : (d + 1) * rows] = split3(jnp.where(row_iota(8, rows) < 6, pack, 0.0))
    for j in range(owners):

        def fill(d, carry, j=j):
            at = pl.ds(pl.multiple_of(d * rows, rows), rows)
            members[:, at] = member(j, packet_of(d)[6:7])
            return carry

        lax.fori_loop(0, owners, fill, 0, unroll=8)
        s = jnp.transpose(dot_tt(members[...], parts[...]))
        coarse[8 * j : 8 * j + 8] = s[0:8] + (s[8:16] + s[16:24])

    for block in range(owners // 8):
        v = [coarse[pl.ds(64 * block + k, 8, stride=8), :] for k in range(6)]
        for i in range(6):
            total = None
            for k in range(6):
                m = inverses[pl.ds(36 * 8 * block + 6 * i + k, 8, stride=36), :]
                total = m * v[k] if total is None else total + m * v[k]
            correction[pl.ds(64 * block + i, 8, stride=8), :] = total
        for i in (6, 7):
            correction[pl.ds(64 * block + i, 8, stride=8), :] = jnp.zeros_like(total)

    def ids_of(y, z):
        inside = (y >= 0) & (y < n_y) & (z >= 0) & (z < n_z)
        y = jnp.clip(y, 0, n_y - 1)
        z = jnp.clip(z, 0, n_z - 1)
        return jnp.where(inside, packet_of(y * n_z + z)[6:7], -1.0)

    upper = lax.rem(lane_iota(1, rows), dims.ny) >= dims.ny // 2

    def y_ids(z):
        return jnp.where(upper, ids_of(my_y - 1, z), ids_of(my_y + 1, z))

    beyond = [1 - my_z] if n_z == 2 else [my_z - 1, my_z + 1]
    wanted = [ids_of(my_y, my_z), y_ids(my_z)]
    wanted += [ids_of(my_y, z) for z in beyond]
    totals = [jnp.zeros((24, rows), jnp.float32) for _ in wanted]
    for j in range(owners):
        left = split3(correction[8 * j : 8 * j + 8])
        for t in range(len(wanted)):
            totals[t] = totals[t] + lax.dot_general(
                left,
                member(j, wanted[t]),
                (((1,), (0,)), ((), ())),
                preferred_element_type=jnp.float32,
            )
    totals = [s[0:8] + (s[8:16] + s[16:24]) for s in totals]
    stack[...] = totals[0]
    beyond_out[0:8] = totals[1]
    if n_z == 2:
        beyond_out[8:16] = jnp.where(my_z == 1, totals[2], 0.0)
        beyond_out[16:24] = jnp.where(my_z == 0, totals[2], 0.0)
    else:
        beyond_out[8:16], beyond_out[16:24] = totals[2], totals[3]


def third_kernel(dims, n_z, inverse, couplings, second, stack, beyond, *refs):
    stacks, third, sends = refs[:2], refs[2], refs[3:7]
    z_sends, (field, y_field, z_field) = refs[7 : 7 + n_z], refs[7 + n_z :]
    nx, ny, nz = dims.nx, dims.ny, dims.nz
    side = nx * ny // 2
    m0, m1 = mode_rows(8, nz)
    row = row_iota(8, nz)
    modes = jnp.concatenate(
        [
            jnp.where(row == 2 * c, m0, jnp.where(row == 2 * c + 1, m1, 0.0))
            for c in range(3)
        ],
        axis=1,
    )
    at = lax.rem(lane_iota(8, 3 * nz), nz)
    wide = pairs6_right(modes)
    last = pairs6_right(jnp.where(at == nz - 1, modes, 0.0))
    start = pairs6_right(jnp.where(at == 0, modes, 0.0))
    my_x, n_x = lax.axis_index("gx"), lax.axis_size("gx")
    x_low = neighbour("gx", [s[:, side:] for s in stacks], False)
    x_high = neighbour("gx", [s[:, :side] for s in stacks], True)
    x_low = jnp.where(my_x > 0, x_low, 0.0)
    x_high = jnp.where(my_x < n_x - 1, x_high, 0.0)
    x_mix = jnp.where(lane_iota(8, side) < side // 2, x_high, x_low)
    x_field = dot_00(pairs6(x_mix), wide)
    for ref, value in (
        (field, dot_00(pairs6(stack[...]), wide)),
        (y_field, dot_00(pairs6(beyond[0:8]), wide)),
        (z_field, dot_00(pairs6(beyond[8:16]), last) + dot_00(pairs6(beyond[16:24]), start)),
    ):
        for c in range(3):
            ref[c] = value[:, c * nz : (c + 1) * nz]

    def x_halo(c, high):
        v = x_field[:, c * nz : (c + 1) * nz]
        return v[0:ny] if high else v[side - ny : side]

    def y_halo(c, x, high):
        return tile(y_field, c, x, ny)

    for x in range(nx):
        coup = tiles(couplings, 6, x, ny)
        center, total = sums_at(dims, x, field, x_halo, y_halo, z_field, coup)
        change = times(tiles(inverse, 9, x, ny), total)
        at = rows_at(dims, x)
        for c in range(3):
            third[c, at, :] = second[c, at, :] + ((1.0 - DAMPING) * center[c] + change[c])
    put_faces(dims, third, sends)
    put_z(dims, third, z_sends)


def last_kernel(dims, n_z, inverse, couplings, first, third, *refs):
    recv, z_recv, (out, z_halo, result, sems) = refs[:4], refs[4 : 4 + n_z], refs[4 + n_z :]
    nx, ny = dims.nx, dims.ny
    copies = []
    step = nx // CHUNKS
    x_halo, y_halo = received(dims, recv)
    place_z(dims, z_recv, z_halo)
    for x in range(nx):
        coup = tiles(couplings, 6, x, ny)
        center, total = sums_at(dims, x, third, x_halo, y_halo, z_halo, coup)
        change = times(tiles(inverse, 9, x, ny), total)
        at = rows_at(dims, x)
        for c in range(3):
            result[c, at, :] = first[c, at, :] + ((1.0 - DAMPING) * center[c] + change[c])
        if (x + 1) % step == 0:
            at = pl.ds((x + 1 - step) * ny, step * ny)
            copy = (result.at[:, at, :], out.at[:, at, :], sems.at[x // step])
            copies.append(pltpu.make_async_copy(*copy))
            copies[-1].start()
    for copy in copies:
        copy.wait()


def swap(value, axis, odd):
    count = lax.axis_size(axis)
    return lax.ppermute(value, axis, [(partner(i, count, odd), i) for i in range(count)])


def swap_inner(value, axis, spare):
    count, other = lax.axis_size(axis), lax.axis_size(spare)
    which = []
    for i in range(count):
        for k in range(other):
            inside = 0 < i < count - 1
            source = (partner(i, count, True), k) if inside else (i, partner(k, other, False))
            which.append((source[0] * other + source[1], i * other + k))
    return lax.ppermute(value, (axis, spare), which)


def exchange(sends, z_sends):
    xe, xo, ye, yo = sends
    z_recv = []
    for k, v in enumerate(z_sends):
        z_recv.append(swap(v, "gz", k))
    ye = swap(ye, "gy", 0)
    yo = swap_inner(yo, "gy", "gz")
    return exchange_x([xe, xo]) + [ye, yo], z_recv


def exchange_x(sends):
    xo = swap(sends[1], "gx", 1)
    xe = swap(sends[0], "gx", 0)
    return [xe, xo]


def fetch(value, word_y, word_z):
    n_y, n_z = lax.axis_size("gy"), lax.axis_size("gz")
    which = []
    for y in range(n_y):
        for z in range(n_z):
            source = follow(y, n_y, word_y) * n_z + follow(z, n_z, word_z)
            which.append((source, y * n_z + z))
    return lax.ppermute(value, ("gy", "gz"), which)


def call(body, out_shapes, scratch, *args, in_hbm=0, out_hbm=False):
    near = pl.BlockSpec(memory_space=pltpu.VMEM)
    far = pl.BlockSpec(memory_space=pltpu.HBM)
    return pl.pallas_call(
        body,
        out_shape=[
            s if hasattr(s, "dtype") else jax.ShapeDtypeStruct(s, jnp.float32) for s in out_shapes
        ],
        in_specs=[far] * in_hbm + [near] * (len(args) - in_hbm),
        out_specs=[far if out_hbm else near] * len(out_shapes),
        scratch_shapes=scratch,
        compiler_params=pltpu.CompilerParams(vmem_limit_bytes=VMEM_LIMIT),
    )(*args)


def cycle(rhs, blocks, couplings, agg_ids, coarse_inv):
    _, nx, ny, nz = rhs.shape
    dims = Dims(nx, ny, nz)
    rows = nx * ny
    rhs = rhs.reshape(3, rows, nz)
    blocks = blocks.reshape(9, rows, nz)
    couplings = couplings.reshape(6, rows, nz)
    own = coarse_inv.shape[2]
    n_y, n_z = lax.axis_size("gy"), lax.axis_size("gz")
    owners = n_y * n_z
    z_count = 1 if n_z == 2 else 2
    vector = (3, rows, nz)
    part = functools.partial
    f32 = jnp.float32

    def faces(count, even, odd):
        return [(count * ny, nz)] * 2 + [(count * nx + even, nz), (count * nx + odd, nz)]

    def z_faces(extra):
        return [(8 + extra, nz)] + [(8, nz)] * (z_count - 1)

    _, rest = blocks_of(n_y, n_z)
    pieces = [fetch(coarse_inv, y, z) for y, z in rest]
    first, inverse, rhs, couplings, own_inv, ids, spread_y, spread_z, *sends = call(
        part(first_kernel, dims, z_count),
        [vector, (9, rows, nz), vector, (6, rows, nz), (36, own), (1, rows)]
        + [jax.ShapeDtypeStruct((rows // 2, 3 * rows), jnp.bfloat16)] * 2
        + faces(3, nx + 36, nx)
        + z_faces(36),
        [
            pltpu.VMEM((9, rows, nz), f32),
            pltpu.VMEM(coarse_inv.shape, f32),
            pltpu.VMEM(agg_ids.shape, jnp.int32),
            pltpu.SemaphoreType.DMA((2 * CHUNKS + 3,)),
        ],
        *[
            pltpu.with_memory_space_constraint(v, pltpu.HBM)
            for v in (rhs, blocks, couplings, coarse_inv, agg_ids)
        ],
        in_hbm=5,
    )
    fat, fat_z = exchange(sends[:4], sends[4:])
    second, sums, *sends, inv_out = call(
        part(second_kernel, dims, z_count),
        [vector, vector] + faces(3, 0, 0)[:2] + [(3 * 36, own)],
        [pltpu.VMEM(vector, f32)],
        inverse,
        couplings,
        first,
        own_inv,
        *fat,
        *fat_z,
    )
    second_x = exchange_x(sends)
    far_inv = fetch(inv_out, EO, ())
    half = rows // 2
    packet, *z_more = call(
        part(coarse_kernel, dims, z_count),
        [(32, half)] + [(16, half)] * (z_count - 1),
        [pltpu.VMEM(vector, f32), pltpu.VMEM((half, nz), f32)],
        rhs,
        sums,
        couplings,
        second,
        ids,
        spread_z,
        *second_x,
        *fat[2:],
        *fat_z,
    )
    z_words, y_words = words_of(n_z), words_of(n_y)
    if n_z == 2:
        more_z = fetch(packet, (), z_words[1])
        mine = packet[:16] + more_z[16:32]
        theirs = more_z[:16] + packet[16:32]
        joined = jnp.concatenate([mine, theirs], axis=0)
    else:
        mine = packet[:16] + swap(packet[16:32], "gz", 0) + swap(z_more[0], "gz", 1)
        joined = jnp.concatenate([mine] + [fetch(mine, (), z) for z in z_words[1:]], axis=0)
    with_more = jnp.concatenate([joined, fat_z[0][8:44], far_inv[36:72]], axis=0)
    packets = [joined]
    for k, y in enumerate(y_words[1:]):
        packets.append(fetch(joined if k else with_more, y, ()))
    stack, beyond = call(
        part(solve_kernel, dims, (n_y, n_z), own),
        [(8, rows), (24, rows)],
        [pltpu.VMEM((owners * 8, own), f32)] * 2 + [pltpu.VMEM((owners * 36, own), f32)]
        + [pltpu.VMEM((owners * 8, half), f32)] * 2
        + [pltpu.VMEM((n, owners * rows), jnp.bfloat16) for n in (24, own)],
        *packets,
        own_inv,
        spread_y,
        fat[2],
        fat_z[0],
        far_inv,
        packets[1],
        *pieces,
    )
    xe, xo = exchange_x([stack, stack])
    third, *sends = call(
        part(third_kernel, dims, z_count),
        [vector] + faces(3, 0, 0) + z_faces(0),
        [pltpu.VMEM(vector, f32)] * 3,
        inverse,
        couplings,
        second,
        stack,
        beyond,
        xe,
        xo,
    )
    recv, z_recv = exchange(sends[:4], sends[4:])
    (out,) = call(
        part(last_kernel, dims, z_count),
        [vector],
        [pltpu.VMEM(vector, f32)] * 2 + [pltpu.SemaphoreType.DMA((CHUNKS,))],
        inverse,
        couplings,
        first,
        third,
        *recv,
        *z_recv,
        out_hbm=True,
    )
    return out.reshape(3, nx, ny, nz)


def solution(mesh):
    return jax.shard_map(
        cycle,
        mesh=mesh,
        in_specs=(
            P(None, "gx", "gy", "gz"),
            P(None, "gx", "gy", "gz"),
            P(None, "gx", "gy", "gz"),
            P("gz", "gx", "gy"),
            P(None, "gx", ("gy", "gz")),
        ),
        out_specs=P(None, "gx", "gy", "gz"),
        check_vma=False,
    )
```

```python
import functools

import jax
import jax.numpy as jnp
from jax import lax
from jax.experimental import pallas as pl
from jax.experimental.pallas import tpu as pltpu
from jax.sharding import PartitionSpec as P


DAMPING = 0.8
VMEM_LIMIT = 12 * 1024 * 1024
EO = (False, True)


def dot_tt(a, b):
    return lax.dot_general(
        a, b, (((1,), (1,)), ((), ())), preferred_element_type=jnp.float32
    )


def dot_00(a, b):
    return lax.dot_general(
        a, b, (((0,), (0,)), ((), ())), preferred_element_type=jnp.float32
    )


def parts3(v):
    high = v.astype(jnp.bfloat16)
    rest = v - high.astype(jnp.float32)
    mid = rest.astype(jnp.bfloat16)
    low = (rest - mid.astype(jnp.float32)).astype(jnp.bfloat16)
    return high, mid, low


def split3(v):
    return jnp.concatenate(parts3(v), axis=0)


def pairs6(v):
    high, mid, low = parts3(v)
    return jnp.concatenate([high, high, high, mid, mid, low], axis=0)


def pairs6_right(v):
    high, mid, low = parts3(v)
    return jnp.concatenate([high, mid, low, high, mid, high], axis=0)


def lane_iota(rows, lanes):
    return lax.broadcasted_iota(jnp.int32, (rows, lanes), 1)


def row_iota(rows, lanes):
    return lax.broadcasted_iota(jnp.int32, (rows, lanes), 0)


def mode_rows(rows, length):
    k = lane_iota(rows, length).astype(jnp.float32)
    m1 = (k - (length - 1) / 2.0) / (length / 2.0) * (3.0 / length) ** 0.5
    m0 = jnp.full((rows, length), length ** (-0.5), jnp.float32)
    return m0, m1


def is_even(axis):
    return lax.rem(lax.axis_index(axis), 2) == 0


def damped_inverse(m):
    a, b, c, d, e, f, g, h, i = m
    co_a = e * i - f * h
    co_b = f * g - d * i
    co_c = d * h - e * g
    determ = a * co_a + b * co_b + c * co_c
    scale = DAMPING / determ
    rows = [
        co_a,
        c * h - b * i,
        b * f - c * e,
        co_b,
        a * i - c * g,
        c * d - a * f,
        co_c,
        b * g - a * h,
        a * e - b * d,
    ]
    return [r * scale for r in rows]


def times(m, v):
    return [m[3 * r] * v[0] + m[3 * r + 1] * v[1] + m[3 * r + 2] * v[2] for r in range(3)]


class Dims:
    def __init__(self, nx, ny, nz):
        self.nx, self.ny, self.nz = nx, ny, nz
        self.rows = nx * ny
        self.groups = self.rows // 8


def tile(ref, c, x, size):
    return ref[c, x * size : (x + 1) * size, :]


def tiles(ref, count, x, size):
    return [tile(ref, c, x, size) for c in range(count)]


def face_index(axis, count):
    even = jnp.where(is_even(axis), count - 1, 0)
    return even, (count - 1) - even


def inner_odd(axis, value):
    count = lax.axis_size(axis)
    at = lax.axis_index(axis)
    return jnp.where((at > 0) & (at < count - 1), value, 0.0)


def put_x(dims, field, sends):
    ny = dims.ny
    for odd, (ref, x) in enumerate(zip(sends, face_index("gx", dims.nx))):
        for c in range(3):
            v = field[c, pl.ds(pl.multiple_of(x * ny, ny), ny), :]
            ref[c * ny : (c + 1) * ny, :] = inner_odd("gx", v) if odd else v


def put_faces(dims, field, sends):
    nx, ny = dims.nx, dims.ny
    put_x(dims, field, sends[:2])
    for odd, (ref, y) in enumerate(zip(sends[2:], face_index("gy", ny))):
        for c in range(3):
            v = field[c, pl.ds(y, nx, stride=ny), :]
            ref[c * nx : (c + 1) * nx, :] = inner_odd("gy", v) if odd else v


def pack_z(dims, planes, k):
    groups, nz = dims.groups, dims.nz
    to = lax.rem(lane_iota(8, nz) + nz - k, nz)
    total = None
    for c, plane in enumerate(planes):
        face = jnp.zeros((8, nz), jnp.float32)
        for g in range(groups):
            at = c * groups + g
            face = jnp.where(to == at, pltpu.roll(plane[8 * g : 8 * g + 8, :], at, 1), face)
        total = face if total is None else total + face
    return pltpu.roll(total, lax.rem(nz - k, nz), 1)


def put_z(dims, field, sends, couplings=None):
    for odd, (ref, k) in enumerate(zip(sends, face_index("gz", dims.nz))):
        planes = [field.at[c] for c in range(3)]
        if couplings is not None:
            planes.append(couplings.at[jnp.where(k > 0, 5, 4)])
        face = pack_z(dims, planes, k)
        ref[0:8, :] = inner_odd("gz", face) if odd else face


def neighbour(axis, pair, high):
    e, o = pair
    even = is_even(axis)
    return jnp.where(even, e, o) if high else jnp.where(even, o, e)


def place_z(dims, recv, out):
    nz = dims.nz
    lane = lane_iota(8, nz)
    recv = [r[0:8, :] for r in recv]
    if len(recv) == 2:
        low, high = neighbour("gz", recv, False), neighbour("gz", recv, True)
    else:
        at = jnp.where(is_even("gz"), 0, nz - 1)
        moved = pltpu.roll(recv[0], at, 1)
    for c in range(3):
        for g in range(dims.groups):
            k = c * dims.groups + g
            if len(recv) == 2:
                v = jnp.where(
                    lane == nz - 1,
                    pltpu.roll(low, (nz - 1 - k) % nz, 1),
                    pltpu.roll(high, (nz - k) % nz, 1),
                )
            else:
                v = jnp.where(lane == at, pltpu.roll(moved, (nz - k) % nz, 1), 0.0)
            out[c, 8 * g : 8 * g + 8, :] = v


def shifted(v, low, high, axis):
    size = v.shape[axis]
    at = lax.broadcasted_iota(jnp.int32, v.shape, axis)
    below = pltpu.roll(jnp.where(at == size - 1, low, v), 1, axis)
    above = pltpu.roll(jnp.where(at == 0, high, v), size - 1, axis)
    return below, above


def beside(coup, x_pair, y_pair, z_pair):
    return (
        coup[0] * x_pair[0]
        + coup[1] * x_pair[1]
        + (coup[2] * y_pair[0] + coup[3] * y_pair[1])
        + (coup[4] * z_pair[0] + coup[5] * z_pair[1])
    )


def sums_at(dims, x, field, x_halo, y_halo, z_halo, coup):
    nx, ny = dims.nx, dims.ny
    center = tiles(field, 3, x, ny)
    out = []
    for c in range(3):
        low = tile(field, c, x - 1, ny) if x > 0 else x_halo(c, False)
        high = tile(field, c, x + 1, ny) if x < nx - 1 else x_halo(c, True)
        y_pair = shifted(center[c], y_halo(c, x, False), y_halo(c, x, True), 0)
        z = tile(z_halo, c, x, ny)
        z_pair = shifted(center[c], z, z, 1)
        out.append(beside(coup, (low, high), y_pair, z_pair))
    return center, out


def received(dims, recv):
    xe, xo, ye, yo = recv
    nx, ny = dims.nx, dims.ny

    def x_halo(c, high):
        pair = [r[c * ny : (c + 1) * ny, :] for r in (xe, xo)]
        return neighbour("gx", pair, high)

    def y_halo(c, x, high):
        pair = [r[c * nx + x : c * nx + x + 1, :] for r in (ye, yo)]
        return neighbour("gy", pair, high)

    return x_halo, y_halo


def rows_at(dims, x):
    return slice(x * dims.ny, (x + 1) * dims.ny)


def put_inverses(ref, start, pieces):
    for piece in pieces:
        ref[start : start + 36, :] = piece
        start += 36


def put_tables(dims, spread_y, spread_z):
    nx, ny, rows = dims.nx, dims.ny, dims.rows
    half = rows // 2
    for c in range(3):
        row, p = row_iota(half, rows), lane_iota(half, rows)
        x, y = lax.div(p, ny), lax.rem(p, ny)
        low, high = row == 2 * c * nx + x, row == (2 * c + 1) * nx + x
        at = slice(c * rows, (c + 1) * rows)
        hit = ((y == ny - 1) & low) | ((y == 0) & high)
        spread_y[:, at] = jnp.where(hit, 1.0, 0.0).astype(jnp.bfloat16)
        hit = row == c * dims.groups + lax.div(p, 8)
        spread_z[:, at] = jnp.where(hit, 1.0, 0.0).astype(jnp.bfloat16)


CHUNKS = 4


def first_kernel(dims, n_z, *refs):
    rhs_in, blocks_in, couplings_in, coarse_inv_in, ids_in = refs[:5]
    first, inverse, rhs, couplings, own, ids, spread_y, spread_z, xe, xo, ye, yo = refs[5:17]
    z_sends, (blocks, coarse_inv, square, sems) = refs[17 : 17 + n_z], refs[17 + n_z :]
    step = dims.rows // CHUNKS

    def copy(k, src, dst, rows):
        return pltpu.make_async_copy(src.at[:, rows, :], dst.at[:, rows, :], sems.at[k])

    copies = []
    for k in range(CHUNKS):
        rows = pl.ds(k * step, step)
        copies.append(copy(2 * k, blocks_in, blocks, rows))
        copies.append(copy(2 * k + 1, rhs_in, rhs, rows))
    copies.append(copy(2 * CHUNKS, couplings_in, couplings, pl.ds(0, dims.rows)))
    copies.append(pltpu.make_async_copy(coarse_inv_in, coarse_inv, sems.at[2 * CHUNKS + 1]))
    copies.append(pltpu.make_async_copy(ids_in, square, sems.at[2 * CHUNKS + 2]))
    for c in copies:
        c.start()
    put_tables(dims, spread_y, spread_z)
    for x in range(dims.nx):
        if x % (dims.nx // CHUNKS) == 0:
            k = x // (dims.nx // CHUNKS)
            copies[2 * k].wait()
            copies[2 * k + 1].wait()
        inv = damped_inverse(tiles(blocks, 9, x, dims.ny))
        at = rows_at(dims, x)
        for k in range(9):
            inverse[k, at, :] = inv[k]
        v = times(inv, tiles(rhs, 3, x, dims.ny))
        for c in range(3):
            first[c, at, :] = v[c]
    for c in copies[-3:]:
        c.wait()
    put_faces(dims, first, (xe, xo, ye, yo))
    put_z(dims, first, z_sends, couplings)
    for odd, (ref, y) in enumerate(zip((ye, yo), face_index("gy", dims.ny))):
        v = couplings[jnp.where(y > 0, 3, 2), pl.ds(y, dims.nx, stride=dims.ny), :]
        ref[3 * dims.nx : 4 * dims.nx, :] = inner_odd("gy", v) if odd else v
    own[...] = coarse_inv[:, 0, :]
    put_inverses(ye, 4 * dims.nx, [own[...]])
    put_inverses(z_sends[0], 8, [own[...]])
    ids[...] = pencil_row(dims, square[0].astype(jnp.float32))


def second_kernel(dims, n_z, inverse, couplings, first, own, *refs):
    recv, z_recv, refs = refs[:4], refs[4 : 4 + n_z], refs[4 + n_z :]
    second, sums, *sends = refs[:4]
    inverses, z_halo = refs[4:]
    e_block = recv[2][4 * dims.nx : 4 * dims.nx + 36, :]
    put_inverses(inverses, 0, [own[...], z_recv[0][8:44, :], e_block])
    x_halo, y_halo = received(dims, recv)
    place_z(dims, z_recv, z_halo)
    for x in range(dims.nx):
        coup = tiles(couplings, 6, x, dims.ny)
        center, total = sums_at(dims, x, first, x_halo, y_halo, z_halo, coup)
        step = times(tiles(inverse, 9, x, dims.ny), total)
        at = rows_at(dims, x)
        for c in range(3):
            sums[c, at, :] = total[c]
            second[c, at, :] = (2.0 - DAMPING) * center[c] + step[c]
    put_x(dims, second, sends)


def mode_sums(nz, v):
    m0, m1 = mode_rows(8, nz)
    row = row_iota(8, nz)
    modes = split3(jnp.where(row == 0, m0, jnp.where(row == 1, m1, 0.0)))
    s = sum(dot_tt(modes, part) for part in parts3(v))
    return s[0:8] + (s[8:16] + s[16:24])


def coarse_kernel(dims, n_z, rhs, sums, couplings, second, ids, spread, *refs):
    nx, ny, nz, rows = dims.nx, dims.ny, dims.nz, dims.rows
    half = rows // 2
    (ye, yo), z_recv, refs = refs[:2], refs[2 : 2 + n_z], refs[2 + n_z :]
    packet, z_more, (resid, wide) = refs[0], refs[1:n_z], refs[n_z:]

    zero = jnp.zeros((ny, nz), jnp.float32)
    rest = 1.0 - DAMPING * (2.0 - DAMPING)
    row = row_iota(ny, nz)
    lane = lane_iota(ny, nz)
    for x in range(nx):
        coup = tiles(couplings, 6, x, ny)
        coup[2] = jnp.where(row == 0, 0.0, coup[2])
        coup[3] = jnp.where(row == ny - 1, 0.0, coup[3])
        coup[4] = jnp.where(lane == 0, 0.0, coup[4])
        coup[5] = jnp.where(lane == nz - 1, 0.0, coup[5])
        at = rows_at(dims, x)
        for c in range(3):
            v = tile(second, c, x, ny)
            low = tile(second, c, x - 1, ny) if x > 0 else zero
            high = tile(second, c, x + 1, ny) if x < nx - 1 else zero
            y_pair = (pltpu.roll(v, 1, 0), pltpu.roll(v, ny - 1, 0))
            z_pair = (pltpu.roll(v, 1, 1), pltpu.roll(v, nz - 1, 1))
            total = beside(coup, (low, high), y_pair, z_pair)
            resid[c, at, :] = rest * rhs[c, at, :] + (total - DAMPING * sums[c, at, :])
    for c in range(3):
        s = mode_sums(nz, resid[c])
        packet[2 * c : 2 * c + 2, :] = s[0:2, :half]
        packet[8 + 2 * c : 10 + 2 * c, :] = s[0:2, half:]
    toward = [
        neighbour("gy", [r[3 * nx : 4 * nx, :] for r in (ye, yo)], high) for high in (False, True)
    ]
    wide[...] = jnp.zeros_like(wide)
    for c in range(3):
        for side, y in enumerate((0, ny - 1)):
            at = (2 * c + side) * nx
            wide[at : at + nx, :] = toward[side] * second[c, pl.ds(y, nx, stride=ny), :]
    s = mode_sums(nz, wide[...])
    for k in range(2):
        packet[8 * k + 6 : 8 * k + 7, :] = ids[:, k * half : (k + 1) * half]
        packet[8 * k + 7 : 8 * k + 8, :] = s[k : k + 1, :]
    groups = dims.groups
    keep = lax.rem(lane_iota(8, 3 * rows), 8) == row_iota(8, 3 * rows)
    steps = [(packet, 16), *[(ref, 0) for ref in z_more]]
    for (ref, at), recv, k in zip(steps, z_recv, face_index("gz", nz)):
        face = pack_z(dims, [second.at[c] for c in range(3)], k)
        beyond = recv[0:8, :]
        coup = jnp.zeros_like(beyond)
        lane = lane_iota(8, nz)
        for c in range(3):
            inside = (lane >= c * groups) & (lane < (c + 1) * groups)
            coup = jnp.where(inside, pltpu.roll(beyond, (nz - (3 - c) * groups) % nz, 1), coup)
        s = lax.dot_general(
            split3(coup * face),
            spread[...],
            (((1,), (0,)), ((), ())),
            preferred_element_type=jnp.float32,
        )
        s = jnp.where(keep, s[0:8] + (s[8:16] + s[16:24]), 0.0)
        s = jnp.sum(s, axis=0, keepdims=True)
        mode = ((nz - 1 - k).astype(jnp.float32) - (nz - 1) / 2.0) / (nz / 2.0) * (3.0 / nz) ** 0.5
        ref[at : at + 16, :] = jnp.zeros((16, half), jnp.float32)
        for c in range(3):
            for side in range(2):
                v = s[:, c * rows + side * half : c * rows + (side + 1) * half]
                to = at + 8 * side + 2 * c
                ref[to : to + 1, :] = v * nz ** (-0.5)
                ref[to + 1 : to + 2, :] = v * mode


def edges_kernel(dims, inside, couplings, xe, xo, packet, wide):
    nx, ny, nz = dims.nx, dims.ny, dims.nz
    half = dims.rows // 2
    wide[...] = jnp.zeros_like(wide)
    for c in range(3):
        for side, x in enumerate((0, nx - 1)):
            pair = [r[c * ny : (c + 1) * ny, :] for r in (xe, xo)]
            v = tile(couplings, side, x, ny) * neighbour("gx", pair, side == 1)
            at = (2 * c + side) * ny
            wide[at : at + ny, :] = v
    s = mode_sums(nz, wide[...])
    row, lane = row_iota(8, half), lane_iota(8, half)
    packet[16:, :] = inside[16:, :]
    for side, (start, keep) in enumerate(((0, lane < ny), (half - ny, lane >= half - ny))):
        total = inside[8 * side : 8 * side + 8, :]
        for c in range(3):
            moved = pltpu.roll(s, (start - (2 * c + side) * ny) % half, 1)
            for m in range(2):
                hit = keep & (row == 2 * c + m)
                total = total + jnp.where(hit, moved[m : m + 1], 0.0)
        packet[8 * side : 8 * side + 8, :] = total


def pencil_row(dims, square):
    nx, ny, rows = dims.nx, dims.ny, dims.rows
    lane = lane_iota(ny, rows)
    spread = jnp.where(lax.rem(lane, ny) == row_iota(ny, rows), 1.0, 0.0)
    wide = lax.dot_general(
        square,
        spread,
        (((1,), (0,)), ((), ())),
        precision=lax.Precision.HIGHEST,
        preferred_element_type=jnp.float32,
    )
    lane = lane_iota(nx, rows)
    keep = lax.div(lane, ny) == row_iota(nx, rows)
    return jnp.sum(jnp.where(keep, wide, 0.0), axis=0, keepdims=True)


def partner(index, count, odd):
    if odd:
        return ((index + 1) % count ^ 1) - 1 + (((index + 1) % count ^ 1) == 0) * count
    return index ^ 1


def follow(index, count, word):
    for odd in word:
        index = partner(index, count, odd)
    return index


def words_of(count):
    words, seen = [], set()
    for length in range(count):
        for start in (False, True):
            word = tuple(bool(start) ^ bool(k % 2) for k in range(length))
            to = follow(0, count, word)
            if to not in seen:
                seen.add(to)
                words.append(word)
    return words


def blocks_of(n_y, n_z):
    e, o, none = (False,), (True,), ()
    held = [(none, none), (e, none), (none, e), (EO, none), (EO, e), (EO + e, none), (e, e), (o, e)]
    found = {(follow(0, n_y, y), follow(0, n_z, z)) for y, z in held}
    rest = []
    for y in words_of(n_y):
        for z in words_of(n_z):
            at = (follow(0, n_y, y), follow(0, n_z, z))
            if at not in found:
                found.add(at)
                rest.append((y, z))
    return held, rest


def add_beside(dims, sizes, packets, spread):
    n_y, n_z = sizes
    owners = n_y * n_z
    ny, rows = dims.ny, dims.rows
    half = rows // 2
    y = lax.rem(lane_iota(owners, 3 * rows), ny)
    for m in range(2):
        parts = parts3(packets[m][pl.ds(7, owners, stride=8), :])
        s = sum(
            lax.dot_general(
                part, spread[...], (((1,), (0,)), ((), ())), preferred_element_type=jnp.float32
            )
            for part in parts
        )
        above, below = pltpu.roll(s, owners - n_z, 0), pltpu.roll(s, n_z, 0)
        s = jnp.where(y == ny - 1, above, jnp.where(y == 0, below, 0.0))
        for c in range(3):
            at = pl.ds(2 * c + m, owners, stride=8)
            for side in range(2):
                v = s[:, c * rows + side * half : c * rows + (side + 1) * half]
                packets[side][at, :] = packets[side][at, :] + v


def solve_kernel(dims, sizes, own, *refs):
    n_y, n_z = sizes
    owners = n_y * n_z
    rows = dims.rows
    my_y, my_z = lax.axis_index("gy"), lax.axis_index("gz")
    arrived, coarse_inv, spread, refs = refs[:n_y], refs[n_y], refs[n_y + 1], refs[n_y + 2 :]
    held, rest = blocks_of(n_y, n_z)
    pieces, refs = refs[: 4 + len(rest)], refs[4 + len(rest) :]
    stack, beyond_out, coarse, correction, inverses, low_half, high_half, parts, members = refs
    packets = (low_half, high_half)
    put_inverses(inverses, 0, [coarse_inv[...]])
    at = 36
    ye, z, far, more_e = pieces[:4]
    for ref, start, count in (
        (ye, 4 * dims.nx, 36),
        (z, 8, 36),
        (far, 0, 108),
        (more_e, 16 * n_z, 72),
    ):
        inverses[at : at + count, :] = ref[start : start + count, :]
        at += count
    for piece in pieces[4:]:
        put_inverses(inverses, at, [piece[:, 0, :]])
        at += 36
    order = held + rest
    for y, ref in zip(words_of(n_y), arrived):
        for k, z in enumerate(words_of(n_z)):
            at = follow(my_y, n_y, y) * n_z + follow(my_z, n_z, z)
            at = pl.ds(pl.multiple_of(8 * at, 8), 8)
            for side in range(2):
                packets[side][at, :] = ref[16 * k + 8 * side : 16 * k + 8 * side + 8, :]
    add_beside(dims, sizes, packets, spread)

    def packet_of(d):
        at = pl.ds(pl.multiple_of(8 * d, 8), 8)
        return jnp.concatenate([packets[0][at, :], packets[1][at, :]], axis=1)

    local = row_iota(own, rows).astype(jnp.bfloat16)
    one_b = jnp.ones((own, rows), jnp.bfloat16)
    zero_b = jnp.zeros((own, rows), jnp.bfloat16)

    def owner_at(j):
        y, z = order[j]
        return follow(my_y, n_y, y) * n_z + follow(my_z, n_z, z)

    def member(j, ids):
        base = (owner_at(j) * own).astype(jnp.float32)
        rel = jnp.clip(ids - base, -1.0, float(own)).astype(jnp.bfloat16)
        return jnp.where(local == rel, one_b, zero_b)

    for d in range(owners):
        pack = packet_of(d)
        parts[:, d * rows : (d + 1) * rows] = split3(jnp.where(row_iota(8, rows) < 6, pack, 0.0))
    for j in range(owners):

        def fill(d, carry, j=j):
            at = pl.ds(pl.multiple_of(d * rows, rows), rows)
            members[:, at] = member(j, packet_of(d)[6:7])
            return carry

        lax.fori_loop(0, owners, fill, 0, unroll=8)
        s = jnp.transpose(dot_tt(members[...], parts[...]))
        coarse[8 * j : 8 * j + 8] = s[0:8] + (s[8:16] + s[16:24])

    for block in range(owners // 8):
        v = [coarse[pl.ds(64 * block + k, 8, stride=8), :] for k in range(6)]
        for i in range(6):
            total = None
            for k in range(6):
                m = inverses[pl.ds(36 * 8 * block + 6 * i + k, 8, stride=36), :]
                total = m * v[k] if total is None else total + m * v[k]
            correction[pl.ds(64 * block + i, 8, stride=8), :] = total
        for i in (6, 7):
            correction[pl.ds(64 * block + i, 8, stride=8), :] = jnp.zeros_like(total)

    def ids_of(y, z):
        inside = (y >= 0) & (y < n_y) & (z >= 0) & (z < n_z)
        y = jnp.clip(y, 0, n_y - 1)
        z = jnp.clip(z, 0, n_z - 1)
        return jnp.where(inside, packet_of(y * n_z + z)[6:7], -1.0)

    upper = lax.rem(lane_iota(1, rows), dims.ny) >= dims.ny // 2

    def y_ids(z):
        return jnp.where(upper, ids_of(my_y - 1, z), ids_of(my_y + 1, z))

    beyond = [1 - my_z] if n_z == 2 else [my_z - 1, my_z + 1]
    wanted = [ids_of(my_y, my_z), y_ids(my_z)]
    wanted += [ids_of(my_y, z) for z in beyond]
    totals = [jnp.zeros((24, rows), jnp.float32) for _ in wanted]
    for j in range(owners):
        left = split3(correction[8 * j : 8 * j + 8])
        for t in range(len(wanted)):
            totals[t] = totals[t] + lax.dot_general(
                left,
                member(j, wanted[t]),
                (((1,), (0,)), ((), ())),
                preferred_element_type=jnp.float32,
            )
    totals = [s[0:8] + (s[8:16] + s[16:24]) for s in totals]
    stack[...] = totals[0]
    beyond_out[0:8] = totals[1]
    if n_z == 2:
        beyond_out[8:16] = jnp.where(my_z == 1, totals[2], 0.0)
        beyond_out[16:24] = jnp.where(my_z == 0, totals[2], 0.0)
    else:
        beyond_out[8:16], beyond_out[16:24] = totals[2], totals[3]


def mode_columns(dims):
    m0, m1 = mode_rows(8, dims.nz)
    row = row_iota(8, dims.nz)
    parts = [
        jnp.where(row == 2 * c, m0, jnp.where(row == 2 * c + 1, m1, 0.0)) for c in range(3)
    ]
    return jnp.concatenate(parts, axis=1)


def third_kernel(dims, inverse, couplings, second, stack, beyond, third, *fields):
    field, y_field, z_field = fields
    nx, ny, nz = dims.nx, dims.ny, dims.nz
    modes = mode_columns(dims)
    at = lax.rem(lane_iota(8, 3 * nz), nz)
    wide = pairs6_right(modes)
    last = pairs6_right(jnp.where(at == nz - 1, modes, 0.0))
    start = pairs6_right(jnp.where(at == 0, modes, 0.0))
    for ref, value in (
        (field, dot_00(pairs6(stack[...]), wide)),
        (y_field, dot_00(pairs6(beyond[0:8]), wide)),
        (z_field, dot_00(pairs6(beyond[8:16]), last) + dot_00(pairs6(beyond[16:24]), start)),
    ):
        for c in range(3):
            ref[c] = value[:, c * nz : (c + 1) * nz]

    def x_halo(c, high):
        return jnp.zeros((ny, nz), jnp.float32)

    def y_halo(c, x, high):
        return tile(y_field, c, x, ny)

    for x in range(nx):
        coup = tiles(couplings, 6, x, ny)
        center, total = sums_at(dims, x, field, x_halo, y_halo, z_field, coup)
        change = times(tiles(inverse, 9, x, ny), total)
        at = rows_at(dims, x)
        for c in range(3):
            third[c, at, :] = second[c, at, :] + ((1.0 - DAMPING) * center[c] + change[c])


def faces_kernel(dims, inside, inverse, couplings, xe, xo, third, *sends):
    nx, ny, nz = dims.nx, dims.ny, dims.nz
    side = nx * ny // 2
    my_x, n_x = lax.axis_index("gx"), lax.axis_size("gx")
    x_low = neighbour("gx", [s[:, side:] for s in (xe, xo)], False)
    x_high = neighbour("gx", [s[:, :side] for s in (xe, xo)], True)
    x_low = jnp.where(my_x > 0, x_low, 0.0)
    x_high = jnp.where(my_x < n_x - 1, x_high, 0.0)
    x_mix = jnp.where(lane_iota(8, side) < side // 2, x_high, x_low)
    x_field = dot_00(pairs6(x_mix), pairs6_right(mode_columns(dims)))
    for x, toward, rows in ((0, 0, slice(side - ny, side)), (nx - 1, 1, slice(0, ny))):
        coup = tile(couplings, toward, x, ny)
        v = [coup * x_field[rows, c * nz : (c + 1) * nz] for c in range(3)]
        change = times(tiles(inverse, 9, x, ny), v)
        at = rows_at(dims, x)
        for c in range(3):
            third[c, at, :] = inside[c, at, :] + change[c]
    put_faces(dims, third, sends[:4])
    put_z(dims, third, sends[4:])


def last_kernel(dims, n_z, inverse, couplings, first, third, *refs):
    recv, z_recv, (out, z_halo, result, sems) = refs[:4], refs[4 : 4 + n_z], refs[4 + n_z :]
    nx, ny = dims.nx, dims.ny
    copies = []
    step = nx // CHUNKS
    x_halo, y_halo = received(dims, recv)
    place_z(dims, z_recv, z_halo)
    for x in range(nx):
        coup = tiles(couplings, 6, x, ny)
        center, total = sums_at(dims, x, third, x_halo, y_halo, z_halo, coup)
        change = times(tiles(inverse, 9, x, ny), total)
        at = rows_at(dims, x)
        for c in range(3):
            result[c, at, :] = first[c, at, :] + ((1.0 - DAMPING) * center[c] + change[c])
        if (x + 1) % step == 0:
            at = pl.ds((x + 1 - step) * ny, step * ny)
            copy = (result.at[:, at, :], out.at[:, at, :], sems.at[x // step])
            copies.append(pltpu.make_async_copy(*copy))
            copies[-1].start()
    for copy in copies:
        copy.wait()


def swap(value, axis, odd):
    count = lax.axis_size(axis)
    return lax.ppermute(value, axis, [(partner(i, count, odd), i) for i in range(count)])


def swap_inner(value, axis, spare):
    count, other = lax.axis_size(axis), lax.axis_size(spare)
    which = []
    for i in range(count):
        for k in range(other):
            inside = 0 < i < count - 1
            source = (partner(i, count, True), k) if inside else (i, partner(k, other, False))
            which.append((source[0] * other + source[1], i * other + k))
    return lax.ppermute(value, (axis, spare), which)


def exchange(sends, z_sends):
    xe, xo, ye, yo = sends
    z_recv = []
    for k, v in enumerate(z_sends):
        z_recv.append(swap(v, "gz", k))
    ye = swap(ye, "gy", 0)
    yo = swap_inner(yo, "gy", "gz")
    return exchange_x([xe, xo]) + [ye, yo], z_recv


def exchange_x(sends):
    xo = swap(sends[1], "gx", 1)
    xe = swap(sends[0], "gx", 0)
    return [xe, xo]


def fetch(value, word_y, word_z):
    n_y, n_z = lax.axis_size("gy"), lax.axis_size("gz")
    which = []
    for y in range(n_y):
        for z in range(n_z):
            source = follow(y, n_y, word_y) * n_z + follow(z, n_z, word_z)
            which.append((source, y * n_z + z))
    return lax.ppermute(value, ("gy", "gz"), which)


def call(body, out_shapes, scratch, *args, in_hbm=0, out_hbm=False, alias=None):
    near = pl.BlockSpec(memory_space=pltpu.VMEM)
    far = pl.BlockSpec(memory_space=pltpu.HBM)
    return pl.pallas_call(
        body,
        out_shape=[
            s if hasattr(s, "dtype") else jax.ShapeDtypeStruct(s, jnp.float32) for s in out_shapes
        ],
        in_specs=[far] * in_hbm + [near] * (len(args) - in_hbm),
        out_specs=[far if out_hbm else near] * len(out_shapes),
        scratch_shapes=scratch,
        input_output_aliases=alias or {},
        compiler_params=pltpu.CompilerParams(vmem_limit_bytes=VMEM_LIMIT),
    )(*args)


def cycle(rhs, blocks, couplings, agg_ids, coarse_inv):
    _, nx, ny, nz = rhs.shape
    dims = Dims(nx, ny, nz)
    rows = nx * ny
    rhs = rhs.reshape(3, rows, nz)
    blocks = blocks.reshape(9, rows, nz)
    couplings = couplings.reshape(6, rows, nz)
    own = coarse_inv.shape[2]
    n_y, n_z = lax.axis_size("gy"), lax.axis_size("gz")
    owners = n_y * n_z
    z_count = 1 if n_z == 2 else 2
    vector = (3, rows, nz)
    part = functools.partial
    f32 = jnp.float32

    def faces(count, even, odd):
        return [(count * ny, nz)] * 2 + [(count * nx + even, nz), (count * nx + odd, nz)]

    def z_faces(extra):
        return [(8 + extra, nz)] + [(8, nz)] * (z_count - 1)

    _, rest = blocks_of(n_y, n_z)
    pieces = [fetch(coarse_inv, y, z) for y, z in rest]
    first, inverse, rhs, couplings, own_inv, ids, spread_y, spread_z, *sends = call(
        part(first_kernel, dims, z_count),
        [vector, (9, rows, nz), vector, (6, rows, nz), (36, own), (1, rows)]
        + [jax.ShapeDtypeStruct((rows // 2, 3 * rows), jnp.bfloat16)] * 2
        + faces(3, nx + 36, nx)
        + z_faces(36),
        [
            pltpu.VMEM((9, rows, nz), f32),
            pltpu.VMEM(coarse_inv.shape, f32),
            pltpu.VMEM(agg_ids.shape, jnp.int32),
            pltpu.SemaphoreType.DMA((2 * CHUNKS + 3,)),
        ],
        *[
            pltpu.with_memory_space_constraint(v, pltpu.HBM)
            for v in (rhs, blocks, couplings, coarse_inv, agg_ids)
        ],
        in_hbm=5,
    )
    fat, fat_z = exchange(sends[:4], sends[4:])
    second, sums, *sends, inv_out = call(
        part(second_kernel, dims, z_count),
        [vector, vector] + faces(3, 0, 0)[:2] + [(3 * 36, own)],
        [pltpu.VMEM(vector, f32)],
        inverse,
        couplings,
        first,
        own_inv,
        *fat,
        *fat_z,
    )
    second_x = exchange_x(sends)
    far_inv = fetch(inv_out, EO, ())
    half = rows // 2
    inside, *z_more = call(
        part(coarse_kernel, dims, z_count),
        [(32, half)] + [(16, half)] * (z_count - 1),
        [pltpu.VMEM(vector, f32), pltpu.VMEM((half, nz), f32)],
        rhs,
        sums,
        couplings,
        second,
        ids,
        spread_z,
        *fat[2:],
        *fat_z,
    )
    (packet,) = call(
        part(edges_kernel, dims),
        [(32, half)],
        [pltpu.VMEM((half, nz), f32)],
        inside,
        couplings,
        *second_x,
    )
    z_words, y_words = words_of(n_z), words_of(n_y)
    if n_z == 2:
        more_z = fetch(packet, (), z_words[1])
        mine = packet[:16] + more_z[16:32]
        theirs = more_z[:16] + packet[16:32]
        joined = jnp.concatenate([mine, theirs], axis=0)
    else:
        mine = packet[:16] + swap(packet[16:32], "gz", 0) + swap(z_more[0], "gz", 1)
        joined = jnp.concatenate([mine] + [fetch(mine, (), z) for z in z_words[1:]], axis=0)
    with_more = jnp.concatenate([joined, fat_z[0][8:44], far_inv[36:72]], axis=0)
    packets = [joined]
    for k, y in enumerate(y_words[1:]):
        packets.append(fetch(joined if k else with_more, y, ()))
    stack, beyond = call(
        part(solve_kernel, dims, (n_y, n_z), own),
        [(8, rows), (24, rows)],
        [pltpu.VMEM((owners * 8, own), f32)] * 2 + [pltpu.VMEM((owners * 36, own), f32)]
        + [pltpu.VMEM((owners * 8, half), f32)] * 2
        + [pltpu.VMEM((n, owners * rows), jnp.bfloat16) for n in (24, own)],
        *packets,
        own_inv,
        spread_y,
        fat[2],
        fat_z[0],
        far_inv,
        packets[1],
        *pieces,
    )
    xe, xo = exchange_x([stack, stack])
    (inside,) = call(
        part(third_kernel, dims),
        [vector],
        [pltpu.VMEM(vector, f32)] * 3,
        inverse,
        couplings,
        second,
        stack,
        beyond,
    )
    third, *sends = call(
        part(faces_kernel, dims),
        [vector] + faces(3, 0, 0) + z_faces(0),
        [],
        inside,
        inverse,
        couplings,
        xe,
        xo,
        alias={0: 0},
    )
    recv, z_recv = exchange(sends[:4], sends[4:])
    (out,) = call(
        part(last_kernel, dims, z_count),
        [vector],
        [pltpu.VMEM(vector, f32)] * 2 + [pltpu.SemaphoreType.DMA((CHUNKS,))],
        inverse,
        couplings,
        first,
        third,
        *recv,
        *z_recv,
        out_hbm=True,
    )
    return out.reshape(3, nx, ny, nz)


def solution(mesh):
    return jax.shard_map(
        cycle,
        mesh=mesh,
        in_specs=(
            P(None, "gx", "gy", "gz"),
            P(None, "gx", "gy", "gz"),
            P(None, "gx", "gy", "gz"),
            P("gz", "gx", "gy"),
            P(None, "gx", ("gy", "gz")),
        ),
        out_specs=P(None, "gx", "gy", "gz"),
        check_vma=False,
    )
```
